32 devices in a mesh: groups: 2 (over y), tm: 4 (over z), space: 2 (over x), clip: 2 (over core).
Axes of the slice: x: 2, y: 2, z: 4, core: 2. Of those that a mesh axis runs over, the one named last changes fastest.
Arguments:
- features: bfloat16 [4, 16, 8, 16, 256], P(('groups', 'clip'), 'tm', 'space'), parts along dimension 0, may hold values from -6 to 6
- frame_counts: int32 [4], P(('groups', 'clip')), parts along dimension 0, may hold values from 1 to 16, as said below
- routes: int32 [4, 512, 1], P(('groups', 'clip'), ('tm', 'space')), parts along dimension 0, may hold values from 0 to 7; in each aligned block of 64 rows (0 to 63, 64 to 127, ..., all dimensions but the last counted through in order) at most 9 rows name the same one
- norm_gains: float32 [3, 256], replicated, may hold values from 0.5 to 1.5
- conv_weights: bfloat16 [2, 256, 27, 256], P(None, 'tm'), may hold values from -0.078125 to 0.078125
- conv_biases: float32 [2, 256], replicated, may hold values from -3 to 3
- latent_weight: bfloat16 [256, 16], replicated, may hold values from -0.375 to 0.375
- embed_weight: bfloat16 [64, 3072], replicated, may hold values from -0.75 to 0.75
- embed_bias: float32 [3072], replicated, may hold values from -3 to 3
Outputs:
- packed: bfloat16 [4, 576, 3072], P(('groups', 'clip'), ('tm', 'space')), parts along dimension 0
The draws below stay inside these ranges and needn't reach their ends.
There are 2 independent parts, one for each index of `groups`. The reference program is written for one: setup_inputs(seed, part) draws one part's arguments, and reference() takes and returns one part's arrays. A program takes and returns all parts, laid end to end along the dimension named above; an argument that names none is the same for every part. Nothing has to cross between parts.
Inputs may be any that keep to these rules, and one draw needn't show every extreme that they name: `routes`: in each clip, the 64 patches of one span and tile name any one owner at most 9 times. `frame_counts`: one clip of each part has all 16 frames valid.
All inputs are finite; a program needn't handle non-finite values.
Results may differ from the reference program's by a relative error of at most 0.0054.
Values may be sent and summed in bfloat16 or wider, within the bound.
A program may use at most 64 MiB of HBM per device.

```python
import math
import jax
import jax.numpy as jnp
import numpy as np
from jax import lax

C = 256
LAT = 16
EMBED = 3072
FR = 4
ROWS = 4
COLS = 16
CLIPS = 2
FRAMES = 16
ROWS_ALL = 8
OWNERS = 8
TOK_DEV = 64
PATCHES = 512
MOST = 9
SLOTS = 72
N_TM = 4
N_SPACE = 2


def draw_frame_counts(key, part):
    first_key, second_key = jax.random.split(jax.random.fold_in(key, 17))
    counts = jax.random.randint(first_key, (CLIPS,), 1, FRAMES + 1)
    chosen = jax.random.randint(second_key, (), 0, CLIPS)
    return jnp.where(jnp.arange(CLIPS) == chosen, FRAMES, counts).astype(jnp.int32)


def levels(key, dims, shards, least, top_value):
    def one(position, parts):
        heights = jax.random.uniform(jax.random.fold_in(jax.random.fold_in(key, 6), position), (parts,), jnp.float32, least / len(shards), top_value / len(shards))
        return jnp.repeat(jnp.exp(heights), dims[position] // parts).reshape((-1,) + (1,) * (len(dims) - position - 1))

    level = one(*shards[0])
    for cut in shards[1:]:
        level = level * one(*cut)
    return level


def routed_block(key, own, number, rows, count, top, bound, skew):
    sequence = jax.random.permutation(key, count)
    heavy_load, usual = portions_of(count, rows * top, bound, skew, True), portions_of(count, rows * top, bound, skew, False)
    places = jnp.arange(count)

    def named(tallies, rotation):
        used = int((tallies > 0).sum())
        fixed = max(1, used // 4)
        moved = fixed + (places - fixed + rotation * (used - fixed)) % max(1, count - fixed)
        return jnp.zeros((count,), jnp.int32).at[sequence[jnp.where(places < fixed, places, moved)]].set(jnp.asarray(tallies, jnp.int32))

    tallies = jnp.where(number % 4 == 0, named(heavy_load, number // 4), named(usual, number - number // 4 - 1))
    mixed = jax.random.permutation(jax.random.fold_in(own, 3), count)
    giver, receiver = mixed[0:count // 2 * 2:2], mixed[1:count // 2 * 2:2]
    slack = jnp.minimum(tallies[giver] - 1, bound - tallies[receiver]) // 2
    slack = jnp.where((giver == sequence[0]) | (receiver == sequence[0]) | (tallies[receiver] == 0), 0, jnp.maximum(slack, 0))
    moved = jax.random.randint(jax.random.fold_in(own, 4), (count // 2,), 0, 1 << 20) % (slack + 1)
    tallies = tallies.at[giver].add(-moved).at[receiver].add(moved)
    items = jnp.searchsorted(jnp.cumsum(tallies), jnp.arange(rows * top), side="right").astype(jnp.int32)
    table = items.reshape(top, rows).T
    table = table[jax.random.permutation(jax.random.fold_in(own, 1), rows)]
    rotation = jax.random.randint(jax.random.fold_in(own, 2), (rows, 1), 0, top)
    return jnp.take_along_axis(table, (jnp.arange(top)[None, :] + rotation) % top, axis=1)


def portions_of(number_of, total, limit, slope, full):
    weights = [(1 << 20) // math.isqrt(rank ** slope) + 1 for rank in range(1, number_of + 1)]
    largest = limit if full else min(limit, max(-(-total // number_of), total * weights[0] // sum(weights)))
    least = 1 if total - largest >= number_of - 1 else 0
    given, surplus = [largest] + [least] * (number_of - 1), total - largest - least * (number_of - 1)
    while surplus > 0:
        candidates = [i for i in range(1, number_of) if given[i] < largest] or [i for i in range(1, number_of) if given[i] < limit]
        whole, budget = sum([weights[i] for i in candidates]), surplus
        for i in candidates:
            extra = min(limit - given[i], max(1, budget * weights[i] // whole), surplus)
            given[i] = given[i] + extra
            surplus = surplus - extra
    return np.array(given)


def noise(rng, extent, deviation, bound, shards=(), held_as=jnp.bfloat16):
    entries = deviation * jax.random.normal(rng, extent, jnp.float32)
    if shards:
        entries = entries * levels(rng, extent, shards, -0.22, 0.18)
    return jnp.clip(entries, -bound, bound).astype(held_as)


def setup_inputs(seed: int = 0, part: int = 0) -> dict:
    key_of = jax.random.split(jax.random.key(seed), 10)
    part_splits = jax.random.split(jax.random.fold_in(key_of[9], part), 10)
    features = noise(part_splits[0], (CLIPS, FRAMES, ROWS_ALL, COLS, C), 1.0, 6.0, ((0, 2), (1, 4), (2, 2)))
    frame_counts = draw_frame_counts(jax.random.fold_in(jax.random.fold_in(key_of[9], part), 71), part)
    routes_keys = jax.random.split(jax.random.fold_in(part_splits[2], 1), CLIPS * PATCHES // TOK_DEV)
    routes_turns = jax.random.permutation(jax.random.fold_in(part_splits[2], 3), CLIPS * PATCHES // TOK_DEV)
    routes = jax.vmap(lambda own, number: routed_block(jax.random.fold_in(part_splits[2], 2), own, number, TOK_DEV, OWNERS, 1, MOST, 2))(routes_keys, routes_turns).reshape((CLIPS, PATCHES, 1))
    norm_gains = jnp.clip(jax.random.uniform(key_of[3], (3, C), jnp.float32, 0.5, 1.5), 0.5, 1.5)
    conv_weights = noise(key_of[4], (2, C, 27, C), (27 * C) ** -0.5, 0.078125, ((1, 4),))
    conv_biases = noise(key_of[5], (2, C), 0.5, 3.0, (), jnp.float32)
    latent_weight = noise(key_of[6], (C, LAT), C ** -0.5, 0.375)
    embed_weight = noise(key_of[7], (4 * LAT, EMBED), (4 * LAT) ** -0.5, 0.75)
    embed_bias = noise(key_of[8], (EMBED,), 0.5, 3.0, (), jnp.float32)
    return dict(features=features, frame_counts=frame_counts, routes=routes, norm_gains=norm_gains, conv_weights=conv_weights, conv_biases=conv_biases, latent_weight=latent_weight, embed_weight=embed_weight, embed_bias=embed_bias)


def norm_silu(values, gain):
    scale = lax.rsqrt(lax.optimization_barrier(jnp.mean(values * values, axis=-1, keepdims=True)) + 1e-06)
    return jax.nn.silu(values * scale * gain)

def causal_conv(inputs, weights):
    kernel = weights.astype(jnp.float32).reshape(C, 3, 3, 3, C).transpose(1, 2, 3, 4, 0)
    result = lax.conv_general_dilated(inputs.astype(jnp.float32)[None], kernel, (1, 1, 1), ((2, 0), (1, 1), (1, 1)), dimension_numbers=('NDHWC', 'DHWIO', 'NDHWC'), precision=lax.Precision.HIGHEST)
    return result[0]

def encode_clip(clip_features, clip_count, clip_routes, norm_gains, conv_weights, conv_biases, latent_weight, embed_weight, embed_bias):
    inputs = clip_features.astype(jnp.float32)
    active = norm_silu(inputs, norm_gains[0]).astype(jnp.bfloat16)
    hidden = causal_conv(active, conv_weights[0]) + conv_biases[0]
    active = norm_silu(hidden, norm_gains[1]).astype(jnp.bfloat16)
    hidden = causal_conv(active, conv_weights[1]) + conv_biases[1]
    merged = inputs + hidden
    active = norm_silu(merged, norm_gains[2]).astype(jnp.bfloat16)
    latent = jnp.dot(active.reshape(-1, C), latent_weight, preferred_element_type=jnp.float32)
    latent = latent.reshape(N_TM, FR, N_SPACE, ROWS // 2, 2, COLS // 2, 2, LAT)
    patches = latent.transpose(0, 2, 1, 3, 5, 4, 6, 7).reshape(PATCHES, 4 * LAT).astype(jnp.bfloat16)
    embedded = jnp.dot(patches, embed_weight, preferred_element_type=jnp.float32) + embed_bias
    destinations = clip_routes[:, 0].astype(jnp.int32)
    blocks = destinations.reshape(OWNERS, TOK_DEV)
    positions = jnp.arange(TOK_DEV).astype(jnp.int32)
    before = positions[:, None] > positions[None, :]
    matches = (blocks[:, :, None] == blocks[:, None, :]) & before[None]
    ranks = lax.optimization_barrier(jnp.sum(matches.astype(jnp.int32), axis=2)).reshape(PATCHES)
    indices = jnp.arange(PATCHES).astype(jnp.int32)
    sources = indices // TOK_DEV
    target_rows = destinations * SLOTS + sources * MOST + ranks
    frame_ids = sources // N_SPACE * FR + indices % TOK_DEV // (ROWS // 2 * (COLS // 2))
    alive = (frame_ids < clip_count).astype(jnp.float32)
    values = (embedded * alive[:, None]).astype(jnp.bfloat16)
    return jnp.zeros((OWNERS * SLOTS, EMBED), jnp.bfloat16).at[target_rows].set(values)

def reference(features, frame_counts, routes, norm_gains, conv_weights, conv_biases, latent_weight, embed_weight, embed_bias):
    results = [encode_clip(features[clip_index], frame_counts[clip_index], routes[clip_index], norm_gains, conv_weights, conv_biases, latent_weight, embed_weight, embed_bias) for clip_index in range(CLIPS)]
    return jnp.stack(results)
```

```python
import functools

import jax
import jax.numpy as jnp
from jax import lax
from jax.experimental import pallas as pl
from jax.experimental.pallas import tpu as pltpu
from jax.sharding import PartitionSpec as P

MESH = pl.DeviceIdType.MESH
LANES = 128
SUBLANES = 16
CUTS = 4


def norm_silu(values, gain):
    scale = lax.rsqrt(jnp.mean(values * values, axis=-1, keepdims=True) + 1e-06)
    scaled = values * scale * gain
    return scaled / (1.0 + jnp.exp(-scaled))


def encoder(
    n, ns, most, width_latent,
    feat, weights_any, gains, biases, latent_rows, owner_of, count,
    tokens_out,
    field, taps, placing, slab_out, slab_in, edge_out, edge_in, tok_out, tok_in,
    raw_sem, block_send, relay_send, block_recv,
    slab_send, slab_recv, edge_send, edge_recv, tok_send, tok_recv,
):
    t = lax.axis_index("tm")
    s = lax.axis_index("space")
    me = t * ns + s
    owners = n * ns
    frames, rows, cols, width = feat.shape
    cells = frames * rows * cols
    out = weights_any.shape[2] // 3
    cuts = block_recv.shape[2]
    size = frames // cuts
    pack = max(1, LANES // out)
    relays = n == 4

    barrier = pltpu.get_barrier_semaphore()

    def greet(d, carry):
        o = (me + d) % owners
        pl.semaphore_signal(
            barrier, inc=1, device_id={"tm": o // ns, "space": o % ns}, device_id_type=MESH
        )
        return carry

    lax.fori_loop(1, owners, greet, 0)
    weight_copy = pltpu.make_async_copy(weights_any, taps, raw_sem)
    weight_copy.start()

    field[:, 0:2] = jnp.zeros((2, 2) + field.shape[2:], field.dtype)

    @pl.when(s == 0)
    def _():
        edge_in[:, 0] = jnp.zeros((2,) + edge_in.shape[2:], edge_in.dtype)

    @pl.when(s == ns - 1)
    def _():
        edge_in[:, 1] = jnp.zeros((2,) + edge_in.shape[2:], edge_in.dtype)

    inputs = feat[...].reshape(cells, width).astype(jnp.float32)

    def keep(layer, active):
        field[layer, pl.ds(2 + frames * t, frames)] = active.astype(jnp.bfloat16).reshape(
            frames, rows, cols, width
        )

    def block_copy(layer, c, f, target, send_sem):
        span = field.at[layer, pl.ds(2 + frames * c + size * f, size)]
        return pltpu.make_async_remote_copy(
            src_ref=span, dst_ref=span, send_sem=send_sem, recv_sem=block_recv.at[layer, c, f],
            device_id={"tm": target}, device_id_type=MESH,
        )

    def slab_copy(layer, source, target):
        return pltpu.make_async_remote_copy(
            src_ref=slab_out.at[layer, target], dst_ref=slab_in.at[layer, source],
            send_sem=slab_send.at[layer, target], recv_sem=slab_recv.at[layer, source],
            device_id={"tm": target}, device_id_type=MESH,
        )

    def edge_copy(layer, side, source, target):
        return pltpu.make_async_remote_copy(
            src_ref=edge_out.at[layer, side, target], dst_ref=edge_in.at[layer, side, source],
            send_sem=edge_send.at[layer, side, target], recv_sem=edge_recv.at[layer, side, source],
            device_id={"tm": target, "space": (s + 1 - 2 * side + ns) % ns}, device_id_type=MESH,
        )

    def sided(side, act):
        pl.when(s < ns - 1 if side == 0 else s > 0)(act)

    def fed(side, act):
        pl.when(s > 0 if side == 0 else s < ns - 1)(act)

    def targets(layer, act):
        for d in range(n - 1, 0, -1):
            for target in (t - d, t + d):
                here = (target >= 0) & (target < n)
                if relays and d == 2:
                    here = here & ((t == 0) | (t == n - 1))
                spot = (target + n) % n

                def each(spot=spot):
                    for f in range(cuts):
                        act(block_copy(layer, t, f, spot, block_send.at[layer, spot, f]))

                pl.when(here)(each)

    def far_targets(layer, act):
        def each(d, carry):
            spot = (t + d) % n
            for f in range(cuts):
                act(block_copy(layer, t, f, spot, block_send.at[layer, spot, f]))
            return carry

        lax.fori_loop(1, n, each, 0)

    reach = targets if n <= 8 else far_targets
    relay_target = jnp.where(t == 1, 0, n - 1)
    relay_source = jnp.where(t == 1, 2, 1)

    def relay_copy(layer, f):
        return block_copy(layer, relay_source, f, relay_target, relay_send.at[layer, f])

    def sent(layer):
        reach(layer, lambda copy: copy.wait_send())
        if relays:

            @pl.when((t == 1) | (t == 2))
            def _():
                for f in range(cuts):
                    relay_copy(layer, f).wait_send()

        def each(c, carry):
            pl.when(c != t)(lambda: slab_copy(layer, t, c).wait_send())
            for side in range(2):
                sided(side, lambda: edge_copy(layer, side, t, c).wait_send())
            return carry

        lax.fori_loop(0, n, each, 0)

    def arrived(layer, c):
        for f in range(cuts):
            block_copy(layer, c, f, c, block_send.at[layer, c, f]).wait_recv()

    def arrived_relay(layer, c):
        for f in range(cuts):
            block_copy(layer, c, f, c, block_send.at[layer, c, f]).wait_recv()
            relay_copy(layer, f).start()

    grid_rows = rows + 2
    column = lax.broadcasted_iota(jnp.int32, (frames * grid_rows * cols, 1), 0) % cols

    def fold(values):
        part = values.shape[0] // pack
        return jnp.concatenate([values[j * part : (j + 1) * part] for j in range(pack)], axis=1)

    def unfold(pieces):
        return jnp.concatenate(
            [
                jnp.concatenate([piece[:, j * out : (j + 1) * out] for piece in pieces], axis=1)
                for j in range(pack)
            ],
            axis=0,
        )

    def convolve(layer):
        def one(b):
            sums = []
            for r in range(3):
                total = None
                for a in range(3):
                    block = field[layer, pl.ds(frames * b + a, frames)]
                    term = lax.dot_general(
                        block.reshape(cells, width), taps[layer, 3 * a + r],
                        (((1,), (1,)), ((), ())), preferred_element_type=jnp.float32,
                    )
                    total = term if total is None else total + term
                sums.append(total.reshape(frames, rows, cols, 3 * out))
            blank = jnp.zeros((frames, 1, cols, 3 * out), jnp.float32)
            two = jnp.concatenate([blank] * 2, axis=1)
            wide = (
                jnp.concatenate([sums[2], two], axis=1)
                + jnp.concatenate([blank, sums[1], blank], axis=1)
                + jnp.concatenate([two, sums[0]], axis=1)
            ).reshape(frames * grid_rows * cols, 3 * out)
            last = frames * grid_rows * cols - 1
            left = jnp.where(column == 0, 0.0, pltpu.roll(wide[:, :out], 1, 0))
            right = jnp.where(column == cols - 1, 0.0, pltpu.roll(wide[:, 2 * out :], last, 0))
            summed = (left + wide[:, out : 2 * out] + right).reshape(frames, grid_rows, cols, out)
            inner = summed[:, 1 : rows + 1].reshape(cells, out)
            edges = (
                summed[:, rows + 1 :].reshape(frames * cols, out),
                summed[:, :1].reshape(frames * cols, out),
            )
            packed = fold(inner).astype(jnp.bfloat16)

            @pl.when(b == t)
            def _():
                slab_in[layer, pl.ds(t, 1)] = packed[None]

            @pl.when(b != t)
            def _():
                slab_out[layer, pl.ds(b, 1)] = packed[None]
                slab_copy(layer, t, b).start()

            for side in range(2):

                def give(side=side):
                    edge_out[layer, side, pl.ds(b, 1)] = fold(edges[side]).astype(jnp.bfloat16)[None]
                    edge_copy(layer, side, t, b).start()

                sided(side, give)

        if relays:
            order = ((0, 1, 3, 2), (2, 3, 0, 1), (2, 0, 1, 3), (0, 3, 1, 2))
            needs = (
                ((), (1,), (3, 2), ()),
                ((2,), (3,), (0,), ()),
                ((1,), (0,), (), (3,)),
                ((0,), (2,), (1,), ()),
            )

            def pick(k):
                spot = order[0][k]
                for i in range(1, n):
                    spot = jnp.where(t == i, order[i][k], spot)
                return spot

            for i in range(n):
                if needs[i][0]:
                    wait = arrived_relay if i in (1, 2) else arrived
                    pl.when(t == i)(functools.partial(wait, layer, needs[i][0][0]))

            def step(k, carry):
                for i in range(n):
                    for kk in range(1, n):
                        for c in needs[i][kk]:
                            pl.when((t == i) & (k == kk))(functools.partial(arrived, layer, c))
                spot = pick(0)
                for kk in range(1, n):
                    spot = jnp.where(k == kk, pick(kk), spot)
                one(spot)
                return carry

            lax.fori_loop(0, n, step, 0)
        else:

            def hold(d, carry):
                arrived(layer, (t + d) % n)
                return carry

            lax.fori_loop(1, n, hold, 0)

            def step(d, carry):
                one((t + d) % n)
                return carry

            lax.fori_loop(1, n + 1, step, 0)

        def came(k, carry):
            q = (t + k) % n
            pl.when(k > 0)(lambda: slab_copy(layer, q, q).wait_recv())
            for side in range(2):
                fed(side, lambda: edge_copy(layer, side, q, q).wait_recv())
            return carry

        lax.fori_loop(0, n, came, 0)
        hidden = unfold([slab_in[layer, q].astype(jnp.float32) for q in range(n)])
        top, low = [
            unfold([edge_in[layer, side, q].astype(jnp.float32) for q in range(n)]).reshape(
                frames, 1, cols, width
            )
            for side in range(2)
        ]
        hidden = hidden.reshape(frames, rows, cols, width)
        if rows > 1:
            hidden = jnp.concatenate(
                [hidden[:, :1] + top, hidden[:, 1 : rows - 1], hidden[:, rows - 1 :] + low], axis=1
            )
        else:
            hidden = hidden + top + low
        return hidden.reshape(cells, width) + biases[layer : layer + 1]

    keep(0, norm_silu(inputs, gains[0:1]))
    toks = owner_of.shape[1]
    before = lax.broadcasted_iota(jnp.int32, (toks, toks), 0)
    after = lax.broadcasted_iota(jnp.int32, (toks, toks), 1)
    owner = owner_of[...]
    owner_column = jnp.sum(jnp.where(before == after, owner, 0), axis=1, keepdims=True)
    same = (owner_column == owner) & (before < after)
    rank = jnp.sum(jnp.where(same, 1, 0), axis=0, keepdims=True)
    slots = lax.broadcasted_iota(jnp.int32, (owners * SUBLANES, toks), 0)
    placing[...] = jnp.where(slots == owner * SUBLANES + rank, 1.0, 0.0).astype(jnp.bfloat16)
    pl.semaphore_wait(barrier, owners - 1)
    reach(0, lambda copy: copy.start())
    weight_copy.wait()
    hidden = convolve(0)
    keep(1, norm_silu(hidden, gains[1:2]))
    reach(1, lambda copy: copy.start())
    hidden = convolve(1)
    merged = feat[...].reshape(cells, width).astype(jnp.float32) + hidden
    active = norm_silu(merged, gains[2:3]).astype(jnp.bfloat16)
    rest = jnp.zeros((LANES - 4 * width_latent, width), jnp.bfloat16)
    latent_wide = jnp.concatenate([latent_rows[...]] * 4 + [rest], axis=0)
    latent = lax.dot_general(
        active, latent_wide, (((1,), (1,)), ((), ())), preferred_element_type=jnp.float32
    )
    cell = lax.broadcasted_iota(jnp.int32, (cells, LANES), 0)
    lane = lax.broadcasted_iota(jnp.int32, (cells, LANES), 1)
    corner = (cell // cols % 2) * 2 + cell % 2
    alive = (t * frames + cell // (rows * cols) < count[0]) & (corner == 0)
    flagged = jnp.where((lane == 4 * width_latent) & alive, 1.0, 0.0)
    patches = jnp.where(lane // width_latent == corner, latent, flagged).astype(jnp.bfloat16)
    spot = lax.broadcasted_iota(jnp.int32, (toks, cells), 1)
    patch = (spot // (2 * cols)) * (cols // 2) + spot % cols // 2
    mine = patch == lax.broadcasted_iota(jnp.int32, (toks, cells), 0)
    patches = jnp.dot(
        jnp.where(mine, 1.0, 0.0).astype(jnp.bfloat16), patches, preferred_element_type=jnp.float32
    ).astype(jnp.bfloat16)
    outgoing = jnp.dot(
        placing[...], patches, preferred_element_type=jnp.float32
    ).astype(jnp.bfloat16)
    tok_out[...] = outgoing.reshape(owners, SUBLANES, LANES)
    tok_in[pl.ds(me, 1)] = tok_out[pl.ds(me, 1)]

    def tok_copy(source, target):
        return pltpu.make_async_remote_copy(
            src_ref=tok_out.at[target], dst_ref=tok_in.at[source],
            send_sem=tok_send.at[target], recv_sem=tok_recv.at[source],
            device_id={"tm": target // ns, "space": target % ns}, device_id_type=MESH,
        )

    def tok_start(d, carry):
        tok_copy(me, (me + d) % owners).start()
        return carry

    def tok_wait(d, carry):
        o = (me + d) % owners
        tok_copy(o, o).wait_recv()
        return carry

    def tok_sent(d, carry):
        tok_copy(me, (me + d) % owners).wait_send()
        return carry

    lax.fori_loop(1, owners, tok_start, 0)
    sent(0)
    sent(1)
    lax.fori_loop(1, owners, tok_wait, 0)
    row = lax.broadcasted_iota(jnp.int32, (owners * most, owners * SUBLANES), 0)
    held = lax.broadcasted_iota(jnp.int32, (owners * most, owners * SUBLANES), 1)
    inner = held % SUBLANES
    chosen = (row == held // SUBLANES * most + inner) & (inner < most)
    tokens_out[...] = jnp.dot(
        jnp.where(chosen, 1.0, 0.0).astype(jnp.bfloat16),
        tok_in[...].reshape(owners * SUBLANES, LANES),
        preferred_element_type=jnp.float32,
    ).astype(jnp.bfloat16)
    lax.fori_loop(1, owners, tok_sent, 0)


def embedder(channels, tokens, weight, bias, packed):
    held = tokens[...]
    projected = jnp.dot(held[:, :channels], weight[...], preferred_element_type=jnp.float32)
    flags = held[:, channels : channels + 1].astype(jnp.float32)
    packed[...] = ((projected + bias[...]) * flags).astype(jnp.bfloat16)


def shards(
    features,
    frame_counts,
    routes,
    norm_gains,
    conv_weights,
    conv_biases,
    latent_weight,
    embed_weight,
    embed_bias,
):
    feat = features[0]
    frames, rows, cols, width = feat.shape
    cells = frames * rows * cols
    n, ns = lax.axis_size("tm"), lax.axis_size("space")
    owners = n * ns
    out = conv_weights.shape[1]
    pack = max(1, LANES // out)
    latents = latent_weight.shape[1]
    tok_count = routes.shape[1]
    most = (tok_count + owners - 1) // owners + 1
    vmem = pl.BlockSpec(memory_space=pltpu.VMEM)
    dma = pltpu.SemaphoreType.DMA
    field = pltpu.VMEM((2, n * frames + 2, rows, cols, width), jnp.bfloat16)
    slab = pltpu.VMEM((2, n, cells // pack, pack * out), jnp.bfloat16)
    edge = pltpu.VMEM((2, 2, n, frames * cols // pack, pack * out), jnp.bfloat16)
    cuts = CUTS if frames % CUTS == 0 else 1
    tok = pltpu.VMEM((owners, SUBLANES, LANES), jnp.bfloat16)
    tokens = pl.pallas_call(
        functools.partial(encoder, n, ns, most, latents),
        out_shape=jax.ShapeDtypeStruct((owners * most, LANES), jnp.bfloat16),
        in_specs=[vmem, pl.BlockSpec(memory_space=pl.ANY), vmem, vmem, vmem, vmem,
                  pl.BlockSpec(memory_space=pltpu.SMEM)],
        out_specs=vmem,
        scratch_shapes=[
            field,
            pltpu.VMEM((2, 9, 3 * out, width), jnp.bfloat16),
            pltpu.VMEM((owners * SUBLANES, tok_count), jnp.bfloat16),
            slab, slab, edge, edge, tok, tok,
            dma,
            dma((2, n, cuts)), dma((2, cuts)), dma((2, n, cuts)),
            dma((2, n)), dma((2, n)), dma((2, 2, n)), dma((2, 2, n)),
            dma((owners,)), dma((owners,)),
        ],
        compiler_params=pltpu.CompilerParams(collective_id=0, has_side_effects=True),
    )(
        feat,
        conv_weights.transpose(0, 2, 1, 3).reshape(2, 9, 3 * out, width),
        norm_gains,
        conv_biases,
        latent_weight.T,
        routes.reshape(1, tok_count),
        frame_counts,
    )
    channels = 4 * latents
    embed = embed_weight.shape[1]
    chunk = embed // 1 if embed % (1 * LANES) == 0 else embed
    packed = pl.pallas_call(
        functools.partial(embedder, channels),
        grid=(embed // chunk,),
        out_shape=jax.ShapeDtypeStruct((owners * most, embed), jnp.bfloat16),
        in_specs=[
            pl.BlockSpec((owners * most, LANES), lambda i: (0, 0)),
            pl.BlockSpec((channels, chunk), lambda i: (0, i)),
            pl.BlockSpec((1, chunk), lambda i: (0, i)),
        ],
        out_specs=pl.BlockSpec((owners * most, chunk), lambda i: (0, i)),
    )(tokens, embed_weight, embed_bias.reshape(1, embed))
    return packed[None]


def solution(mesh):
    return jax.shard_map(
        shards,
        mesh=mesh,
        in_specs=(
            P(("groups", "clip"), "tm", "space", None, None),
            P(("groups", "clip")),
            P(("groups", "clip"), ("tm", "space"), None),
            P(),
            P(None, "tm", None, None),
            P(),
            P(),
            P(),
            P(),
        ),
        out_specs=P(("groups", "clip"), ("tm", "space"), None),
        check_vma=False,
    )
```

```python
import functools

import jax
import jax.numpy as jnp
from jax import lax
from jax.experimental import pallas as pl
from jax.experimental.pallas import tpu as pltpu
from jax.sharding import PartitionSpec as P

MESH = pl.DeviceIdType.MESH
LANES = 128
SUBLANES = 16
CUTS = 4


def norm_silu(values, gain):
    scale = lax.rsqrt(jnp.mean(values * values, axis=-1, keepdims=True) + 1e-06)
    scaled = values * scale * gain
    return scaled / (1.0 + jnp.exp(-scaled))


def encoder(
    n, ns, ng, nc, most, width_latent,
    feat, weights_any, shares_any, gains, biases, latent_rows, owner_of, count,
    tokens_out,
    field, inner, taps, shares, placing, slab_out, slab_in, edge_out, edge_in, tok_out, tok_in,
    raw_sem, share_sem, block_send, relay_send, block_recv,
    slab_send, slab_recv, edge_send, edge_recv, halo_send, halo_recv,
    line_send, line_relay, line_recv, plane_send, plane_recv, core_send, core_recv,
    tok_send, tok_recv,
):
    t = lax.axis_index("tm")
    s = lax.axis_index("space")
    g = lax.axis_index("groups")
    core = lax.axis_index("clip")
    me = t * ns + s
    owners = n * ns
    frames, rows, cols, width = feat.shape
    cells = frames * rows * cols
    out = weights_any.shape[2] // 3
    cuts = block_recv.shape[1]
    size = frames // cuts
    pack = max(1, LANES // out)
    relays = n == 4
    columns, parts, _, share_rows, share_lanes = shares.shape[1:]
    shared = columns > 1
    column_of = g * ns + s if shared else 0
    part_of = core if shared else 0

    barrier = pltpu.get_barrier_semaphore()

    def greet(d, carry):
        o = (me + d) % owners
        pl.semaphore_signal(
            barrier, inc=1, device_id={"tm": o // ns, "space": o % ns}, device_id_type=MESH
        )
        return carry

    lax.fori_loop(1, owners, greet, 0)
    expected = owners - 1
    if shared:
        for dg in range(1, ng):
            for other in range(ns):
                pl.semaphore_signal(
                    barrier, inc=1, device_id={"groups": (g + dg) % ng, "space": other},
                    device_id_type=MESH,
                )
                expected += 1
        for dc in range(1, nc):
            pl.semaphore_signal(
                barrier, inc=1, device_id={"clip": (core + dc) % nc}, device_id_type=MESH
            )
            expected += 1
    weight_copy = pltpu.make_async_copy(weights_any.at[0], taps, raw_sem)

    def share_load(col, part):
        lanes = pl.ds(pl.multiple_of(part * share_lanes, LANES), share_lanes)
        return pltpu.make_async_copy(
            shares_any.at[1, :, pl.ds(col * share_rows, share_rows), lanes],
            shares.at[t, col, part], share_sem.at[col, part],
        )

    share_load(column_of, part_of).start()
    weight_copy.start()

    def others(act):
        for col in range(columns):
            for part in range(parts):
                pl.when((column_of != col) | (part_of != part))(lambda: act(share_load(col, part)))

    others(lambda copy: copy.start())

    field[0:2] = jnp.zeros((2,) + field.shape[1:], field.dtype)

    @pl.when(t == 0)
    def _():
        inner[0:2] = jnp.zeros((2,) + inner.shape[1:], inner.dtype)

    @pl.when(s == 0)
    def _():
        edge_in[0] = jnp.zeros(edge_in.shape[1:], edge_in.dtype)
        inner[:, 0:1] = jnp.zeros((inner.shape[0], 1) + inner.shape[2:], inner.dtype)

    @pl.when(s == ns - 1)
    def _():
        edge_in[1] = jnp.zeros(edge_in.shape[1:], edge_in.dtype)
        inner[:, rows + 1 :] = jnp.zeros((inner.shape[0], 1) + inner.shape[2:], inner.dtype)

    inputs = feat[...].reshape(cells, width).astype(jnp.float32)

    def block_copy(c, f, target, send_sem):
        span = field.at[pl.ds(2 + frames * c + size * f, size)]
        return pltpu.make_async_remote_copy(
            src_ref=span, dst_ref=span, send_sem=send_sem, recv_sem=block_recv.at[c, f],
            device_id={"tm": target}, device_id_type=MESH,
        )

    def slab_copy(source, target):
        return pltpu.make_async_remote_copy(
            src_ref=slab_out.at[target], dst_ref=slab_in.at[source],
            send_sem=slab_send.at[target], recv_sem=slab_recv.at[source],
            device_id={"tm": target}, device_id_type=MESH,
        )

    def edge_copy(side, source, target):
        return pltpu.make_async_remote_copy(
            src_ref=edge_out.at[side, target], dst_ref=edge_in.at[side, source],
            send_sem=edge_send.at[side, target], recv_sem=edge_recv.at[side, source],
            device_id={"tm": target, "space": (s + 1 - 2 * side + ns) % ns}, device_id_type=MESH,
        )

    def sided(side, act):
        pl.when(s < ns - 1 if side == 0 else s > 0)(act)

    def fed(side, act):
        pl.when(s > 0 if side == 0 else s < ns - 1)(act)

    def line_copy(q, target, send_sem):
        piece = shares.at[q, column_of, part_of]
        return pltpu.make_async_remote_copy(
            src_ref=piece, dst_ref=piece, send_sem=send_sem, recv_sem=line_recv.at[q],
            device_id={"tm": target}, device_id_type=MESH,
        )

    def plane_copy(q, col, d):
        piece = shares.at[q, col, part_of]
        peer = (column_of + d) % columns
        return pltpu.make_async_remote_copy(
            src_ref=piece, dst_ref=piece,
            send_sem=plane_send.at[q, d], recv_sem=plane_recv.at[q, col],
            device_id={"groups": peer // ns, "space": peer % ns}, device_id_type=MESH,
        )

    def core_copy(q, col, part, d):
        piece = shares.at[q, col, part]
        return pltpu.make_async_remote_copy(
            src_ref=piece, dst_ref=piece,
            send_sem=core_send.at[q, col, d], recv_sem=core_recv.at[q, col, part],
            device_id={"clip": (core + d) % nc}, device_id_type=MESH,
        )

    def along(first, act):
        for d in range(n - 1, 0, -1):
            if first is not None and (d == 1) != first:
                continue
            for target in (t - d, t + d):
                here = (target >= 0) & (target < n)
                if relays and d == 2:
                    here = here & ((t == 0) | (t == n - 1))
                pl.when(here)(functools.partial(act, (target + n) % n))

    def around(act):
        def each(d, carry):
            act((t + d) % n)
            return carry

        lax.fori_loop(1, n, each, 0)

    small = n <= 8

    def blocks(act):
        def each(spot):
            for f in range(cuts):
                act(block_copy(t, f, spot, block_send.at[spot, f]))

        along(None, each) if small else around(each)

    def line_of(act):
        return lambda spot: act(line_copy(t, spot, line_send.at[spot]))

    relay_target = jnp.where(t == 1, 0, n - 1)
    relay_source = jnp.where(t == 1, 2, 1)
    relaying = (t == 1) | (t == 2)

    def relay_copy(f):
        return block_copy(relay_source, f, relay_target, relay_send.at[f])

    def line_relay_copy():
        return line_copy(relay_source, relay_target, line_relay)

    def pass_on(q):
        line_copy(q, q, line_send.at[q]).wait_recv()
        if shared:
            for d in range(1, columns):
                plane_copy(q, column_of, d).start()
            for d in range(1, nc):
                core_copy(q, column_of, part_of, d).start()

    def cross(q):
        for d in range(1, columns):
            col = (column_of + d) % columns
            plane_copy(q, col, d).wait_recv()
            for dc in range(1, nc):
                core_copy(q, col, part_of, dc).start()

    def arrived(c):
        for f in range(cuts):
            block_copy(c, f, c, block_send.at[c, f]).wait_recv()

    grid_rows = rows + 2
    column = lax.broadcasted_iota(jnp.int32, (frames * grid_rows * cols, 1), 0) % cols

    def fold(values):
        part = values.shape[0] // pack
        return jnp.concatenate([values[j * part : (j + 1) * part] for j in range(pack)], axis=1)

    def unfold(pieces):
        return jnp.concatenate(
            [
                jnp.concatenate([piece[:, j * out : (j + 1) * out] for piece in pieces], axis=1)
                for j in range(pack)
            ],
            axis=0,
        )

    def beside(left, middle, right):
        count = left.shape[0]
        mark = column[:count]
        left = jnp.where(mark == 0, 0.0, pltpu.roll(left, 1, 0))
        right = jnp.where(mark == cols - 1, 0.0, pltpu.roll(right, count - 1, 0))
        return left + middle + right

    def one(b):
        sums = []
        for r in range(3):
            total = None
            for a in range(3):
                block = field[pl.ds(frames * b + a, frames)]
                term = lax.dot_general(
                    block.reshape(cells, width), taps[3 * a + r],
                    (((1,), (1,)), ((), ())), preferred_element_type=jnp.float32,
                )
                total = term if total is None else total + term
            sums.append(total.reshape(frames, rows, cols, 3 * out))
        blank = jnp.zeros((frames, 1, cols, 3 * out), jnp.float32)
        two = jnp.concatenate([blank] * 2, axis=1)
        wide = (
            jnp.concatenate([sums[2], two], axis=1)
            + jnp.concatenate([blank, sums[1], blank], axis=1)
            + jnp.concatenate([two, sums[0]], axis=1)
        ).reshape(frames * grid_rows * cols, 3 * out)
        summed = beside(wide[:, :out], wide[:, out : 2 * out], wide[:, 2 * out :])
        summed = summed.reshape(frames, grid_rows, cols, out)
        edges = (
            summed[:, rows + 1 :].reshape(frames * cols, out),
            summed[:, :1].reshape(frames * cols, out),
        )
        packed = fold(summed[:, 1 : rows + 1].reshape(cells, out)).astype(jnp.bfloat16)

        @pl.when(b == t)
        def _():
            slab_in[pl.ds(t, 1)] = packed[None]

        @pl.when(b != t)
        def _():
            slab_out[pl.ds(b, 1)] = packed[None]
            slab_copy(t, b).start()

        for side in range(2):

            def give(side=side):
                edge_out[side, pl.ds(b, 1)] = fold(edges[side]).astype(jnp.bfloat16)[None]
                edge_copy(side, t, b).start()

            sided(side, give)

    def halo_copies(act):
        near, far = pl.ds(frames, 2), pl.ds(0, 2)
        own, body = pl.ds(2, frames), pl.ds(1, rows)
        up = {"tm": (t + 1) % n}
        more = t < n - 1

        def copy(i, here, source, target, device):
            pl.when(here)(
                lambda: act(
                    pltpu.make_async_remote_copy(
                        src_ref=inner.at[source], dst_ref=inner.at[target],
                        send_sem=halo_send.at[i], recv_sem=halo_recv.at[i],
                        device_id=device, device_id_type=MESH,
                    )
                )
            )

        left, right = {"space": (s + ns - 1) % ns}, {"space": (s + 1) % ns}
        first, last = pl.ds(1, 1), pl.ds(rows, 1)
        above, below = pl.ds(0, 1), pl.ds(rows + 1, 1)
        copy(0, more, (near, body), (far, body), up)
        copy(1, more & (s > 0), (near, first), (far, below), up | left)
        copy(2, more & (s < ns - 1), (near, last), (far, above), up | right)
        copy(3, s > 0, (own, first), (own, below), left)
        copy(4, s < ns - 1, (own, last), (own, above), right)

    def halo_came():
        def wait(i, here, target):
            def act():
                span = inner.at[target]
                pltpu.make_async_remote_copy(
                    src_ref=span, dst_ref=span, send_sem=halo_send.at[i],
                    recv_sem=halo_recv.at[i], device_id={"tm": t}, device_id_type=MESH,
                ).wait_recv()

            pl.when(here)(act)

        far, own, body = pl.ds(0, 2), pl.ds(2, frames), pl.ds(1, rows)
        above, below = pl.ds(0, 1), pl.ds(rows + 1, 1)
        wait(3, s < ns - 1, (own, below))
        wait(4, s > 0, (own, above))
        wait(0, t > 0, (far, body))
        wait(1, (t > 0) & (s < ns - 1), (far, below))
        wait(2, (t > 0) & (s > 0), (far, above))

    def kernel_of(tap):
        return jnp.concatenate(
            [
                jnp.concatenate([shares[q, col, part, tap] for part in range(parts)], axis=1)
                for q in range(n)
                for col in range(columns)
            ],
            axis=0,
        )

    field[pl.ds(2 + frames * t, frames)] = norm_silu(inputs, gains[0:1]).astype(
        jnp.bfloat16
    ).reshape(frames, rows, cols, width)
    toks = owner_of.shape[1]
    before = lax.broadcasted_iota(jnp.int32, (toks, toks), 0)
    after = lax.broadcasted_iota(jnp.int32, (toks, toks), 1)
    owner = owner_of[...]
    owner_column = jnp.sum(jnp.where(before == after, owner, 0), axis=1, keepdims=True)
    same = (owner_column == owner) & (before < after)
    rank = jnp.sum(jnp.where(same, 1, 0), axis=0, keepdims=True)
    slots = lax.broadcasted_iota(jnp.int32, (owners * SUBLANES, toks), 0)
    placing[...] = jnp.where(slots == owner * SUBLANES + rank, 1.0, 0.0).astype(jnp.bfloat16)
    share_load(column_of, part_of).wait()
    pl.semaphore_wait(barrier, expected)
    start = lambda copy: copy.start()
    if small:
        along(True, line_of(start))
        blocks(start)
        along(False, line_of(start))
    else:
        blocks(start)
        around(line_of(start))
    weight_copy.wait()
    if relays:
        order = ((0, 1, 3, 2), (2, 3, 0, 1), (2, 0, 1, 3), (0, 3, 1, 2))
        needs = (
            ((), (1,), (3, 2), ()),
            ((), (3,), (0,), ()),
            ((), (0,), (), (3,)),
            ((0,), (2,), (1,), ()),
        )
        flow = ((1, 3, 2), (0, 2, 3), (1, 3, 0), (2, 0, 1))

        def pick(table, k):
            spot = table[0][k]
            for i in range(1, n):
                spot = jnp.where(t == i, table[i][k], spot)
            return spot

        pass_on(pick(flow, 0))
        pl.when(relaying)(lambda: pass_on(pick(flow, 1)))

        @pl.when(relaying)
        def _():
            for f in range(cuts):
                block_copy(relay_source, f, relay_source, block_send.at[relay_source, f]).wait_recv()
                relay_copy(f).start()
            line_relay_copy().start()

        def step(k, carry):
            for i in range(n):
                for kk in range(n):
                    for c in needs[i][kk]:
                        pl.when((t == i) & (k == kk))(functools.partial(arrived, c))
            spot = pick(order, 0)
            for kk in range(1, n):
                spot = jnp.where(k == kk, pick(order, kk), spot)
            one(spot)
            return carry

        lax.fori_loop(0, n, step, 0)
        pl.when(relaying)(lambda: pass_on(pick(flow, 2)))
        pl.when(jnp.logical_not(relaying))(lambda: pass_on(pick(flow, 1)))
    else:

        def hold(d, carry):
            arrived((t + d) % n)
            return carry

        lax.fori_loop(1, n, hold, 0)

        def step(d, carry):
            one((t + d) % n)
            return carry

        lax.fori_loop(1, n + 1, step, 0)

    def came(k, carry):
        q = (t + k) % n
        pl.when(k > 0)(lambda: slab_copy(q, q).wait_recv())
        for side in range(2):
            fed(side, lambda: edge_copy(side, q, q).wait_recv())
        return carry

    lax.fori_loop(0, n, came, 0)
    hidden = unfold([slab_in[q].astype(jnp.float32) for q in range(n)])
    top, low = [
        unfold([edge_in[side, q].astype(jnp.float32) for q in range(n)]).reshape(
            frames, 1, cols, width
        )
        for side in range(2)
    ]
    hidden = hidden.reshape(frames, rows, cols, width)
    if rows > 1:
        hidden = jnp.concatenate(
            [hidden[:, :1] + top, hidden[:, 1 : rows - 1], hidden[:, rows - 1 :] + low], axis=1
        )
    else:
        hidden = hidden + top + low
    hidden = hidden.reshape(cells, width) + biases[0:1]
    inner[2:, 1 : rows + 1] = norm_silu(hidden, gains[1:2]).astype(jnp.bfloat16).reshape(
        frames, rows, cols, width
    )
    halo_copies(start)
    if relays:
        pl.when(jnp.logical_not(relaying))(lambda: pass_on(pick(flow, 2)))
    else:

        def passed(d, carry):
            pass_on((t + d) % n)
            return carry

        lax.fori_loop(1, n, passed, 0)
    if shared:

        def crossed(k, carry):
            if relays:
                q = pick(flow, 0)
                for kk in range(1, n - 1):
                    q = jnp.where(k == kk, pick(flow, kk), q)
            else:
                q = (t + 1 + k) % n
            cross(q)
            return carry

        lax.fori_loop(0, n - 1, crossed, 0)
    others(lambda copy: copy.wait())
    halo_came()
    if shared:

        def joined(k, carry):
            q = (t + 1 + k) % n
            for col in range(columns):
                for d in range(1, nc):
                    core_copy(q, col, (core + d) % nc, d).wait_recv()
            return carry

        lax.fori_loop(0, n - 1, joined, 0)
    sums = []
    for e in range(3):
        total = None
        for a in range(3):
            for r in range(3):
                block = inner[a : a + frames, r : r + rows].reshape(cells, width)
                term = lax.dot_general(
                    block, kernel_of(9 * a + 3 * r + e),
                    (((1,), (1,)), ((), ())), preferred_element_type=jnp.float32,
                )
                total = term if total is None else total + term
        sums.append(total)
    hidden = beside(*sums) + biases[1:2]
    merged = feat[...].reshape(cells, width).astype(jnp.float32) + hidden
    active = norm_silu(merged, gains[2:3]).astype(jnp.bfloat16)
    rest = jnp.zeros((LANES - 4 * width_latent, width), jnp.bfloat16)
    latent_wide = jnp.concatenate([latent_rows[...]] * 4 + [rest], axis=0)
    latent = lax.dot_general(
        active, latent_wide, (((1,), (1,)), ((), ())), preferred_element_type=jnp.float32
    )
    cell = lax.broadcasted_iota(jnp.int32, (cells, LANES), 0)
    lane = lax.broadcasted_iota(jnp.int32, (cells, LANES), 1)
    corner = (cell // cols % 2) * 2 + cell % 2
    alive = (t * frames + cell // (rows * cols) < count[0]) & (corner == 0)
    flagged = jnp.where((lane == 4 * width_latent) & alive, 1.0, 0.0)
    patches = jnp.where(lane // width_latent == corner, latent, flagged).astype(jnp.bfloat16)
    spot = lax.broadcasted_iota(jnp.int32, (toks, cells), 1)
    patch = (spot // (2 * cols)) * (cols // 2) + spot % cols // 2
    mine = patch == lax.broadcasted_iota(jnp.int32, (toks, cells), 0)
    patches = jnp.dot(
        jnp.where(mine, 1.0, 0.0).astype(jnp.bfloat16), patches, preferred_element_type=jnp.float32
    ).astype(jnp.bfloat16)
    outgoing = jnp.dot(
        placing[...], patches, preferred_element_type=jnp.float32
    ).astype(jnp.bfloat16)
    tok_out[...] = outgoing.reshape(owners, SUBLANES, LANES)
    tok_in[pl.ds(me, 1)] = tok_out[pl.ds(me, 1)]

    def tok_copy(source, target):
        return pltpu.make_async_remote_copy(
            src_ref=tok_out.at[target], dst_ref=tok_in.at[source],
            send_sem=tok_send.at[target], recv_sem=tok_recv.at[source],
            device_id={"tm": target // ns, "space": target % ns}, device_id_type=MESH,
        )

    def tok_start(d, carry):
        tok_copy(me, (me + d) % owners).start()
        return carry

    def tok_wait(d, carry):
        o = (me + d) % owners
        tok_copy(o, o).wait_recv()
        return carry

    def tok_sent(d, carry):
        tok_copy(me, (me + d) % owners).wait_send()
        return carry

    lax.fori_loop(1, owners, tok_start, 0)
    blocks(lambda copy: copy.wait_send())
    along(None, line_of(lambda copy: copy.wait_send())) if small else around(
        line_of(lambda copy: copy.wait_send())
    )
    if relays:

        @pl.when(relaying)
        def _():
            for f in range(cuts):
                relay_copy(f).wait_send()
            line_relay_copy().wait_send()

    def sent(c, carry):
        pl.when(c != t)(lambda: slab_copy(t, c).wait_send())
        for side in range(2):
            sided(side, lambda: edge_copy(side, t, c).wait_send())
        if shared:

            @pl.when(c != t)
            def _():
                for d in range(1, columns):
                    plane_copy(c, column_of, d).wait_send()
                for col in range(columns):
                    for d in range(1, nc):
                        core_copy(c, col, part_of, d).wait_send()

        return carry

    lax.fori_loop(0, n, sent, 0)
    halo_copies(lambda copy: copy.wait_send())
    lax.fori_loop(1, owners, tok_wait, 0)
    row = lax.broadcasted_iota(jnp.int32, (owners * most, owners * SUBLANES), 0)
    held = lax.broadcasted_iota(jnp.int32, (owners * most, owners * SUBLANES), 1)
    inner = held % SUBLANES
    chosen = (row == held // SUBLANES * most + inner) & (inner < most)
    tokens_out[...] = jnp.dot(
        jnp.where(chosen, 1.0, 0.0).astype(jnp.bfloat16),
        tok_in[...].reshape(owners * SUBLANES, LANES),
        preferred_element_type=jnp.float32,
    ).astype(jnp.bfloat16)
    lax.fori_loop(1, owners, tok_sent, 0)


def embedder(channels, tokens, weight, bias, packed):
    held = tokens[...]
    projected = jnp.dot(held[:, :channels], weight[...], preferred_element_type=jnp.float32)
    flags = held[:, channels : channels + 1].astype(jnp.float32)
    packed[...] = ((projected + bias[...]) * flags).astype(jnp.bfloat16)


def shards(
    features,
    frame_counts,
    routes,
    norm_gains,
    conv_weights,
    conv_biases,
    latent_weight,
    embed_weight,
    embed_bias,
):
    feat = features[0]
    frames, rows, cols, width = feat.shape
    cells = frames * rows * cols
    n, ns = lax.axis_size("tm"), lax.axis_size("space")
    ng, nc = lax.axis_size("groups"), lax.axis_size("clip")
    owners = n * ns
    out = conv_weights.shape[1]
    pack = max(1, LANES // out)
    latents = latent_weight.shape[1]
    tok_count = routes.shape[1]
    most = (tok_count + owners - 1) // owners + 1
    vmem = pl.BlockSpec(memory_space=pltpu.VMEM)
    anywhere = pl.BlockSpec(memory_space=pl.ANY)
    dma = pltpu.SemaphoreType.DMA
    field = pltpu.VMEM((n * frames + 2, rows, cols, width), jnp.bfloat16)
    inner = pltpu.VMEM((frames + 2, rows + 2, cols, width), jnp.bfloat16)
    slab = pltpu.VMEM((n, cells // pack, pack * out), jnp.bfloat16)
    edge = pltpu.VMEM((2, n, frames * cols // pack, pack * out), jnp.bfloat16)
    columns, parts = ng * ns, nc
    if out % (SUBLANES * columns) or width % (LANES * parts):
        columns = parts = 1
    taps = conv_weights.shape[2]
    shares = pltpu.VMEM((n, columns, parts, taps, out // columns, width // parts), jnp.bfloat16)
    cuts = CUTS if frames % CUTS == 0 else 1
    tok = pltpu.VMEM((owners, SUBLANES, LANES), jnp.bfloat16)
    tokens = pl.pallas_call(
        functools.partial(encoder, n, ns, ng, nc, most, latents),
        out_shape=jax.ShapeDtypeStruct((owners * most, LANES), jnp.bfloat16),
        in_specs=[vmem, anywhere, anywhere, vmem, vmem, vmem, vmem,
                  pl.BlockSpec(memory_space=pltpu.SMEM)],
        out_specs=vmem,
        scratch_shapes=[
            field, inner,
            pltpu.VMEM((9, 3 * out, width), jnp.bfloat16),
            shares,
            pltpu.VMEM((owners * SUBLANES, tok_count), jnp.bfloat16),
            slab, slab, edge, edge, tok, tok,
            dma, dma((columns, parts)),
            dma((n, cuts)), dma((cuts,)), dma((n, cuts)),
            dma((n,)), dma((n,)), dma((2, n)), dma((2, n)), dma((5,)), dma((5,)),
            dma((n,)), dma, dma((n,)),
            dma((n, columns)), dma((n, columns)), dma((n, columns, nc)), dma((n, columns, nc)),
            dma((owners,)), dma((owners,)),
        ],
        compiler_params=pltpu.CompilerParams(collective_id=0, has_side_effects=True),
    )(
        feat,
        conv_weights.transpose(0, 2, 1, 3).reshape(2, 9, 3 * out, width),
        conv_weights.transpose(0, 2, 1, 3),
        norm_gains,
        conv_biases,
        latent_weight.T,
        routes.reshape(1, tok_count),
        frame_counts,
    )
    channels = 4 * latents
    embed = embed_weight.shape[1]
    chunk = embed // 1 if embed % (1 * LANES) == 0 else embed
    packed = pl.pallas_call(
        functools.partial(embedder, channels),
        grid=(embed // chunk,),
        out_shape=jax.ShapeDtypeStruct((owners * most, embed), jnp.bfloat16),
        in_specs=[
            pl.BlockSpec((owners * most, LANES), lambda i: (0, 0)),
            pl.BlockSpec((channels, chunk), lambda i: (0, i)),
            pl.BlockSpec((1, chunk), lambda i: (0, i)),
        ],
        out_specs=pl.BlockSpec((owners * most, chunk), lambda i: (0, i)),
    )(tokens, embed_weight, embed_bias.reshape(1, embed))
    return packed[None]


def solution(mesh):
    return jax.shard_map(
        shards,
        mesh=mesh,
        in_specs=(
            P(("groups", "clip"), "tm", "space", None, None),
            P(("groups", "clip")),
            P(("groups", "clip"), ("tm", "space"), None),
            P(),
            P(None, "tm", None, None),
            P(),
            P(),
            P(),
            P(),
        ),
        out_specs=P(("groups", "clip"), ("tm", "space"), None),
        check_vma=False,
    )
```

```python
import functools

import jax
import jax.numpy as jnp
from jax import lax
from jax.experimental import pallas as pl
from jax.experimental.pallas import tpu as pltpu
from jax.sharding import PartitionSpec as P

MESH = pl.DeviceIdType.MESH
LANES = 128
SUBLANES = 16
CUTS = 4
GRANT = 28 << 20


def norm_silu(values, gain):
    scale = lax.rsqrt(jnp.mean(values * values, axis=-1, keepdims=True) + 1e-06)
    scaled = values * scale * gain
    return scaled / (1.0 + jnp.exp(-scaled))


def encoder(
    n, ns, ng, nc, most, width_latent,
    feat_any, weights_any, shares_any, gains_any, biases_any, latent_any, owner_any, count,
    tokens_out,
    feat, gains, biases, latent_rows, owner_of, field, inner, taps, shares, placing, slab_out, slab_in, edge_out, edge_in, tok_out, tok_in,
    load_sem, raw_sem, share_sem, block_send, relay_send, block_recv,
    slab_send, slab_recv, edge_send, edge_recv, halo_send, halo_recv,
    line_send, line_relay_send, line_recv, plane_send, plane_recv, core_send, core_recv,
    tok_send, tok_recv,
):
    t = lax.axis_index("tm")
    s = lax.axis_index("space")
    g = lax.axis_index("groups")
    core = lax.axis_index("clip")
    me = t * ns + s
    owners = n * ns
    frames, rows, cols, width = feat.shape
    cells = frames * rows * cols
    out = weights_any.shape[2] // 3
    cuts = block_recv.shape[1]
    size = frames // cuts
    pack = max(1, LANES // out)
    relays = n == 4
    columns, parts, _, share_rows, share_lanes = shares.shape[1:]
    shared = columns > 1
    column_of = g * ns + s if shared else 0
    part_of = core if shared else 0

    barrier = pltpu.get_barrier_semaphore()

    def greet(d, carry):
        o = (me + d) % owners
        pl.semaphore_signal(
            barrier, inc=1, device_id={"tm": o // ns, "space": o % ns}, device_id_type=MESH
        )
        return carry

    lax.fori_loop(1, owners, greet, 0)
    expected = owners - 1
    if shared:
        for dg in range(1, ng):
            for other in range(ns):
                pl.semaphore_signal(
                    barrier, inc=1, device_id={"groups": (g + dg) % ng, "space": other},
                    device_id_type=MESH,
                )
                expected += 1
        for dc in range(1, nc):
            pl.semaphore_signal(
                barrier, inc=1, device_id={"clip": (core + dc) % nc}, device_id_type=MESH
            )
            expected += 1
    weight_copy = pltpu.make_async_copy(weights_any.at[0], taps, raw_sem)

    def share_load(col, part):
        lanes = pl.ds(pl.multiple_of(part * share_lanes, LANES), share_lanes)
        return pltpu.make_async_copy(
            shares_any.at[1, :, pl.ds(col * share_rows, share_rows), lanes],
            shares.at[t, col, part], share_sem.at[col, part],
        )

    loads = [
        pltpu.make_async_copy(source, target, load_sem.at[i])
        for i, (source, target) in enumerate((
            (feat_any, feat), (gains_any, gains), (owner_any, owner_of),
            (biases_any, biases), (latent_any, latent_rows),
        ))
    ]
    for copy in loads[:2]:
        copy.start()
    share_load(column_of, part_of).start()
    for copy in loads[2:]:
        copy.start()
    weight_copy.start()

    def others(act):
        for col in range(columns):
            for part in range(parts):
                pl.when((column_of != col) | (part_of != part))(lambda: act(share_load(col, part)))

    others(lambda copy: copy.start())

    field[0:2] = jnp.zeros((2,) + field.shape[1:], field.dtype)

    @pl.when(t == 0)
    def _():
        inner[0:2] = jnp.zeros((2,) + inner.shape[1:], inner.dtype)

    @pl.when(s == 0)
    def _():
        edge_in[0] = jnp.zeros(edge_in.shape[1:], edge_in.dtype)
        inner[:, 0:1] = jnp.zeros((inner.shape[0], 1) + inner.shape[2:], inner.dtype)

    @pl.when(s == ns - 1)
    def _():
        edge_in[1] = jnp.zeros(edge_in.shape[1:], edge_in.dtype)
        inner[:, rows + 1 :] = jnp.zeros((inner.shape[0], 1) + inner.shape[2:], inner.dtype)

    for copy in loads[:2]:
        copy.wait()
    inputs = feat[...].reshape(cells, width).astype(jnp.float32)

    def block_copy(c, f, target, send_sem):
        span = field.at[pl.ds(2 + frames * c + size * f, size)]
        return pltpu.make_async_remote_copy(
            src_ref=span, dst_ref=span, send_sem=send_sem, recv_sem=block_recv.at[c, f],
            device_id={"tm": target}, device_id_type=MESH,
        )

    def slab_copy(source, target):
        return pltpu.make_async_remote_copy(
            src_ref=slab_out.at[target], dst_ref=slab_in.at[source],
            send_sem=slab_send.at[target], recv_sem=slab_recv.at[source],
            device_id={"tm": target}, device_id_type=MESH,
        )

    def edge_copy(side, source, target):
        return pltpu.make_async_remote_copy(
            src_ref=edge_out.at[side, target], dst_ref=edge_in.at[side, source],
            send_sem=edge_send.at[side, target], recv_sem=edge_recv.at[side, source],
            device_id={"tm": target, "space": (s + 1 - 2 * side + ns) % ns}, device_id_type=MESH,
        )

    def sided(side, act):
        pl.when(s < ns - 1 if side == 0 else s > 0)(act)

    def fed(side, act):
        pl.when(s > 0 if side == 0 else s < ns - 1)(act)

    def line_copy(q, target, send_sem):
        piece = shares.at[q, column_of, part_of]
        return pltpu.make_async_remote_copy(
            src_ref=piece, dst_ref=piece, send_sem=send_sem, recv_sem=line_recv.at[q],
            device_id={"tm": target}, device_id_type=MESH,
        )

    def plane_copy(q, col, d):
        piece = shares.at[q, col, part_of]
        peer = (column_of + d) % columns
        return pltpu.make_async_remote_copy(
            src_ref=piece, dst_ref=piece,
            send_sem=plane_send.at[q, d], recv_sem=plane_recv.at[q, col],
            device_id={"groups": peer // ns, "space": peer % ns}, device_id_type=MESH,
        )

    def core_copy(q, col, part, d):
        piece = shares.at[q, col, part]
        return pltpu.make_async_remote_copy(
            src_ref=piece, dst_ref=piece,
            send_sem=core_send.at[q, col, d], recv_sem=core_recv.at[q, col, part],
            device_id={"clip": (core + d) % nc}, device_id_type=MESH,
        )

    def beside_line(act):
        for target in (t - 1, t + 1):
            pl.when((target >= 0) & (target < n))(functools.partial(act, (target + n) % n))

    def around(act):
        def each(d, carry):
            act((t + d) % n)
            return carry

        lax.fori_loop(1, n, each, 0)

    reach = beside_line if relays else around
    def blocks(act):
        def each(spot):
            for f in range(cuts):
                act(block_copy(t, f, spot, block_send.at[spot, f]))

        reach(each)

    def line_of(act):
        return lambda spot: act(line_copy(t, spot, line_send.at[spot]))

    middle = (t == 1) | (t == 2)
    low = t == 1
    end, mate, far = [jnp.where(low, one, two) for one, two in ((0, 3), (2, 1), (3, 0))]
    courses = ((end, mate), (mate, end), (far, end))

    def relay_copy(i, f):
        q, target = courses[i]
        return block_copy(q, f, target, relay_send.at[i, f])

    def line_relay(i):
        q, target = courses[i]
        return line_copy(q, target, line_relay_send.at[i])

    def relay_block(*which):
        for f in range(cuts):
            for i in which:
                q = courses[i][0]
                block_copy(q, f, q, block_send.at[q, f]).wait_recv()
                relay_copy(i, f).start()

    def pass_on(q):
        line_copy(q, q, line_send.at[q]).wait_recv()
        if shared:
            for d in range(1, columns):
                plane_copy(q, column_of, d).start()
            for d in range(1, nc):
                core_copy(q, column_of, part_of, d).start()

    def cross(q):
        for d in range(1, columns):
            col = (column_of + d) % columns
            plane_copy(q, col, d).wait_recv()
            for dc in range(1, nc):
                core_copy(q, col, part_of, dc).start()

    def arrived(c):
        for f in range(cuts):
            block_copy(c, f, c, block_send.at[c, f]).wait_recv()

    grid_rows = rows + 2
    column = lax.broadcasted_iota(jnp.int32, (frames * grid_rows * cols, 1), 0) % cols

    def fold(values):
        part = values.shape[0] // pack
        return jnp.concatenate([values[j * part : (j + 1) * part] for j in range(pack)], axis=1)

    def unfold(pieces):
        return jnp.concatenate(
            [
                jnp.concatenate([piece[:, j * out : (j + 1) * out] for piece in pieces], axis=1)
                for j in range(pack)
            ],
            axis=0,
        )

    def beside(left, middle, right):
        count = left.shape[0]
        mark = column[:count]
        left = jnp.where(mark == 0, 0.0, pltpu.roll(left, 1, 0))
        right = jnp.where(mark == cols - 1, 0.0, pltpu.roll(right, count - 1, 0))
        return left + middle + right

    def one(b):
        sums = []
        for r in range(3):
            total = None
            for a in range(3):
                block = field[pl.ds(frames * b + a, frames)]
                term = lax.dot_general(
                    block.reshape(cells, width), taps[3 * a + r],
                    (((1,), (1,)), ((), ())), preferred_element_type=jnp.float32,
                )
                total = term if total is None else total + term
            sums.append(total.reshape(frames, rows, cols, 3 * out))
        blank = jnp.zeros((frames, 1, cols, 3 * out), jnp.float32)
        two = jnp.concatenate([blank] * 2, axis=1)
        wide = (
            jnp.concatenate([sums[2], two], axis=1)
            + jnp.concatenate([blank, sums[1], blank], axis=1)
            + jnp.concatenate([two, sums[0]], axis=1)
        ).reshape(frames * grid_rows * cols, 3 * out)
        summed = beside(wide[:, :out], wide[:, out : 2 * out], wide[:, 2 * out :])
        summed = summed.reshape(frames, grid_rows, cols, out)
        edges = (
            summed[:, rows + 1 :].reshape(frames * cols, out),
            summed[:, :1].reshape(frames * cols, out),
        )
        packed = fold(summed[:, 1 : rows + 1].reshape(cells, out)).astype(jnp.bfloat16)

        @pl.when(b == t)
        def _():
            slab_in[pl.ds(t, 1)] = packed[None]

        @pl.when(b != t)
        def _():
            slab_out[pl.ds(b, 1)] = packed[None]
            slab_copy(t, b).start()

        for side in range(2):

            def give(side=side):
                edge_out[side, pl.ds(b, 1)] = fold(edges[side]).astype(jnp.bfloat16)[None]
                edge_copy(side, t, b).start()

            sided(side, give)

    def halo_copies(act):
        near, far = pl.ds(frames, 2), pl.ds(0, 2)
        own, body = pl.ds(2, frames), pl.ds(1, rows)
        up = {"tm": (t + 1) % n}
        more = t < n - 1

        def copy(i, here, source, target, device):
            pl.when(here)(
                lambda: act(
                    pltpu.make_async_remote_copy(
                        src_ref=inner.at[source], dst_ref=inner.at[target],
                        send_sem=halo_send.at[i], recv_sem=halo_recv.at[i],
                        device_id=device, device_id_type=MESH,
                    )
                )
            )

        left, right = {"space": (s + ns - 1) % ns}, {"space": (s + 1) % ns}
        first, last = pl.ds(1, 1), pl.ds(rows, 1)
        above, below = pl.ds(0, 1), pl.ds(rows + 1, 1)
        copy(0, more, (near, body), (far, body), up)
        copy(1, more & (s > 0), (near, first), (far, below), up | left)
        copy(2, more & (s < ns - 1), (near, last), (far, above), up | right)
        copy(3, s > 0, (own, first), (own, below), left)
        copy(4, s < ns - 1, (own, last), (own, above), right)

    def halo_came():
        def wait(i, here, target):
            def act():
                span = inner.at[target]
                pltpu.make_async_remote_copy(
                    src_ref=span, dst_ref=span, send_sem=halo_send.at[i],
                    recv_sem=halo_recv.at[i], device_id={"tm": t}, device_id_type=MESH,
                ).wait_recv()

            pl.when(here)(act)

        far, own, body = pl.ds(0, 2), pl.ds(2, frames), pl.ds(1, rows)
        above, below = pl.ds(0, 1), pl.ds(rows + 1, 1)
        wait(3, s < ns - 1, (own, below))
        wait(4, s > 0, (own, above))
        wait(0, t > 0, (far, body))
        wait(1, (t > 0) & (s < ns - 1), (far, below))
        wait(2, (t > 0) & (s > 0), (far, above))

    def kernel_of(tap):
        return jnp.concatenate(
            [
                jnp.concatenate([shares[q, col, part, tap] for part in range(parts)], axis=1)
                for q in range(n)
                for col in range(columns)
            ],
            axis=0,
        )

    field[pl.ds(2 + frames * t, frames)] = norm_silu(inputs, gains[0:1]).astype(
        jnp.bfloat16
    ).reshape(frames, rows, cols, width)
    for copy in loads[2:]:
        copy.wait()
    toks = owner_of.shape[1]
    before = lax.broadcasted_iota(jnp.int32, (toks, toks), 0)
    after = lax.broadcasted_iota(jnp.int32, (toks, toks), 1)
    owner = owner_of[...]
    owner_column = jnp.sum(jnp.where(before == after, owner, 0), axis=1, keepdims=True)
    same = (owner_column == owner) & (before < after)
    rank = jnp.sum(jnp.where(same, 1, 0), axis=0, keepdims=True)
    slots = lax.broadcasted_iota(jnp.int32, (owners * SUBLANES, toks), 0)
    placing[...] = jnp.where(slots == owner * SUBLANES + rank, 1.0, 0.0).astype(jnp.bfloat16)
    share_load(column_of, part_of).wait()
    pl.semaphore_wait(barrier, expected)
    start = lambda copy: copy.start()
    reach(line_of(start))
    blocks(start)
    weight_copy.wait()
    if relays:
        order = ((0, 1, 2, 3), (3, 2, 0, 1), (0, 3, 1, 2), (3, 2, 0, 1))
        flow = ((1, 2, 3), (0, 2, 3), (3, 1, 0), (2, 1, 0))

        def forward():
            pass_on(end)
            pass_on(mate)
            relay_block(0, 1)
            line_relay(0).start()
            line_relay(1).start()
            relay_block(2)

        def last(q):
            pass_on(q)
            line_relay(2).start()

        before = (
            ((), ((pass_on, 1), (arrived, 1)), ((arrived, 2),), ((pass_on, 2), (arrived, 3))),
            ((), (), ((last, 3),), ()),
            ((), (), ((last, 0),), ()),
            (((pass_on, 2), (arrived, 2)), ((arrived, 1),), ((pass_on, 1), (arrived, 0)), ()),
        )

        def pick(table, k):
            spot = table[0][k]
            for i in range(1, n):
                spot = jnp.where(t == i, table[i][k], spot)
            return spot

        def chosen(table, k):
            spot = pick(table, 0)
            for kk in range(1, len(table[0])):
                spot = jnp.where(k == kk, pick(table, kk), spot)
            return spot

        pl.when(middle)(forward)

        def step(k, carry):
            for i in range(n):
                for kk in range(n):
                    if before[i][kk]:

                        @pl.when((t == i) & (k == kk))
                        def _():
                            for act, c in before[i][kk]:
                                act(c)

            one(chosen(order, k))
            return carry

        lax.fori_loop(0, n, step, 0)
        pl.when(jnp.logical_not(middle))(lambda: pass_on(pick(flow, 2)))
    else:

        def hold(d, carry):
            arrived((t + d) % n)
            return carry

        lax.fori_loop(1, n, hold, 0)

        def step(d, carry):
            one((t + d) % n)
            return carry

        lax.fori_loop(1, n + 1, step, 0)

    def came(k, carry):
        q = (t + k) % n
        pl.when(k > 0)(lambda: slab_copy(q, q).wait_recv())
        for side in range(2):
            fed(side, lambda: edge_copy(side, q, q).wait_recv())
        return carry

    lax.fori_loop(0, n, came, 0)
    hidden = unfold([slab_in[q].astype(jnp.float32) for q in range(n)])
    top, bottom = [
        unfold([edge_in[side, q].astype(jnp.float32) for q in range(n)]).reshape(
            frames, 1, cols, width
        )
        for side in range(2)
    ]
    hidden = hidden.reshape(frames, rows, cols, width)
    if rows > 1:
        hidden = jnp.concatenate(
            [hidden[:, :1] + top, hidden[:, 1 : rows - 1], hidden[:, rows - 1 :] + bottom], axis=1
        )
    else:
        hidden = hidden + top + bottom
    hidden = hidden.reshape(cells, width) + biases[0:1]
    inner[2:, 1 : rows + 1] = norm_silu(hidden, gains[1:2]).astype(jnp.bfloat16).reshape(
        frames, rows, cols, width
    )
    halo_copies(start)
    if not relays:

        def passed(d, carry):
            pass_on((t + d) % n)
            return carry

        lax.fori_loop(1, n, passed, 0)
    if shared:

        def crossed(k, carry):
            if relays:
                q = chosen(flow, k)
            else:
                q = (t + 1 + k) % n
            cross(q)
            return carry

        lax.fori_loop(0, n - 1, crossed, 0)
    others(lambda copy: copy.wait())
    halo_came()
    if shared:

        def joined(k, carry):
            q = (t + 1 + k) % n
            for col in range(columns):
                for d in range(1, nc):
                    core_copy(q, col, (core + d) % nc, d).wait_recv()
            return carry

        lax.fori_loop(0, n - 1, joined, 0)
    sums = []
    for e in range(3):
        total = None
        for a in range(3):
            for r in range(3):
                block = inner[a : a + frames, r : r + rows].reshape(cells, width)
                term = lax.dot_general(
                    block, kernel_of(9 * a + 3 * r + e),
                    (((1,), (1,)), ((), ())), preferred_element_type=jnp.float32,
                )
                total = term if total is None else total + term
        sums.append(total)
    hidden = beside(*sums) + biases[1:2]
    merged = feat[...].reshape(cells, width).astype(jnp.float32) + hidden
    active = norm_silu(merged, gains[2:3]).astype(jnp.bfloat16)
    rest = jnp.zeros((LANES - 4 * width_latent, width), jnp.bfloat16)
    latent_wide = jnp.concatenate([latent_rows[...]] * 4 + [rest], axis=0)
    latent = lax.dot_general(
        active, latent_wide, (((1,), (1,)), ((), ())), preferred_element_type=jnp.float32
    )
    cell = lax.broadcasted_iota(jnp.int32, (cells, LANES), 0)
    lane = lax.broadcasted_iota(jnp.int32, (cells, LANES), 1)
    corner = (cell // cols % 2) * 2 + cell % 2
    alive = (t * frames + cell // (rows * cols) < count[0]) & (corner == 0)
    flagged = jnp.where((lane == 4 * width_latent) & alive, 1.0, 0.0)
    patches = jnp.where(lane // width_latent == corner, latent, flagged).astype(jnp.bfloat16)
    spot = lax.broadcasted_iota(jnp.int32, (toks, cells), 1)
    patch = (spot // (2 * cols)) * (cols // 2) + spot % cols // 2
    mine = patch == lax.broadcasted_iota(jnp.int32, (toks, cells), 0)
    patches = jnp.dot(
        jnp.where(mine, 1.0, 0.0).astype(jnp.bfloat16), patches, preferred_element_type=jnp.float32
    ).astype(jnp.bfloat16)
    outgoing = jnp.dot(
        placing[...], patches, preferred_element_type=jnp.float32
    ).astype(jnp.bfloat16)
    tok_out[...] = outgoing.reshape(owners, SUBLANES, LANES)
    tok_in[pl.ds(me, 1)] = tok_out[pl.ds(me, 1)]

    def tok_copy(source, target):
        return pltpu.make_async_remote_copy(
            src_ref=tok_out.at[target], dst_ref=tok_in.at[source],
            send_sem=tok_send.at[target], recv_sem=tok_recv.at[source],
            device_id={"tm": target // ns, "space": target % ns}, device_id_type=MESH,
        )

    def tok_start(d, carry):
        tok_copy(me, (me + d) % owners).start()
        return carry

    def tok_wait(d, carry):
        o = (me + d) % owners
        tok_copy(o, o).wait_recv()
        return carry

    def tok_sent(d, carry):
        tok_copy(me, (me + d) % owners).wait_send()
        return carry

    lax.fori_loop(1, owners, tok_start, 0)
    blocks(lambda copy: copy.wait_send())
    reach(line_of(lambda copy: copy.wait_send()))
    if relays:

        @pl.when(middle)
        def _():
            for i in range(3):
                for f in range(cuts):
                    relay_copy(i, f).wait_send()
                line_relay(i).wait_send()

    def sent(c, carry):
        pl.when(c != t)(lambda: slab_copy(t, c).wait_send())
        for side in range(2):
            sided(side, lambda: edge_copy(side, t, c).wait_send())
        if shared:

            @pl.when(c != t)
            def _():
                for d in range(1, columns):
                    plane_copy(c, column_of, d).wait_send()
                for col in range(columns):
                    for d in range(1, nc):
                        core_copy(c, col, part_of, d).wait_send()

        return carry

    lax.fori_loop(0, n, sent, 0)
    halo_copies(lambda copy: copy.wait_send())
    lax.fori_loop(1, owners, tok_wait, 0)
    row = lax.broadcasted_iota(jnp.int32, (owners * most, owners * SUBLANES), 0)
    held = lax.broadcasted_iota(jnp.int32, (owners * most, owners * SUBLANES), 1)
    inner = held % SUBLANES
    chosen = (row == held // SUBLANES * most + inner) & (inner < most)
    tokens_out[...] = jnp.dot(
        jnp.where(chosen, 1.0, 0.0).astype(jnp.bfloat16),
        tok_in[...].reshape(owners * SUBLANES, LANES),
        preferred_element_type=jnp.float32,
    ).astype(jnp.bfloat16)
    lax.fori_loop(1, owners, tok_sent, 0)


def embedder(channels, tokens, weight, bias, packed):
    held = tokens[...]
    projected = jnp.dot(held[:, :channels], weight[...], preferred_element_type=jnp.float32)
    flags = held[:, channels : channels + 1].astype(jnp.float32)
    packed[...] = ((projected + bias[...]) * flags).astype(jnp.bfloat16)


def shards(
    features,
    frame_counts,
    routes,
    norm_gains,
    conv_weights,
    conv_biases,
    latent_weight,
    embed_weight,
    embed_bias,
):
    feat = features[0]
    frames, rows, cols, width = feat.shape
    cells = frames * rows * cols
    n, ns = lax.axis_size("tm"), lax.axis_size("space")
    ng, nc = lax.axis_size("groups"), lax.axis_size("clip")
    owners = n * ns
    out = conv_weights.shape[1]
    pack = max(1, LANES // out)
    latents = latent_weight.shape[1]
    tok_count = routes.shape[1]
    most = (tok_count + owners - 1) // owners + 1
    vmem = pl.BlockSpec(memory_space=pltpu.VMEM)
    hbm = pl.BlockSpec(memory_space=pltpu.HBM)
    away = lambda value: pltpu.with_memory_space_constraint(value, pltpu.HBM)
    dma = pltpu.SemaphoreType.DMA
    field = pltpu.VMEM((n * frames + 2, rows, cols, width), jnp.bfloat16)
    inner = pltpu.VMEM((frames + 2, rows + 2, cols, width), jnp.bfloat16)
    slab = pltpu.VMEM((n, cells // pack, pack * out), jnp.bfloat16)
    edge = pltpu.VMEM((2, n, frames * cols // pack, pack * out), jnp.bfloat16)
    columns, parts = ng * ns, nc
    if out % (SUBLANES * columns) or width % (LANES * parts):
        columns = parts = 1
    taps = conv_weights.shape[2]
    shares = pltpu.VMEM((n, columns, parts, taps, out // columns, width // parts), jnp.bfloat16)
    cuts = CUTS if frames % CUTS == 0 else 1
    tok = pltpu.VMEM((owners, SUBLANES, LANES), jnp.bfloat16)
    tokens = pl.pallas_call(
        functools.partial(encoder, n, ns, ng, nc, most, latents),
        out_shape=jax.ShapeDtypeStruct((owners * most, LANES), jnp.bfloat16),
        in_specs=[hbm] * 7 + [pl.BlockSpec(memory_space=pltpu.SMEM)],
        out_specs=vmem,
        scratch_shapes=[
            pltpu.VMEM(feat.shape, feat.dtype),
            pltpu.VMEM(norm_gains.shape, norm_gains.dtype),
            pltpu.VMEM(conv_biases.shape, conv_biases.dtype),
            pltpu.VMEM((latents, width), latent_weight.dtype),
            pltpu.VMEM((1, tok_count), routes.dtype),
            field, inner,
            pltpu.VMEM((9, 3 * out, width), jnp.bfloat16),
            shares,
            pltpu.VMEM((owners * SUBLANES, tok_count), jnp.bfloat16),
            slab, slab, edge, edge, tok, tok,
            dma((5,)), dma, dma((columns, parts)),
            dma((n, cuts)), dma((3, cuts)), dma((n, cuts)),
            dma((n,)), dma((n,)), dma((2, n)), dma((2, n)), dma((5,)), dma((5,)),
            dma((n,)), dma((3,)), dma((n,)),
            dma((n, columns)), dma((n, columns)), dma((n, columns, nc)), dma((n, columns, nc)),
            dma((owners,)), dma((owners,)),
        ],
        compiler_params=pltpu.CompilerParams(
            collective_id=0, has_side_effects=True, vmem_limit_bytes=GRANT
        ),
    )(
        away(feat),
        away(conv_weights.transpose(0, 2, 1, 3).reshape(2, 9, 3 * out, width)),
        away(conv_weights.transpose(0, 2, 1, 3)),
        away(norm_gains),
        away(conv_biases),
        away(latent_weight.T),
        away(routes.reshape(1, tok_count)),
        frame_counts,
    )
    channels = 4 * latents
    embed = embed_weight.shape[1]
    chunk = embed // 1 if embed % (1 * LANES) == 0 else embed
    packed = pl.pallas_call(
        functools.partial(embedder, channels),
        grid=(embed // chunk,),
        out_shape=jax.ShapeDtypeStruct((owners * most, embed), jnp.bfloat16),
        in_specs=[
            pl.BlockSpec((owners * most, LANES), lambda i: (0, 0)),
            pl.BlockSpec((channels, chunk), lambda i: (0, i)),
            pl.BlockSpec((1, chunk), lambda i: (0, i)),
        ],
        out_specs=pl.BlockSpec((owners * most, chunk), lambda i: (0, i)),
        compiler_params=pltpu.CompilerParams(vmem_limit_bytes=GRANT),
    )(tokens, embed_weight, embed_bias.reshape(1, embed))
    return packed[None]


def solution(mesh):
    return jax.shard_map(
        shards,
        mesh=mesh,
        in_specs=(
            P(("groups", "clip"), "tm", "space", None, None),
            P(("groups", "clip")),
            P(("groups", "clip"), ("tm", "space"), None),
            P(),
            P(None, "tm", None, None),
            P(),
            P(),
            P(),
            P(),
        ),
        out_specs=P(("groups", "clip"), ("tm", "space"), None),
        check_vma=False,
    )
```

```python
import functools

import jax
import jax.numpy as jnp
from jax import lax
from jax.experimental import pallas as pl
from jax.experimental.pallas import tpu as pltpu
from jax.sharding import PartitionSpec as P

MESH = pl.DeviceIdType.MESH
LANES = 128
SUBLANES = 16
CUTS = 4
BITS = 3
GRANT = 28 << 20


def norm_silu(values, gain):
    scale = lax.rsqrt(jnp.mean(values * values, axis=-1, keepdims=True) + 1e-06)
    scaled = values * scale * gain
    return scaled / (1.0 + jnp.exp(-scaled))


def encoder(
    n, ns, ng, nc, most, width_latent,
    feat_any, weights_any, shares_any, gains_any, biases_any, latent_any, owner_any, count,
    tokens_out,
    feat, gains, biases, latent_rows, owner_of, field, inner, taps, mine, shares, placing, slab_out, slab_in, edge_out, edge_in, tok_out, tok_in,
    load_sem, raw_sem, share_sem, block_send, relay_send, block_recv, slab_sem, edge_sem,
    halo_send, halo_recv, line_send, line_relay_send, line_recv, plane_recv, bulk_sem, tok_sem,
):
    t = lax.axis_index("tm")
    s = lax.axis_index("space")
    g = lax.axis_index("groups")
    core = lax.axis_index("clip")
    me = t * ns + s
    owners = n * ns
    frames, rows, cols, width = feat.shape
    cells = frames * rows * cols
    out = weights_any.shape[2] // 3
    cuts = block_recv.shape[1]
    size = frames // cuts
    pack = max(1, LANES // out)
    relays = n == 4
    columns, parts, share_taps, share_rows, share_lanes = shares.shape[1:]
    bits = line_recv.shape[1]
    bit = share_taps // bits
    shared = columns > 1
    column_of = g * ns + s if shared else 0
    part_of = core if shared else 0

    barrier = pltpu.get_barrier_semaphore()

    def greet(d, carry):
        o = (me + d) % owners
        pl.semaphore_signal(
            barrier, inc=1, device_id={"tm": o // ns, "space": o % ns}, device_id_type=MESH
        )
        return carry

    lax.fori_loop(1, owners, greet, 0)
    expected = owners - 1
    if shared:
        for dg in range(1, ng):
            for other in range(ns):
                pl.semaphore_signal(
                    barrier, inc=1, device_id={"groups": (g + dg) % ng, "space": other},
                    device_id_type=MESH,
                )
                expected += 1
        for dc in range(1, nc):
            pl.semaphore_signal(
                barrier, inc=1, device_id={"clip": (core + dc) % nc}, device_id_type=MESH
            )
            expected += 1
    weight_copy = pltpu.make_async_copy(weights_any.at[0], taps, raw_sem)

    def share_load(col, part, target, sem):
        lanes = pl.ds(pl.multiple_of(part * share_lanes, LANES), share_lanes)
        return pltpu.make_async_copy(
            shares_any.at[1, :, pl.ds(col * share_rows, share_rows), lanes], target, sem
        )

    mine_load = share_load(column_of, part_of, mine, share_sem.at[0])
    loads = [
        pltpu.make_async_copy(source, target, load_sem.at[i])
        for i, (source, target) in enumerate((
            (feat_any, feat), (gains_any, gains), (owner_any, owner_of),
            (biases_any, biases), (latent_any, latent_rows),
        ))
    ]
    for copy in loads[:2]:
        copy.start()
    mine_load.start()
    for copy in loads[2:]:
        copy.start()
    weight_copy.start()

    for col in range(columns):
        for part in range(parts):
            share_load(col, part, shares.at[t, col, part], share_sem.at[1]).start()

    field[0:2] = jnp.zeros((2,) + field.shape[1:], field.dtype)

    @pl.when(t == 0)
    def _():
        inner[0:2] = jnp.zeros((2,) + inner.shape[1:], inner.dtype)

    @pl.when(s == 0)
    def _():
        edge_in[0] = jnp.zeros(edge_in.shape[1:], edge_in.dtype)
        inner[:, 0:1] = jnp.zeros((inner.shape[0], 1) + inner.shape[2:], inner.dtype)

    @pl.when(s == ns - 1)
    def _():
        edge_in[1] = jnp.zeros(edge_in.shape[1:], edge_in.dtype)
        inner[:, rows + 1 :] = jnp.zeros((inner.shape[0], 1) + inner.shape[2:], inner.dtype)

    for copy in loads[:2]:
        copy.wait()
    inputs = feat[...].reshape(cells, width).astype(jnp.float32)

    def block_copy(c, f, target, send_sem):
        span = field.at[pl.ds(2 + frames * c + size * f, size)]
        return pltpu.make_async_remote_copy(
            src_ref=span, dst_ref=span, send_sem=send_sem, recv_sem=block_recv.at[c, f],
            device_id={"tm": target}, device_id_type=MESH,
        )

    def slab_copy(source, target):
        return pltpu.make_async_remote_copy(
            src_ref=slab_out.at[target], dst_ref=slab_in.at[source],
            send_sem=slab_sem.at[0], recv_sem=slab_sem.at[1],
            device_id={"tm": target}, device_id_type=MESH,
        )

    def edge_copy(side, source, target):
        return pltpu.make_async_remote_copy(
            src_ref=edge_out.at[side, target], dst_ref=edge_in.at[side, source],
            send_sem=edge_sem.at[0, side], recv_sem=edge_sem.at[1, side],
            device_id={"tm": target, "space": (s + 1 - 2 * side + ns) % ns}, device_id_type=MESH,
        )

    def gathered(ref, send_sem, recv_sem=None):
        return pltpu.make_async_remote_copy(
            src_ref=ref, dst_ref=ref, send_sem=send_sem,
            recv_sem=send_sem if recv_sem is None else recv_sem,
            device_id={"tm": t}, device_id_type=MESH,
        )

    def sided(side, act):
        pl.when(s < ns - 1 if side == 0 else s > 0)(act)

    def fed(side, act):
        pl.when(s > 0 if side == 0 else s < ns - 1)(act)

    def line_copy(q, k, target, send_sem, own=False):
        piece = shares.at[q, column_of, part_of, pl.ds(bit * k, bit)]
        return pltpu.make_async_remote_copy(
            src_ref=mine.at[pl.ds(bit * k, bit)] if own else piece, dst_ref=piece,
            send_sem=send_sem, recv_sem=line_recv.at[q, k],
            device_id={"tm": target}, device_id_type=MESH,
        )

    def plane_copy(q, k, d):
        piece = shares.at[q, column_of, part_of, pl.ds(bit * k, bit)]
        peer = (column_of + d) % columns
        return pltpu.make_async_remote_copy(
            src_ref=piece, dst_ref=piece, send_sem=bulk_sem.at[0],
            recv_sem=plane_recv.at[(q - t + n) % n - 1, k],
            device_id={"groups": peer // ns, "space": peer % ns}, device_id_type=MESH,
        )

    def core_copy(q, col, k, d):
        piece = shares.at[q, col, part_of, pl.ds(bit * k, bit)]
        return pltpu.make_async_remote_copy(
            src_ref=piece, dst_ref=piece, send_sem=bulk_sem.at[1], recv_sem=bulk_sem.at[2],
            device_id={"clip": (core + d) % nc}, device_id_type=MESH,
        )

    def beside_line(act):
        for way in range(2):
            target = t - 1 + 2 * way
            pl.when((target >= 0) & (target < n))(
                functools.partial(act, (target + n) % n, way)
            )

    def around(act):
        def each(d, carry):
            act((t + d) % n, 0)
            return carry

        lax.fori_loop(1, n, each, 0)

    reach = beside_line if relays else around
    def send_blocks(spot, way):
        for f in range(cuts):
            block_copy(t, f, spot, block_send.at[way]).start()

    def send_lines(spot, way):
        for k in range(bits):
            line_copy(t, k, spot, line_send.at[way], own=True).start()

    middle = (t == 1) | (t == 2)
    low = t == 1
    end, mate, far = [jnp.where(low, one, two) for one, two in ((0, 3), (2, 1), (3, 0))]
    courses = ((end, mate), (mate, end), (far, end))

    def relay_copy(i, f):
        q, target = courses[i]
        return block_copy(q, f, target, relay_send.at[i])

    def line_relay(i, k):
        q, target = courses[i]
        return line_copy(q, k, target, line_relay_send.at[i])

    def relay_block(*which):
        for f in range(cuts):
            for i in which:
                q = courses[i][0]
                block_copy(q, f, q, block_send.at[0]).wait_recv()
                relay_copy(i, f).start()

    def pass_bit(q, k):
        if shared:
            for d in range(1, columns):
                plane_copy(q, k, d).start()
            for d in range(1, nc):
                core_copy(q, column_of, k, d).start()

    def line_came(q, k):
        line_copy(q, k, q, line_send.at[0]).wait_recv()

    def pass_on(q):
        for k in range(bits):
            line_came(q, k)
            pass_bit(q, k)

    def cross(q):
        for k in range(bits):
            gathered(
                shares.at[0, pl.ds(0, columns - 1), 0, pl.ds(0, bit)],
                bulk_sem.at[0], plane_recv.at[(q - t + n) % n - 1, k],
            ).wait_recv()
            for d in range(1, columns):
                for dc in range(1, nc):
                    core_copy(q, (column_of + d) % columns, k, dc).start()

    def arrived(c):
        for f in range(cuts):
            block_copy(c, f, c, block_send.at[0]).wait_recv()

    grid_rows = rows + 2
    column = lax.broadcasted_iota(jnp.int32, (frames * grid_rows * cols, 1), 0) % cols

    def fold(values):
        part = values.shape[0] // pack
        return jnp.concatenate([values[j * part : (j + 1) * part] for j in range(pack)], axis=1)

    def unfold(pieces):
        return jnp.concatenate(
            [
                jnp.concatenate([piece[:, j * out : (j + 1) * out] for piece in pieces], axis=1)
                for j in range(pack)
            ],
            axis=0,
        )

    def beside(left, middle, right):
        count = left.shape[0]
        mark = column[:count]
        left = jnp.where(mark == 0, 0.0, pltpu.roll(left, 1, 0))
        right = jnp.where(mark == cols - 1, 0.0, pltpu.roll(right, count - 1, 0))
        return left + middle + right

    def one(b):
        sums = []
        for r in range(3):
            total = None
            for a in range(3):
                block = field[pl.ds(frames * b + a, frames)]
                term = lax.dot_general(
                    block.reshape(cells, width), taps[3 * a + r],
                    (((1,), (1,)), ((), ())), preferred_element_type=jnp.float32,
                )
                total = term if total is None else total + term
            sums.append(total.reshape(frames, rows, cols, 3 * out))
        blank = jnp.zeros((frames, 1, cols, 3 * out), jnp.float32)
        two = jnp.concatenate([blank] * 2, axis=1)
        wide = (
            jnp.concatenate([sums[2], two], axis=1)
            + jnp.concatenate([blank, sums[1], blank], axis=1)
            + jnp.concatenate([two, sums[0]], axis=1)
        ).reshape(frames * grid_rows * cols, 3 * out)
        summed = beside(wide[:, :out], wide[:, out : 2 * out], wide[:, 2 * out :])
        summed = summed.reshape(frames, grid_rows, cols, out)
        edges = (
            summed[:, rows + 1 :].reshape(frames * cols, out),
            summed[:, :1].reshape(frames * cols, out),
        )
        packed = fold(summed[:, 1 : rows + 1].reshape(cells, out)).astype(jnp.bfloat16)

        @pl.when(b == t)
        def _():
            slab_in[pl.ds(t, 1)] = packed[None]

        @pl.when(b != t)
        def _():
            slab_out[pl.ds(b, 1)] = packed[None]
            slab_copy(t, b).start()

        for side in range(2):

            def give(side=side):
                edge_out[side, pl.ds(b, 1)] = fold(edges[side]).astype(jnp.bfloat16)[None]
                edge_copy(side, t, b).start()

            sided(side, give)

    def halo_copies(act):
        near, far = pl.ds(frames, 2), pl.ds(0, 2)
        own, body = pl.ds(2, frames), pl.ds(1, rows)
        up = {"tm": (t + 1) % n}
        more = t < n - 1

        def copy(i, here, source, target, device):
            pl.when(here)(
                lambda: act(
                    pltpu.make_async_remote_copy(
                        src_ref=inner.at[source], dst_ref=inner.at[target],
                        send_sem=halo_send.at[i], recv_sem=halo_recv.at[i],
                        device_id=device, device_id_type=MESH,
                    )
                )
            )

        left, right = {"space": (s + ns - 1) % ns}, {"space": (s + 1) % ns}
        first, last = pl.ds(1, 1), pl.ds(rows, 1)
        above, below = pl.ds(0, 1), pl.ds(rows + 1, 1)
        copy(0, more, (near, body), (far, body), up)
        copy(1, more & (s > 0), (near, first), (far, below), up | left)
        copy(2, more & (s < ns - 1), (near, last), (far, above), up | right)
        copy(3, s > 0, (own, first), (own, below), left)
        copy(4, s < ns - 1, (own, last), (own, above), right)

    def halo_came():
        def wait(i, here, target):
            def act():
                span = inner.at[target]
                pltpu.make_async_remote_copy(
                    src_ref=span, dst_ref=span, send_sem=halo_send.at[i],
                    recv_sem=halo_recv.at[i], device_id={"tm": t}, device_id_type=MESH,
                ).wait_recv()

            pl.when(here)(act)

        far, own, body = pl.ds(0, 2), pl.ds(2, frames), pl.ds(1, rows)
        above, below = pl.ds(0, 1), pl.ds(rows + 1, 1)
        wait(3, s < ns - 1, (own, below))
        wait(4, s > 0, (own, above))
        wait(0, t > 0, (far, body))
        wait(1, (t > 0) & (s < ns - 1), (far, below))
        wait(2, (t > 0) & (s > 0), (far, above))

    def kernel_of(tap):
        return jnp.concatenate(
            [
                jnp.concatenate([shares[q, col, part, tap] for part in range(parts)], axis=1)
                for q in range(n)
                for col in range(columns)
            ],
            axis=0,
        )

    field[pl.ds(2 + frames * t, frames)] = norm_silu(inputs, gains[0:1]).astype(
        jnp.bfloat16
    ).reshape(frames, rows, cols, width)
    for copy in loads[2:]:
        copy.wait()
    toks = owner_of.shape[1]
    before = lax.broadcasted_iota(jnp.int32, (toks, toks), 0)
    after = lax.broadcasted_iota(jnp.int32, (toks, toks), 1)
    owner = owner_of[...]
    owner_column = jnp.sum(jnp.where(before == after, owner, 0), axis=1, keepdims=True)
    same = (owner_column == owner) & (before < after)
    rank = jnp.sum(jnp.where(same, 1, 0), axis=0, keepdims=True)
    slots = lax.broadcasted_iota(jnp.int32, (owners * SUBLANES, toks), 0)
    placing[...] = jnp.where(slots == owner * SUBLANES + rank, 1.0, 0.0).astype(jnp.bfloat16)
    mine_load.wait()
    pl.semaphore_wait(barrier, expected)
    start = lambda copy: copy.start()
    reach(send_lines)
    reach(send_blocks)
    weight_copy.wait()
    if relays:
        order = ((0, 1, 2, 3), (3, 2, 0, 1), (0, 3, 1, 2), (3, 2, 0, 1))
        flow = ((1, 2, 3), (0, 2, 3), (3, 1, 0), (2, 1, 0))

        def forward():
            pass_on(end)
            pass_on(mate)
            relay_block(0, 1)
            for k in range(bits):
                line_relay(0, k).start()
                line_relay(1, k).start()
            relay_block(2)

        def last(q):
            for k in range(bits):
                line_came(q, k)
                line_relay(2, k).start()
                pass_bit(q, k)

        before = (
            ((), ((pass_on, 1), (arrived, 1)), ((arrived, 2),), ((pass_on, 2), (arrived, 3))),
            ((), (), ((last, 3),), ()),
            ((), (), ((last, 0),), ()),
            (((pass_on, 2), (arrived, 2)), ((arrived, 1),), ((pass_on, 1), (arrived, 0)), ()),
        )

        def pick(table, k):
            spot = table[0][k]
            for i in range(1, n):
                spot = jnp.where(t == i, table[i][k], spot)
            return spot

        def chosen(table, k):
            spot = pick(table, 0)
            for kk in range(1, len(table[0])):
                spot = jnp.where(k == kk, pick(table, kk), spot)
            return spot

        pl.when(middle)(forward)

        def step(k, carry):
            for i in range(n):
                for kk in range(n):
                    if before[i][kk]:

                        @pl.when((t == i) & (k == kk))
                        def _():
                            for act, c in before[i][kk]:
                                act(c)

            one(chosen(order, k))
            return carry

        lax.fori_loop(0, n, step, 0)
        pl.when(jnp.logical_not(middle))(lambda: pass_on(pick(flow, 2)))
    else:

        def hold(d, carry):
            arrived((t + d) % n)
            return carry

        lax.fori_loop(1, n, hold, 0)

        def step(d, carry):
            one((t + d) % n)
            return carry

        lax.fori_loop(1, n + 1, step, 0)

    gathered(slab_in.at[pl.ds(0, n - 1)], slab_sem.at[0], slab_sem.at[1]).wait_recv()
    for side in range(2):
        fed(side, lambda: gathered(edge_in.at[side], edge_sem.at[0, side], edge_sem.at[1, side]).wait_recv())
    hidden = unfold([slab_in[q].astype(jnp.float32) for q in range(n)])
    top, bottom = [
        unfold([edge_in[side, q].astype(jnp.float32) for q in range(n)]).reshape(
            frames, 1, cols, width
        )
        for side in range(2)
    ]
    hidden = hidden.reshape(frames, rows, cols, width)
    if rows > 1:
        hidden = jnp.concatenate(
            [hidden[:, :1] + top, hidden[:, 1 : rows - 1], hidden[:, rows - 1 :] + bottom], axis=1
        )
    else:
        hidden = hidden + top + bottom
    hidden = hidden.reshape(cells, width) + biases[0:1]
    inner[2:, 1 : rows + 1] = norm_silu(hidden, gains[1:2]).astype(jnp.bfloat16).reshape(
        frames, rows, cols, width
    )
    halo_copies(start)
    if not relays:

        def passed(d, carry):
            pass_on((t + d) % n)
            return carry

        lax.fori_loop(1, n, passed, 0)
    if shared:

        def crossed(k, carry):
            if relays:
                q = chosen(flow, k)
            else:
                q = (t + 1 + k) % n
            cross(q)
            return carry

        lax.fori_loop(0, n - 1, crossed, 0)
    pltpu.make_async_copy(shares.at[t], shares.at[t], share_sem.at[1]).wait()
    halo_came()
    if shared:

        gathered(shares.at[pl.ds(0, n - 1), :, 0], bulk_sem.at[1], bulk_sem.at[2]).wait_recv()
    sums = []
    for e in range(3):
        total = None
        for a in range(3):
            for r in range(3):
                block = inner[a : a + frames, r : r + rows].reshape(cells, width)
                term = lax.dot_general(
                    block, kernel_of(9 * a + 3 * r + e),
                    (((1,), (1,)), ((), ())), preferred_element_type=jnp.float32,
                )
                total = term if total is None else total + term
        sums.append(total)
    hidden = beside(*sums) + biases[1:2]
    merged = feat[...].reshape(cells, width).astype(jnp.float32) + hidden
    active = norm_silu(merged, gains[2:3]).astype(jnp.bfloat16)
    rest = jnp.zeros((LANES - 4 * width_latent, width), jnp.bfloat16)
    latent_wide = jnp.concatenate([latent_rows[...]] * 4 + [rest], axis=0)
    latent = lax.dot_general(
        active, latent_wide, (((1,), (1,)), ((), ())), preferred_element_type=jnp.float32
    )
    cell = lax.broadcasted_iota(jnp.int32, (cells, LANES), 0)
    lane = lax.broadcasted_iota(jnp.int32, (cells, LANES), 1)
    corner = (cell // cols % 2) * 2 + cell % 2
    alive = (t * frames + cell // (rows * cols) < count[0]) & (corner == 0)
    flagged = jnp.where((lane == 4 * width_latent) & alive, 1.0, 0.0)
    patches = jnp.where(lane // width_latent == corner, latent, flagged).astype(jnp.bfloat16)
    spot = lax.broadcasted_iota(jnp.int32, (toks, cells), 1)
    patch = (spot // (2 * cols)) * (cols // 2) + spot % cols // 2
    mine = patch == lax.broadcasted_iota(jnp.int32, (toks, cells), 0)
    patches = jnp.dot(
        jnp.where(mine, 1.0, 0.0).astype(jnp.bfloat16), patches, preferred_element_type=jnp.float32
    ).astype(jnp.bfloat16)
    outgoing = jnp.dot(
        placing[...], patches, preferred_element_type=jnp.float32
    ).astype(jnp.bfloat16)
    tok_out[...] = outgoing.reshape(owners, SUBLANES, LANES)
    tok_in[pl.ds(me, 1)] = tok_out[pl.ds(me, 1)]

    def tok_start(d, carry):
        target = (me + d) % owners
        pltpu.make_async_remote_copy(
            src_ref=tok_out.at[target], dst_ref=tok_in.at[me],
            send_sem=tok_sem.at[0], recv_sem=tok_sem.at[1],
            device_id={"tm": target // ns, "space": target % ns}, device_id_type=MESH,
        ).start()
        return carry

    lax.fori_loop(1, owners, tok_start, 0)
    def line_sent(_, way):
        count = 1 if relays else n - 1
        gathered(field.at[pl.ds(0, frames * count)], block_send.at[way]).wait_send()
        gathered(shares.at[pl.ds(0, count), 0, 0], line_send.at[way]).wait_send()

    if relays:
        beside_line(line_sent)

        @pl.when(middle)
        def _():
            for i in range(3):
                gathered(field.at[pl.ds(0, frames)], relay_send.at[i]).wait_send()
                gathered(shares.at[0, 0, 0], line_relay_send.at[i]).wait_send()

    else:
        line_sent(0, 0)
    gathered(slab_out.at[pl.ds(0, n - 1)], slab_sem.at[0]).wait_send()
    for side in range(2):
        sided(side, lambda: gathered(edge_out.at[side], edge_sem.at[0, side]).wait_send())
    if shared:
        gathered(shares.at[pl.ds(0, n - 1), pl.ds(0, columns - 1), 0], bulk_sem.at[0]).wait_send()
        gathered(shares.at[pl.ds(0, n - 1), :, 0], bulk_sem.at[1]).wait_send()
    halo_copies(lambda copy: copy.wait_send())
    everyone = gathered(tok_in.at[pl.ds(0, owners - 1)], tok_sem.at[0], tok_sem.at[1])
    everyone.wait_recv()
    row = lax.broadcasted_iota(jnp.int32, (owners * most, owners * SUBLANES), 0)
    held = lax.broadcasted_iota(jnp.int32, (owners * most, owners * SUBLANES), 1)
    inner = held % SUBLANES
    chosen = (row == held // SUBLANES * most + inner) & (inner < most)
    tokens_out[...] = jnp.dot(
        jnp.where(chosen, 1.0, 0.0).astype(jnp.bfloat16),
        tok_in[...].reshape(owners * SUBLANES, LANES),
        preferred_element_type=jnp.float32,
    ).astype(jnp.bfloat16)
    everyone.wait_send()


def embedder(channels, tokens, weight, bias, packed):
    held = tokens[...]
    projected = jnp.dot(held[:, :channels], weight[...], preferred_element_type=jnp.float32)
    flags = held[:, channels : channels + 1].astype(jnp.float32)
    packed[...] = ((projected + bias[...]) * flags).astype(jnp.bfloat16)


def shards(
    features,
    frame_counts,
    routes,
    norm_gains,
    conv_weights,
    conv_biases,
    latent_weight,
    embed_weight,
    embed_bias,
):
    feat = features[0]
    frames, rows, cols, width = feat.shape
    cells = frames * rows * cols
    n, ns = lax.axis_size("tm"), lax.axis_size("space")
    ng, nc = lax.axis_size("groups"), lax.axis_size("clip")
    owners = n * ns
    out = conv_weights.shape[1]
    pack = max(1, LANES // out)
    latents = latent_weight.shape[1]
    tok_count = routes.shape[1]
    most = (tok_count + owners - 1) // owners + 1
    vmem = pl.BlockSpec(memory_space=pltpu.VMEM)
    hbm = pl.BlockSpec(memory_space=pltpu.HBM)
    away = lambda value: pltpu.with_memory_space_constraint(value, pltpu.HBM)
    dma = pltpu.SemaphoreType.DMA
    field = pltpu.VMEM((n * frames + 2, rows, cols, width), jnp.bfloat16)
    inner = pltpu.VMEM((frames + 2, rows + 2, cols, width), jnp.bfloat16)
    slab = pltpu.VMEM((n, cells // pack, pack * out), jnp.bfloat16)
    edge = pltpu.VMEM((2, n, frames * cols // pack, pack * out), jnp.bfloat16)
    columns, parts = ng * ns, nc
    if out % (SUBLANES * columns) or width % (LANES * parts):
        columns = parts = 1
    taps = conv_weights.shape[2]
    shares = pltpu.VMEM((n, columns, parts, taps, out // columns, width // parts), jnp.bfloat16)
    cuts = CUTS if frames % CUTS == 0 else 1
    bits = BITS if taps % BITS == 0 else 1
    tok = pltpu.VMEM((owners, SUBLANES, LANES), jnp.bfloat16)
    tokens = pl.pallas_call(
        functools.partial(encoder, n, ns, ng, nc, most, latents),
        out_shape=jax.ShapeDtypeStruct((owners * most, LANES), jnp.bfloat16),
        in_specs=[hbm] * 7 + [pl.BlockSpec(memory_space=pltpu.SMEM)],
        out_specs=vmem,
        scratch_shapes=[
            pltpu.VMEM(feat.shape, feat.dtype),
            pltpu.VMEM(norm_gains.shape, norm_gains.dtype),
            pltpu.VMEM(conv_biases.shape, conv_biases.dtype),
            pltpu.VMEM((latents, width), latent_weight.dtype),
            pltpu.VMEM((1, tok_count), routes.dtype),
            field, inner,
            pltpu.VMEM((9, 3 * out, width), jnp.bfloat16),
            pltpu.VMEM(shares.shape[3:], jnp.bfloat16), shares,
            pltpu.VMEM((owners * SUBLANES, tok_count), jnp.bfloat16),
            slab, slab, edge, edge, tok, tok,
            dma((5,)), dma, dma((2,)), dma((2,)), dma((3,)), dma((n, cuts)), dma((2,)), dma((2, 2)),
            dma((5,)), dma((5,)), dma((2,)), dma((3,)), dma((n, bits)), dma((n - 1, bits)),
            dma((3,)), dma((2,)),
        ],
        compiler_params=pltpu.CompilerParams(
            collective_id=0, has_side_effects=True, vmem_limit_bytes=GRANT
        ),
    )(
        away(feat),
        away(conv_weights.transpose(0, 2, 1, 3).reshape(2, 9, 3 * out, width)),
        away(conv_weights.transpose(0, 2, 1, 3)),
        away(norm_gains),
        away(conv_biases),
        away(latent_weight.T),
        away(routes.reshape(1, tok_count)),
        frame_counts,
    )
    channels = 4 * latents
    embed = embed_weight.shape[1]
    chunk = embed // 1 if embed % (1 * LANES) == 0 else embed
    packed = pl.pallas_call(
        functools.partial(embedder, channels),
        grid=(embed // chunk,),
        out_shape=jax.ShapeDtypeStruct((owners * most, embed), jnp.bfloat16),
        in_specs=[
            pl.BlockSpec((owners * most, LANES), lambda i: (0, 0)),
            pl.BlockSpec((channels, chunk), lambda i: (0, i)),
            pl.BlockSpec((1, chunk), lambda i: (0, i)),
        ],
        out_specs=pl.BlockSpec((owners * most, chunk), lambda i: (0, i)),
        compiler_params=pltpu.CompilerParams(vmem_limit_bytes=GRANT),
    )(tokens, embed_weight, embed_bias.reshape(1, embed))
    return packed[None]


def solution(mesh):
    return jax.shard_map(
        shards,
        mesh=mesh,
        in_specs=(
            P(("groups", "clip"), "tm", "space", None, None),
            P(("groups", "clip")),
            P(("groups", "clip"), ("tm", "space"), None),
            P(),
            P(None, "tm", None, None),
            P(),
            P(),
            P(),
            P(),
        ),
        out_specs=P(("groups", "clip"), ("tm", "space"), None),
        check_vma=False,
    )
```

```python
import functools

import jax
import jax.numpy as jnp
from jax import lax
from jax.experimental import pallas as pl
from jax.experimental.pallas import tpu as pltpu
from jax.sharding import PartitionSpec as P

MESH = pl.DeviceIdType.MESH
LANES = 128
SUBLANES = 16
CUTS = 4
BITS = 3
GRANT = 28 << 20


def norm_silu(values, gain):
    scale = lax.rsqrt(jnp.mean(values * values, axis=-1, keepdims=True) + 1e-06)
    scaled = values * scale * gain
    return scaled / (1.0 + jnp.exp(-scaled))


def encoder(
    n, ns, ng, nc, most, width_latent,
    feat_any, weights_any, shares_any, gains_any, biases_any, latent_any, owner_any, count,
    tokens_out,
    feat, gains, biases, latent_rows, owner_of, field, inner, taps, mine, shares, placing, slab_out, slab_in, edge_out, edge_in, tok_out, tok_in,
    load_sem, raw_sem, share_sem, block_send, relay_send, block_recv, slab_sem, edge_sem,
    halo_send, halo_recv, line_send, line_relay_send, line_recv, plane_recv, bulk_sem, tok_sem,
):
    t = lax.axis_index("tm")
    s = lax.axis_index("space")
    g = lax.axis_index("groups")
    core = lax.axis_index("clip")
    me = t * ns + s
    owners = n * ns
    frames, rows, cols, width = feat.shape
    cells = frames * rows * cols
    out = weights_any.shape[2] // 3
    cuts = block_recv.shape[1]
    size = frames // cuts
    pack = max(1, LANES // out)
    relays = n == 4
    columns, parts, share_taps, share_rows, share_lanes = shares.shape[1:]
    bits = line_recv.shape[1]
    bit = share_taps // bits
    shared = columns > 1
    column_of = g * ns + s if shared else 0
    part_of = core if shared else 0

    barrier = pltpu.get_barrier_semaphore()

    def greet(d, carry):
        o = (me + d) % owners
        pl.semaphore_signal(
            barrier, inc=1, device_id={"tm": o // ns, "space": o % ns}, device_id_type=MESH
        )
        return carry

    lax.fori_loop(1, owners, greet, 0)
    expected = owners - 1
    if shared:
        for dg in range(1, ng):
            for other in range(ns):
                pl.semaphore_signal(
                    barrier, inc=1, device_id={"groups": (g + dg) % ng, "space": other},
                    device_id_type=MESH,
                )
                expected += 1
        for dc in range(1, nc):
            pl.semaphore_signal(
                barrier, inc=1, device_id={"clip": (core + dc) % nc}, device_id_type=MESH
            )
            expected += 1
    weight_copy = pltpu.make_async_copy(weights_any.at[0], taps, raw_sem)

    def share_load(col, part, target, sem):
        lanes = pl.ds(pl.multiple_of(part * share_lanes, LANES), share_lanes)
        return pltpu.make_async_copy(
            shares_any.at[1, :, pl.ds(col * share_rows, share_rows), lanes], target, sem
        )

    mine_load = share_load(column_of, part_of, mine, share_sem.at[0])
    loads = [
        pltpu.make_async_copy(source, target, load_sem.at[i])
        for i, (source, target) in enumerate((
            (feat_any, feat), (gains_any, gains), (owner_any, owner_of),
            (biases_any, biases), (latent_any, latent_rows),
        ))
    ]
    for copy in loads[:2]:
        copy.start()
    mine_load.start()
    for copy in loads[2:]:
        copy.start()
    weight_copy.start()

    for col in range(columns):
        for part in range(parts):
            share_load(col, part, shares.at[t, col, part], share_sem.at[1]).start()

    field[0:2] = jnp.zeros((2,) + field.shape[1:], field.dtype)

    @pl.when(t == 0)
    def _():
        inner[0:2] = jnp.zeros((2,) + inner.shape[1:], inner.dtype)

    @pl.when(s == 0)
    def _():
        edge_in[0] = jnp.zeros(edge_in.shape[1:], edge_in.dtype)
        inner[:, 0:1] = jnp.zeros((inner.shape[0], 1) + inner.shape[2:], inner.dtype)

    @pl.when(s == ns - 1)
    def _():
        edge_in[1] = jnp.zeros(edge_in.shape[1:], edge_in.dtype)
        inner[:, rows + 1 :] = jnp.zeros((inner.shape[0], 1) + inner.shape[2:], inner.dtype)

    for copy in loads[:2]:
        copy.wait()
    inputs = feat[...].reshape(cells, width).astype(jnp.float32)

    def block_copy(c, f, target, send_sem):
        span = field.at[pl.ds(2 + frames * c + size * f, size)]
        return pltpu.make_async_remote_copy(
            src_ref=span, dst_ref=span, send_sem=send_sem, recv_sem=block_recv.at[c, f],
            device_id={"tm": target}, device_id_type=MESH,
        )

    def slab_copy(source, target):
        return pltpu.make_async_remote_copy(
            src_ref=slab_out.at[target], dst_ref=slab_in.at[source],
            send_sem=slab_sem.at[0], recv_sem=slab_sem.at[1],
            device_id={"tm": target}, device_id_type=MESH,
        )

    def edge_copy(side, source, target):
        return pltpu.make_async_remote_copy(
            src_ref=edge_out.at[side, target], dst_ref=edge_in.at[side, source],
            send_sem=edge_sem.at[0, side], recv_sem=edge_sem.at[1, side],
            device_id={"tm": target, "space": (s + 1 - 2 * side + ns) % ns}, device_id_type=MESH,
        )

    def gathered(ref, send_sem, recv_sem=None):
        return pltpu.make_async_remote_copy(
            src_ref=ref, dst_ref=ref, send_sem=send_sem,
            recv_sem=send_sem if recv_sem is None else recv_sem,
            device_id={"tm": t}, device_id_type=MESH,
        )

    def sided(side, act):
        pl.when(s < ns - 1 if side == 0 else s > 0)(act)

    def fed(side, act):
        pl.when(s > 0 if side == 0 else s < ns - 1)(act)

    def line_copy(q, k, target, send_sem, own=False):
        piece = shares.at[q, column_of, part_of, pl.ds(bit * k, bit)]
        return pltpu.make_async_remote_copy(
            src_ref=mine.at[pl.ds(bit * k, bit)] if own else piece, dst_ref=piece,
            send_sem=send_sem, recv_sem=line_recv.at[q, k],
            device_id={"tm": target}, device_id_type=MESH,
        )

    def plane_copy(q, k, d):
        piece = shares.at[q, column_of, part_of, pl.ds(bit * k, bit)]
        peer = (column_of + d) % columns
        return pltpu.make_async_remote_copy(
            src_ref=piece, dst_ref=piece, send_sem=bulk_sem.at[0],
            recv_sem=plane_recv.at[(q - t + n) % n - 1, k],
            device_id={"groups": peer // ns, "space": peer % ns}, device_id_type=MESH,
        )

    def core_copy(q, col, k, d):
        piece = shares.at[q, col, part_of, pl.ds(bit * k, bit)]
        return pltpu.make_async_remote_copy(
            src_ref=piece, dst_ref=piece, send_sem=bulk_sem.at[1], recv_sem=bulk_sem.at[2],
            device_id={"clip": (core + d) % nc}, device_id_type=MESH,
        )

    def beside_line(act):
        for way in range(2):
            target = t - 1 + 2 * way
            pl.when((target >= 0) & (target < n))(
                functools.partial(act, (target + n) % n, way)
            )

    def around(act):
        def each(d, carry):
            act((t + d) % n, 0)
            return carry

        lax.fori_loop(1, n, each, 0)

    reach = beside_line if relays else around
    def send_blocks(spot, way):
        for f in range(cuts):
            block_copy(t, f, spot, block_send.at[way]).start()

    def send_lines(spot, way):
        for k in range(bits):
            line_copy(t, k, spot, line_send.at[way], own=True).start()

    middle = (t == 1) | (t == 2)
    low = t == 1
    end, mate, far = [jnp.where(low, one, two) for one, two in ((0, 3), (2, 1), (3, 0))]
    courses = ((end, mate), (mate, end), (far, end))

    def relay_copy(i, f):
        q, target = courses[i]
        return block_copy(q, f, target, relay_send.at[i])

    def line_relay(i, k):
        q, target = courses[i]
        return line_copy(q, k, target, line_relay_send.at[i])

    def relay_block(*which):
        for f in range(cuts):
            for i in which:
                q = courses[i][0]
                block_copy(q, f, q, block_send.at[0]).wait_recv()
                relay_copy(i, f).start()

    def pass_bit(q, k):
        if shared:
            for d in range(1, columns):
                plane_copy(q, k, d).start()
            for d in range(1, nc):
                core_copy(q, column_of, k, d).start()

    def line_came(q, k):
        line_copy(q, k, q, line_send.at[0]).wait_recv()

    def pass_on(q):
        for k in range(bits):
            line_came(q, k)
            pass_bit(q, k)

    def cross(q):
        for k in range(bits):
            gathered(
                shares.at[0, pl.ds(0, columns - 1), 0, pl.ds(0, bit)],
                bulk_sem.at[0], plane_recv.at[(q - t + n) % n - 1, k],
            ).wait_recv()
            for d in range(1, columns):
                for dc in range(1, nc):
                    core_copy(q, (column_of + d) % columns, k, dc).start()

    def arrived(c):
        for f in range(cuts):
            block_copy(c, f, c, block_send.at[0]).wait_recv()

    grid_rows = rows + 2
    column = lax.broadcasted_iota(jnp.int32, (frames * grid_rows * cols, 1), 0) % cols

    def fold(values):
        part = values.shape[0] // pack
        return jnp.concatenate([values[j * part : (j + 1) * part] for j in range(pack)], axis=1)

    def unfold(pieces):
        return jnp.concatenate(
            [
                jnp.concatenate([piece[:, j * out : (j + 1) * out] for piece in pieces], axis=1)
                for j in range(pack)
            ],
            axis=0,
        )

    def beside(left, middle, right):
        count = left.shape[0]
        mark = column[:count]
        left = jnp.where(mark == 0, 0.0, pltpu.roll(left, 1, 0))
        right = jnp.where(mark == cols - 1, 0.0, pltpu.roll(right, count - 1, 0))
        return left + middle + right

    def one(b):
        span = jnp.concatenate(
            [field[pl.ds(frames * b + a, frames)].reshape(cells, width) for a in range(3)], axis=1
        )
        sums = [
            lax.dot_general(
                span, jnp.concatenate([taps[3 * a + r] for a in range(3)], axis=1),
                (((1,), (1,)), ((), ())), preferred_element_type=jnp.float32,
            ).reshape(frames, rows, cols, 3 * out)
            for r in range(3)
        ]
        wide = jnp.concatenate(
            [
                functools.reduce(
                    jnp.add,
                    [sums[r][:, row : row + 1] for r in range(3) for row in [j - 2 + r] if 0 <= row < rows],
                )
                for j in range(grid_rows)
            ],
            axis=1,
        ).reshape(frames * grid_rows * cols, 3 * out)
        summed = beside(wide[:, :out], wide[:, out : 2 * out], wide[:, 2 * out :])
        summed = summed.reshape(frames, grid_rows, cols, out)
        edges = (
            summed[:, rows + 1 :].reshape(frames * cols, out),
            summed[:, :1].reshape(frames * cols, out),
        )
        packed = fold(summed[:, 1 : rows + 1].reshape(cells, out)).astype(jnp.bfloat16)

        @pl.when(b == t)
        def _():
            slab_in[pl.ds(t, 1)] = packed[None]

        @pl.when(b != t)
        def _():
            slab_out[pl.ds(b, 1)] = packed[None]
            slab_copy(t, b).start()

        for side in range(2):

            def give(side=side):
                edge_out[side, pl.ds(b, 1)] = fold(edges[side]).astype(jnp.bfloat16)[None]
                edge_copy(side, t, b).start()

            sided(side, give)

    def halo_copies(act):
        near, far = pl.ds(frames, 2), pl.ds(0, 2)
        own, body = pl.ds(2, frames), pl.ds(1, rows)
        up = {"tm": (t + 1) % n}
        more = t < n - 1

        def copy(i, here, source, target, device):
            pl.when(here)(
                lambda: act(
                    pltpu.make_async_remote_copy(
                        src_ref=inner.at[source], dst_ref=inner.at[target],
                        send_sem=halo_send.at[i], recv_sem=halo_recv.at[i],
                        device_id=device, device_id_type=MESH,
                    )
                )
            )

        left, right = {"space": (s + ns - 1) % ns}, {"space": (s + 1) % ns}
        first, last = pl.ds(1, 1), pl.ds(rows, 1)
        above, below = pl.ds(0, 1), pl.ds(rows + 1, 1)
        copy(0, more, (near, body), (far, body), up)
        copy(1, more & (s > 0), (near, first), (far, below), up | left)
        copy(2, more & (s < ns - 1), (near, last), (far, above), up | right)
        copy(3, s > 0, (own, first), (own, below), left)
        copy(4, s < ns - 1, (own, last), (own, above), right)

    def halo_came():
        def wait(i, here, target):
            def act():
                span = inner.at[target]
                pltpu.make_async_remote_copy(
                    src_ref=span, dst_ref=span, send_sem=halo_send.at[i],
                    recv_sem=halo_recv.at[i], device_id={"tm": t}, device_id_type=MESH,
                ).wait_recv()

            pl.when(here)(act)

        far, own, body = pl.ds(0, 2), pl.ds(2, frames), pl.ds(1, rows)
        above, below = pl.ds(0, 1), pl.ds(rows + 1, 1)
        wait(3, s < ns - 1, (own, below))
        wait(4, s > 0, (own, above))
        wait(0, t > 0, (far, body))
        wait(1, (t > 0) & (s < ns - 1), (far, below))
        wait(2, (t > 0) & (s > 0), (far, above))

    def kernel_of(tap):
        return jnp.concatenate(
            [
                jnp.concatenate([shares[q, col, part, tap] for part in range(parts)], axis=1)
                for q in range(n)
                for col in range(columns)
            ],
            axis=0,
        )

    field[pl.ds(2 + frames * t, frames)] = norm_silu(inputs, gains[0:1]).astype(
        jnp.bfloat16
    ).reshape(frames, rows, cols, width)
    for copy in loads[2:]:
        copy.wait()
    toks = owner_of.shape[1]
    before = lax.broadcasted_iota(jnp.int32, (toks, toks), 0)
    after = lax.broadcasted_iota(jnp.int32, (toks, toks), 1)
    owner = owner_of[...]
    owner_column = jnp.sum(jnp.where(before == after, owner, 0), axis=1, keepdims=True)
    same = (owner_column == owner) & (before < after)
    rank = jnp.sum(jnp.where(same, 1, 0), axis=0, keepdims=True)
    slots = lax.broadcasted_iota(jnp.int32, (owners * SUBLANES, toks), 0)
    placing[...] = jnp.where(slots == owner * SUBLANES + rank, 1.0, 0.0).astype(jnp.bfloat16)
    mine_load.wait()
    pl.semaphore_wait(barrier, expected)
    start = lambda copy: copy.start()
    reach(send_blocks)
    reach(send_lines)
    weight_copy.wait()
    if relays:
        order = ((0, 1, 2, 3), (3, 2, 0, 1), (0, 3, 1, 2), (3, 2, 0, 1))
        flow = ((1, 2, 3), (0, 2, 3), (3, 1, 0), (2, 1, 0))

        def forward():
            relay_block(0, 1)
            pass_on(end)
            pass_on(mate)
            for k in range(bits):
                line_relay(0, k).start()
                line_relay(1, k).start()
            relay_block(2)

        def last(q):
            for k in range(bits):
                line_came(q, k)
                line_relay(2, k).start()
                pass_bit(q, k)

        before = (
            ((), ((arrived, 1),), ((pass_on, 1), (arrived, 2)), ((pass_on, 2), (arrived, 3))),
            ((), (), ((last, 3),), ()),
            ((), (), ((last, 0),), ()),
            (((arrived, 2),), ((pass_on, 2), (arrived, 1)), ((pass_on, 1), (arrived, 0)), ()),
        )

        def pick(table, k):
            spot = table[0][k]
            for i in range(1, n):
                spot = jnp.where(t == i, table[i][k], spot)
            return spot

        def chosen(table, k):
            spot = pick(table, 0)
            for kk in range(1, len(table[0])):
                spot = jnp.where(k == kk, pick(table, kk), spot)
            return spot

        pl.when(middle)(forward)

        def step(k, carry):
            for i in range(n):
                for kk in range(n):
                    if before[i][kk]:

                        @pl.when((t == i) & (k == kk))
                        def _():
                            for act, c in before[i][kk]:
                                act(c)

            one(chosen(order, k))
            return carry

        lax.fori_loop(0, n, step, 0)
        pl.when(jnp.logical_not(middle))(lambda: pass_on(pick(flow, 2)))
    else:

        def hold(d, carry):
            arrived((t + d) % n)
            return carry

        lax.fori_loop(1, n, hold, 0)

        def step(d, carry):
            one((t + d) % n)
            return carry

        lax.fori_loop(1, n + 1, step, 0)

    gathered(slab_in.at[pl.ds(0, n - 1)], slab_sem.at[0], slab_sem.at[1]).wait_recv()
    for side in range(2):
        fed(side, lambda: gathered(edge_in.at[side], edge_sem.at[0, side], edge_sem.at[1, side]).wait_recv())
    hidden = unfold([slab_in[q].astype(jnp.float32) for q in range(n)])
    top, bottom = [
        unfold([edge_in[side, q].astype(jnp.float32) for q in range(n)]).reshape(
            frames, 1, cols, width
        )
        for side in range(2)
    ]
    hidden = hidden.reshape(frames, rows, cols, width)
    if rows > 1:
        hidden = jnp.concatenate(
            [hidden[:, :1] + top, hidden[:, 1 : rows - 1], hidden[:, rows - 1 :] + bottom], axis=1
        )
    else:
        hidden = hidden + top + bottom
    hidden = hidden.reshape(cells, width) + biases[0:1]
    inner[2:, 1 : rows + 1] = norm_silu(hidden, gains[1:2]).astype(jnp.bfloat16).reshape(
        frames, rows, cols, width
    )
    halo_copies(start)
    if not relays:

        def passed(d, carry):
            pass_on((t + d) % n)
            return carry

        lax.fori_loop(1, n, passed, 0)
    if shared:

        def crossed(k, carry):
            if relays:
                q = chosen(flow, k)
            else:
                q = (t + 1 + k) % n
            cross(q)
            return carry

        lax.fori_loop(0, n - 1, crossed, 0)
    pltpu.make_async_copy(shares.at[t], shares.at[t], share_sem.at[1]).wait()
    halo_came()
    if shared:

        gathered(shares.at[pl.ds(0, n - 1), :, 0], bulk_sem.at[1], bulk_sem.at[2]).wait_recv()
    sums = []
    for e in range(3):
        total = None
        for a in range(3):
            for r in range(3):
                block = inner[a : a + frames, r : r + rows].reshape(cells, width)
                term = lax.dot_general(
                    block, kernel_of(9 * a + 3 * r + e),
                    (((1,), (1,)), ((), ())), preferred_element_type=jnp.float32,
                )
                total = term if total is None else total + term
        sums.append(total)
    hidden = beside(*sums) + biases[1:2]
    merged = feat[...].reshape(cells, width).astype(jnp.float32) + hidden
    active = norm_silu(merged, gains[2:3]).astype(jnp.bfloat16)
    rest = jnp.zeros((LANES - 4 * width_latent, width), jnp.bfloat16)
    latent_wide = jnp.concatenate([latent_rows[...]] * 4 + [rest], axis=0)
    latent = lax.dot_general(
        active, latent_wide, (((1,), (1,)), ((), ())), preferred_element_type=jnp.float32
    )
    cell = lax.broadcasted_iota(jnp.int32, (cells, LANES), 0)
    lane = lax.broadcasted_iota(jnp.int32, (cells, LANES), 1)
    corner = (cell // cols % 2) * 2 + cell % 2
    alive = (t * frames + cell // (rows * cols) < count[0]) & (corner == 0)
    flagged = jnp.where((lane == 4 * width_latent) & alive, 1.0, 0.0)
    patches = jnp.where(lane // width_latent == corner, latent, flagged).astype(jnp.bfloat16)
    spot = lax.broadcasted_iota(jnp.int32, (toks, cells), 1)
    patch = (spot // (2 * cols)) * (cols // 2) + spot % cols // 2
    mine = patch == lax.broadcasted_iota(jnp.int32, (toks, cells), 0)
    patches = jnp.dot(
        jnp.where(mine, 1.0, 0.0).astype(jnp.bfloat16), patches, preferred_element_type=jnp.float32
    ).astype(jnp.bfloat16)
    outgoing = jnp.dot(
        placing[...], patches, preferred_element_type=jnp.float32
    ).astype(jnp.bfloat16)
    tok_out[...] = outgoing.reshape(owners, SUBLANES, LANES)
    tok_in[pl.ds(me, 1)] = tok_out[pl.ds(me, 1)]

    def tok_start(d, carry):
        target = (me + d) % owners
        pltpu.make_async_remote_copy(
            src_ref=tok_out.at[target], dst_ref=tok_in.at[me],
            send_sem=tok_sem.at[0], recv_sem=tok_sem.at[1],
            device_id={"tm": target // ns, "space": target % ns}, device_id_type=MESH,
        ).start()
        return carry

    lax.fori_loop(1, owners, tok_start, 0)
    def line_sent(_, way):
        count = 1 if relays else n - 1
        gathered(field.at[pl.ds(0, frames * count)], block_send.at[way]).wait_send()
        gathered(shares.at[pl.ds(0, count), 0, 0], line_send.at[way]).wait_send()

    if relays:
        beside_line(line_sent)

        @pl.when(middle)
        def _():
            for i in range(3):
                gathered(field.at[pl.ds(0, frames)], relay_send.at[i]).wait_send()
                gathered(shares.at[0, 0, 0], line_relay_send.at[i]).wait_send()

    else:
        line_sent(0, 0)
    gathered(slab_out.at[pl.ds(0, n - 1)], slab_sem.at[0]).wait_send()
    for side in range(2):
        sided(side, lambda: gathered(edge_out.at[side], edge_sem.at[0, side]).wait_send())
    if shared:
        gathered(shares.at[pl.ds(0, n - 1), pl.ds(0, columns - 1), 0], bulk_sem.at[0]).wait_send()
        gathered(shares.at[pl.ds(0, n - 1), :, 0], bulk_sem.at[1]).wait_send()
    halo_copies(lambda copy: copy.wait_send())
    everyone = gathered(tok_in.at[pl.ds(0, owners - 1)], tok_sem.at[0], tok_sem.at[1])
    everyone.wait_recv()
    row = lax.broadcasted_iota(jnp.int32, (owners * most, owners * SUBLANES), 0)
    held = lax.broadcasted_iota(jnp.int32, (owners * most, owners * SUBLANES), 1)
    inner = held % SUBLANES
    chosen = (row == held // SUBLANES * most + inner) & (inner < most)
    tokens_out[...] = jnp.dot(
        jnp.where(chosen, 1.0, 0.0).astype(jnp.bfloat16),
        tok_in[...].reshape(owners * SUBLANES, LANES),
        preferred_element_type=jnp.float32,
    ).astype(jnp.bfloat16)
    everyone.wait_send()


def embedder(channels, tokens, weight, bias, packed):
    held = tokens[...]
    projected = jnp.dot(held[:, :channels], weight[...], preferred_element_type=jnp.float32)
    flags = held[:, channels : channels + 1].astype(jnp.float32)
    packed[...] = ((projected + bias[...]) * flags).astype(jnp.bfloat16)


def shards(
    features,
    frame_counts,
    routes,
    norm_gains,
    conv_weights,
    conv_biases,
    latent_weight,
    embed_weight,
    embed_bias,
):
    feat = features[0]
    frames, rows, cols, width = feat.shape
    cells = frames * rows * cols
    n, ns = lax.axis_size("tm"), lax.axis_size("space")
    ng, nc = lax.axis_size("groups"), lax.axis_size("clip")
    owners = n * ns
    out = conv_weights.shape[1]
    pack = max(1, LANES // out)
    latents = latent_weight.shape[1]
    tok_count = routes.shape[1]
    most = (tok_count + owners - 1) // owners + 1
    vmem = pl.BlockSpec(memory_space=pltpu.VMEM)
    hbm = pl.BlockSpec(memory_space=pltpu.HBM)
    away = lambda value: pltpu.with_memory_space_constraint(value, pltpu.HBM)
    dma = pltpu.SemaphoreType.DMA
    field = pltpu.VMEM((n * frames + 2, rows, cols, width), jnp.bfloat16)
    inner = pltpu.VMEM((frames + 2, rows + 2, cols, width), jnp.bfloat16)
    slab = pltpu.VMEM((n, cells // pack, pack * out), jnp.bfloat16)
    edge = pltpu.VMEM((2, n, frames * cols // pack, pack * out), jnp.bfloat16)
    columns, parts = ng * ns, nc
    if out % (SUBLANES * columns) or width % (LANES * parts):
        columns = parts = 1
    taps = conv_weights.shape[2]
    shares = pltpu.VMEM((n, columns, parts, taps, out // columns, width // parts), jnp.bfloat16)
    cuts = CUTS if frames % CUTS == 0 else 1
    bits = BITS if taps % BITS == 0 else 1
    tok = pltpu.VMEM((owners, SUBLANES, LANES), jnp.bfloat16)
    tokens = pl.pallas_call(
        functools.partial(encoder, n, ns, ng, nc, most, latents),
        out_shape=jax.ShapeDtypeStruct((owners * most, LANES), jnp.bfloat16),
        in_specs=[hbm] * 7 + [pl.BlockSpec(memory_space=pltpu.SMEM)],
        out_specs=vmem,
        scratch_shapes=[
            pltpu.VMEM(feat.shape, feat.dtype),
            pltpu.VMEM(norm_gains.shape, norm_gains.dtype),
            pltpu.VMEM(conv_biases.shape, conv_biases.dtype),
            pltpu.VMEM((latents, width), latent_weight.dtype),
            pltpu.VMEM((1, tok_count), routes.dtype),
            field, inner,
            pltpu.VMEM((9, 3 * out, width), jnp.bfloat16),
            pltpu.VMEM(shares.shape[3:], jnp.bfloat16), shares,
            pltpu.VMEM((owners * SUBLANES, tok_count), jnp.bfloat16),
            slab, slab, edge, edge, tok, tok,
            dma((5,)), dma, dma((2,)), dma((2,)), dma((3,)), dma((n, cuts)), dma((2,)), dma((2, 2)),
            dma((5,)), dma((5,)), dma((2,)), dma((3,)), dma((n, bits)), dma((n - 1, bits)),
            dma((3,)), dma((2,)),
        ],
        compiler_params=pltpu.CompilerParams(
            collective_id=0, has_side_effects=True, vmem_limit_bytes=GRANT
        ),
    )(
        away(feat),
        away(conv_weights.transpose(0, 2, 1, 3).reshape(2, 9, 3 * out, width)),
        away(conv_weights.transpose(0, 2, 1, 3)),
        away(norm_gains),
        away(conv_biases),
        away(latent_weight.T),
        away(routes.reshape(1, tok_count)),
        frame_counts,
    )
    channels = 4 * latents
    embed = embed_weight.shape[1]
    chunk = embed // 1 if embed % (1 * LANES) == 0 else embed
    packed = pl.pallas_call(
        functools.partial(embedder, channels),
        grid=(embed // chunk,),
        out_shape=jax.ShapeDtypeStruct((owners * most, embed), jnp.bfloat16),
        in_specs=[
            pl.BlockSpec((owners * most, LANES), lambda i: (0, 0)),
            pl.BlockSpec((channels, chunk), lambda i: (0, i)),
            pl.BlockSpec((1, chunk), lambda i: (0, i)),
        ],
        out_specs=pl.BlockSpec((owners * most, chunk), lambda i: (0, i)),
        compiler_params=pltpu.CompilerParams(vmem_limit_bytes=GRANT),
    )(tokens, embed_weight, embed_bias.reshape(1, embed))
    return packed[None]


def solution(mesh):
    return jax.shard_map(
        shards,
        mesh=mesh,
        in_specs=(
            P(("groups", "clip"), "tm", "space", None, None),
            P(("groups", "clip")),
            P(("groups", "clip"), ("tm", "space"), None),
            P(),
            P(None, "tm", None, None),
            P(),
            P(),
            P(),
            P(),
        ),
        out_specs=P(("groups", "clip"), ("tm", "space"), None),
        check_vma=False,
    )
```

```python
import functools

import jax
import jax.numpy as jnp
from jax import lax
from jax.experimental import pallas as pl
from jax.experimental.pallas import tpu as pltpu
from jax.sharding import PartitionSpec as P

MESH = pl.DeviceIdType.MESH
LANES = 128
SUBLANES = 16
CUTS = 4
BITS = 3
GRANT = 28 << 20


def norm_silu(values, gain):
    scale = lax.rsqrt(jnp.mean(values * values, axis=-1, keepdims=True) + 1e-06)
    scaled = values * scale * gain
    return scaled / (1.0 + jnp.exp(-scaled))


def encoder(
    n, ns, ng, nc, most, width_latent,
    feat_any, weights_any, shares_any, gains_any, biases_any, latent_any, owner_any, count,
    tokens_out,
    feat, gains, biases, latent_rows, owner_of, field, inner, taps, mine, shares, placing, slab_out, slab_in, edge_out, edge_in, tok_out, tok_in,
    load_sem, raw_sem, share_sem, block_send, relay_send, block_recv, slab_sem, edge_sem,
    halo_send, halo_recv, line_send, line_relay_send, line_recv, plane_recv, bulk_sem, tok_sem,
):
    t = lax.axis_index("tm")
    s = lax.axis_index("space")
    g = lax.axis_index("groups")
    core = lax.axis_index("clip")
    me = t * ns + s
    owners = n * ns
    frames, rows, cols, width = feat.shape
    cells = frames * rows * cols
    out = weights_any.shape[2] // 3
    cuts = block_recv.shape[1]
    size = frames // cuts
    pack = max(1, LANES // out)
    relays = n == 4
    columns, parts, share_taps, share_rows, share_lanes = shares.shape[1:]
    bits = line_recv.shape[1]
    bit = share_taps // bits
    shared = columns > 1
    column_of = g * ns + s if shared else 0
    part_of = core if shared else 0

    barrier = pltpu.get_barrier_semaphore()

    def greet(d, carry):
        o = (me + d) % owners
        pl.semaphore_signal(
            barrier, inc=1, device_id={"tm": o // ns, "space": o % ns}, device_id_type=MESH
        )
        return carry

    lax.fori_loop(1, owners, greet, 0)
    expected = owners - 1
    if shared:
        for dg in range(1, ng):
            for other in range(ns):
                pl.semaphore_signal(
                    barrier, inc=1, device_id={"groups": (g + dg) % ng, "space": other},
                    device_id_type=MESH,
                )
                expected += 1
        for dc in range(1, nc):
            pl.semaphore_signal(
                barrier, inc=1, device_id={"clip": (core + dc) % nc}, device_id_type=MESH
            )
            expected += 1
    weight_copy = pltpu.make_async_copy(weights_any.at[0], taps, raw_sem)

    def share_load(col, part, target, sem):
        lanes = pl.ds(pl.multiple_of(part * share_lanes, LANES), share_lanes)
        return pltpu.make_async_copy(
            shares_any.at[1, :, pl.ds(col * share_rows, share_rows), lanes], target, sem
        )

    mine_load = share_load(column_of, part_of, mine, share_sem.at[0])
    loads = [
        pltpu.make_async_copy(source, target, load_sem.at[i])
        for i, (source, target) in enumerate((
            (feat_any, feat), (gains_any, gains), (owner_any, owner_of),
            (biases_any, biases), (latent_any, latent_rows),
        ))
    ]
    for copy in loads[:2]:
        copy.start()
    mine_load.start()
    for copy in loads[2:]:
        copy.start()
    weight_copy.start()

    for col in range(columns):
        for part in range(parts):
            share_load(col, part, shares.at[t, col, part], share_sem.at[1]).start()

    field[0:2] = jnp.zeros((2,) + field.shape[1:], field.dtype)

    @pl.when(t == 0)
    def _():
        inner[0:2] = jnp.zeros((2,) + inner.shape[1:], inner.dtype)

    @pl.when(s == 0)
    def _():
        edge_in[0] = jnp.zeros(edge_in.shape[1:], edge_in.dtype)
        inner[:, 0:1] = jnp.zeros((inner.shape[0], 1) + inner.shape[2:], inner.dtype)

    @pl.when(s == ns - 1)
    def _():
        edge_in[1] = jnp.zeros(edge_in.shape[1:], edge_in.dtype)
        inner[:, rows + 1 :] = jnp.zeros((inner.shape[0], 1) + inner.shape[2:], inner.dtype)

    for copy in loads[:2]:
        copy.wait()
    inputs = feat[...].reshape(cells, width).astype(jnp.float32)

    def block_copy(c, f, target, send_sem):
        span = field.at[pl.ds(2 + frames * c + size * f, size)]
        return pltpu.make_async_remote_copy(
            src_ref=span, dst_ref=span, send_sem=send_sem, recv_sem=block_recv.at[c, f],
            device_id={"tm": target}, device_id_type=MESH,
        )

    def slab_copy(source, target):
        return pltpu.make_async_remote_copy(
            src_ref=slab_out.at[target], dst_ref=slab_in.at[source],
            send_sem=slab_sem.at[0], recv_sem=slab_sem.at[1],
            device_id={"tm": target}, device_id_type=MESH,
        )

    def edge_copy(side, source, target):
        return pltpu.make_async_remote_copy(
            src_ref=edge_out.at[side, target], dst_ref=edge_in.at[side, source],
            send_sem=edge_sem.at[0, side], recv_sem=edge_sem.at[1, side],
            device_id={"tm": target, "space": (s + 1 - 2 * side + ns) % ns}, device_id_type=MESH,
        )

    def gathered(ref, send_sem, recv_sem=None):
        return pltpu.make_async_remote_copy(
            src_ref=ref, dst_ref=ref, send_sem=send_sem,
            recv_sem=send_sem if recv_sem is None else recv_sem,
            device_id={"tm": t}, device_id_type=MESH,
        )

    def sided(side, act):
        pl.when(s < ns - 1 if side == 0 else s > 0)(act)

    def fed(side, act):
        pl.when(s > 0 if side == 0 else s < ns - 1)(act)

    def line_copy(q, k, target, send_sem, own=False):
        piece = shares.at[q, column_of, part_of, pl.ds(bit * k, bit)]
        return pltpu.make_async_remote_copy(
            src_ref=mine.at[pl.ds(bit * k, bit)] if own else piece, dst_ref=piece,
            send_sem=send_sem, recv_sem=line_recv.at[q, k],
            device_id={"tm": target}, device_id_type=MESH,
        )

    def plane_copy(q, k, d):
        piece = shares.at[q, column_of, part_of, pl.ds(bit * k, bit)]
        return pltpu.make_async_remote_copy(
            src_ref=piece, dst_ref=piece, send_sem=bulk_sem.at[0],
            recv_sem=plane_recv.at[(q - t + n) % n - 1, k],
            device_id={"groups": (g + d // ns) % ng, "space": (s + d % ns) % ns}, device_id_type=MESH,
        )

    def core_copy(q, col, k, d):
        piece = shares.at[q, col, part_of, pl.ds(bit * k, bit)]
        return pltpu.make_async_remote_copy(
            src_ref=piece, dst_ref=piece, send_sem=bulk_sem.at[1], recv_sem=bulk_sem.at[2],
            device_id={"clip": (core + d) % nc}, device_id_type=MESH,
        )

    def beside_line(act):
        for way in range(2):
            target = t - 1 + 2 * way
            pl.when((target >= 0) & (target < n))(
                functools.partial(act, (target + n) % n, way)
            )

    def around(act):
        def each(d, carry):
            act((t + d) % n, 0)
            return carry

        lax.fori_loop(1, n, each, 0)

    reach = beside_line if relays else around
    def send_blocks(spot, way):
        for f in range(cuts):
            block_copy(t, f, spot, block_send.at[way]).start()

    def send_lines(spot, way):
        for k in range(bits):
            line_copy(t, k, spot, line_send.at[way], own=True).start()

    middle = (t == 1) | (t == 2)
    low = t == 1
    end, mate, far = [jnp.where(low, one, two) for one, two in ((0, 3), (2, 1), (3, 0))]
    courses = ((end, mate), (mate, end), (far, end))

    def relay_copy(i, f):
        q, target = courses[i]
        return block_copy(q, f, target, relay_send.at[i])

    def line_relay(i, k):
        q, target = courses[i]
        return line_copy(q, k, target, line_relay_send.at[i])

    def relay_block(*which):
        for f in range(cuts):
            for i in which:
                q = courses[i][0]
                block_copy(q, f, q, block_send.at[0]).wait_recv()
                relay_copy(i, f).start()

    def pass_bit(q, k):
        if shared:
            for d in range(1, columns):
                plane_copy(q, k, d).start()
            for d in range(1, nc):
                core_copy(q, column_of, k, d).start()

    def line_came(q, k):
        line_copy(q, k, q, line_send.at[0]).wait_recv()

    def pass_on(q):
        for k in range(bits):
            line_came(q, k)
            pass_bit(q, k)

    def cross(q):
        for k in range(bits):
            gathered(
                shares.at[0, pl.ds(0, columns - 1), 0, pl.ds(0, bit)],
                bulk_sem.at[0], plane_recv.at[(q - t + n) % n - 1, k],
            ).wait_recv()
            for d in range(1, columns):
                for dc in range(1, nc):
                    core_copy(q, (column_of + d) % columns, k, dc).start()

    def arrived(c):
        for f in range(cuts):
            block_copy(c, f, c, block_send.at[0]).wait_recv()

    grid_rows = rows + 2
    column = lax.broadcasted_iota(jnp.int32, (frames * grid_rows * cols, 1), 0) % cols

    def fold(values):
        part = values.shape[0] // pack
        return jnp.concatenate([values[j * part : (j + 1) * part] for j in range(pack)], axis=1)

    def unfold(pieces):
        return jnp.concatenate(
            [
                jnp.concatenate([piece[:, j * out : (j + 1) * out] for piece in pieces], axis=1)
                for j in range(pack)
            ],
            axis=0,
        )

    def beside(left, middle, right):
        count = left.shape[0]
        mark = column[:count]
        left = jnp.where(mark == 0, 0.0, pltpu.roll(left, 1, 0))
        right = jnp.where(mark == cols - 1, 0.0, pltpu.roll(right, count - 1, 0))
        return left + middle + right

    def one(b):
        span = jnp.concatenate(
            [field[pl.ds(frames * b + a, frames)].reshape(cells, width) for a in range(3)], axis=1
        )
        sums = [
            lax.dot_general(
                span, jnp.concatenate([taps[3 * a + r] for a in range(3)], axis=1),
                (((1,), (1,)), ((), ())), preferred_element_type=jnp.float32,
            ).reshape(frames, rows, cols, 3 * out)
            for r in range(3)
        ]
        wide = jnp.concatenate(
            [
                functools.reduce(
                    jnp.add,
                    [sums[r][:, row : row + 1] for r in range(3) for row in [j - 2 + r] if 0 <= row < rows],
                )
                for j in range(grid_rows)
            ],
            axis=1,
        ).reshape(frames * grid_rows * cols, 3 * out)
        summed = beside(wide[:, :out], wide[:, out : 2 * out], wide[:, 2 * out :])
        summed = summed.reshape(frames, grid_rows, cols, out)
        edges = (
            summed[:, rows + 1 :].reshape(frames * cols, out),
            summed[:, :1].reshape(frames * cols, out),
        )
        packed = fold(summed[:, 1 : rows + 1].reshape(cells, out)).astype(jnp.bfloat16)

        for side in range(2):

            def give(side=side):
                edge_out[side, pl.ds(b, 1)] = fold(edges[side]).astype(jnp.bfloat16)[None]
                edge_copy(side, t, b).start()

            sided(side, give)

        @pl.when(b == t)
        def _():
            slab_in[pl.ds(t, 1)] = packed[None]

        @pl.when(b != t)
        def _():
            slab_out[pl.ds(b, 1)] = packed[None]
            slab_copy(t, b).start()

    def halo_copies(act):
        near, far = pl.ds(frames, 2), pl.ds(0, 2)
        own, body = pl.ds(2, frames), pl.ds(1, rows)
        up = {"tm": (t + 1) % n}
        more = t < n - 1

        def copy(i, here, source, target, device):
            pl.when(here)(
                lambda: act(
                    pltpu.make_async_remote_copy(
                        src_ref=inner.at[source], dst_ref=inner.at[target],
                        send_sem=halo_send.at[i], recv_sem=halo_recv.at[i],
                        device_id=device, device_id_type=MESH,
                    )
                )
            )

        left, right = {"space": (s + ns - 1) % ns}, {"space": (s + 1) % ns}
        first, last = pl.ds(1, 1), pl.ds(rows, 1)
        above, below = pl.ds(0, 1), pl.ds(rows + 1, 1)
        copy(1, more & (s > 0), (near, first), (far, below), up | left)
        copy(2, more & (s < ns - 1), (near, last), (far, above), up | right)
        copy(0, more, (near, body), (far, body), up)
        copy(3, s > 0, (own, first), (own, below), left)
        copy(4, s < ns - 1, (own, last), (own, above), right)

    def halo_came():
        def wait(i, here, target):
            def act():
                span = inner.at[target]
                pltpu.make_async_remote_copy(
                    src_ref=span, dst_ref=span, send_sem=halo_send.at[i],
                    recv_sem=halo_recv.at[i], device_id={"tm": t}, device_id_type=MESH,
                ).wait_recv()

            pl.when(here)(act)

        far, own, body = pl.ds(0, 2), pl.ds(2, frames), pl.ds(1, rows)
        above, below = pl.ds(0, 1), pl.ds(rows + 1, 1)
        wait(3, s < ns - 1, (own, below))
        wait(4, s > 0, (own, above))
        wait(0, t > 0, (far, body))
        wait(1, (t > 0) & (s < ns - 1), (far, below))
        wait(2, (t > 0) & (s > 0), (far, above))

    def kernel_of(tap):
        return jnp.concatenate(
            [
                jnp.concatenate([shares[q, col, part, tap] for part in range(parts)], axis=1)
                for q in range(n)
                for col in range(columns)
            ],
            axis=0,
        )

    field[pl.ds(2 + frames * t, frames)] = norm_silu(inputs, gains[0:1]).astype(
        jnp.bfloat16
    ).reshape(frames, rows, cols, width)
    for copy in loads[2:]:
        copy.wait()
    toks = owner_of.shape[1]
    before = lax.broadcasted_iota(jnp.int32, (toks, toks), 0)
    after = lax.broadcasted_iota(jnp.int32, (toks, toks), 1)
    owner = owner_of[...]
    owner_column = jnp.sum(jnp.where(before == after, owner, 0), axis=1, keepdims=True)
    same = (owner_column == owner) & (before < after)
    rank = jnp.sum(jnp.where(same, 1, 0), axis=0, keepdims=True)
    slots = lax.broadcasted_iota(jnp.int32, (owners * SUBLANES, toks), 0)
    slotted = jnp.where(slots == owner * SUBLANES + rank, 1.0, 0.0).astype(jnp.bfloat16)
    spot = lax.broadcasted_iota(jnp.int32, (toks, cells), 1)
    patch = (spot // (2 * cols)) * (cols // 2) + spot % cols // 2
    held = patch == lax.broadcasted_iota(jnp.int32, (toks, cells), 0)
    placing[...] = jnp.dot(
        slotted, jnp.where(held, 1.0, 0.0).astype(jnp.bfloat16), preferred_element_type=jnp.float32
    ).astype(jnp.bfloat16)
    mine_load.wait()
    pl.semaphore_wait(barrier, expected)
    start = lambda copy: copy.start()
    reach(send_blocks)
    reach(send_lines)
    weight_copy.wait()
    if relays:
        order = ((0, 1, 2, 3), (3, 2, 0, 1), (0, 3, 1, 2), (3, 2, 0, 1))
        flow = ((1, 2, 3), (0, 2, 3), (3, 1, 0), (2, 1, 0))

        def forward():
            relay_block(0, 1)
            pass_on(end)
            pass_on(mate)
            for k in range(bits):
                line_relay(0, k).start()
                line_relay(1, k).start()
            relay_block(2)

        def last(q):
            for k in range(bits):
                line_came(q, k)
                line_relay(2, k).start()
                pass_bit(q, k)

        before = (
            ((), ((arrived, 1),), ((pass_on, 1), (arrived, 2)), ((pass_on, 2), (arrived, 3))),
            ((), (), ((last, 3),), ()),
            ((), (), ((last, 0),), ()),
            (((arrived, 2),), ((pass_on, 2), (arrived, 1)), ((pass_on, 1), (arrived, 0)), ()),
        )

        def pick(table, k):
            spot = table[0][k]
            for i in range(1, n):
                spot = jnp.where(t == i, table[i][k], spot)
            return spot

        def chosen(table, k):
            spot = pick(table, 0)
            for kk in range(1, len(table[0])):
                spot = jnp.where(k == kk, pick(table, kk), spot)
            return spot

        pl.when(middle)(forward)

        def step(k, carry):
            for i in range(n):
                for kk in range(n):
                    if before[i][kk]:

                        @pl.when((t == i) & (k == kk))
                        def _():
                            for act, c in before[i][kk]:
                                act(c)

            one(chosen(order, k))
            return carry

        lax.fori_loop(0, n, step, 0)
        pl.when(jnp.logical_not(middle))(lambda: pass_on(pick(flow, 2)))
    else:

        def hold(d, carry):
            arrived((t + d) % n)
            return carry

        lax.fori_loop(1, n, hold, 0)

        def step(d, carry):
            one((t + d) % n)
            return carry

        lax.fori_loop(1, n + 1, step, 0)

    gathered(slab_in.at[pl.ds(0, n - 1)], slab_sem.at[0], slab_sem.at[1]).wait_recv()
    for side in range(2):
        fed(side, lambda: gathered(edge_in.at[side], edge_sem.at[0, side], edge_sem.at[1, side]).wait_recv())
    hidden = unfold([slab_in[q].astype(jnp.float32) for q in range(n)])
    top, bottom = [
        unfold([edge_in[side, q].astype(jnp.float32) for q in range(n)]).reshape(
            frames, 1, cols, width
        )
        for side in range(2)
    ]
    hidden = hidden.reshape(frames, rows, cols, width)
    if rows > 1:
        hidden = jnp.concatenate(
            [hidden[:, :1] + top, hidden[:, 1 : rows - 1], hidden[:, rows - 1 :] + bottom], axis=1
        )
    else:
        hidden = hidden + top + bottom
    hidden = hidden.reshape(cells, width) + biases[0:1]
    inner[2:, 1 : rows + 1] = norm_silu(hidden, gains[1:2]).astype(jnp.bfloat16).reshape(
        frames, rows, cols, width
    )
    halo_copies(start)
    if not relays:

        def passed(d, carry):
            pass_on((t + d) % n)
            return carry

        lax.fori_loop(1, n, passed, 0)
    if shared:

        def crossed(k, carry):
            if relays:
                q = chosen(flow, k)
            else:
                q = (t + 1 + k) % n
            cross(q)
            return carry

        lax.fori_loop(0, n - 1, crossed, 0)
    pltpu.make_async_copy(shares.at[t], shares.at[t], share_sem.at[1]).wait()
    halo_came()
    if shared:

        gathered(shares.at[pl.ds(0, n - 1), :, 0], bulk_sem.at[1], bulk_sem.at[2]).wait_recv()
    sums = []
    for e in range(3):
        total = None
        for a in range(3):
            for r in range(3):
                block = inner[a : a + frames, r : r + rows].reshape(cells, width)
                term = lax.dot_general(
                    block, kernel_of(9 * a + 3 * r + e),
                    (((1,), (1,)), ((), ())), preferred_element_type=jnp.float32,
                )
                total = term if total is None else total + term
        sums.append(total)
    hidden = beside(*sums) + biases[1:2]
    merged = feat[...].reshape(cells, width).astype(jnp.float32) + hidden
    active = norm_silu(merged, gains[2:3]).astype(jnp.bfloat16)
    rest = jnp.zeros((LANES - 4 * width_latent, width), jnp.bfloat16)
    latent_wide = jnp.concatenate([latent_rows[...]] * 4 + [rest], axis=0)
    latent = lax.dot_general(
        active, latent_wide, (((1,), (1,)), ((), ())), preferred_element_type=jnp.float32
    )
    cell = lax.broadcasted_iota(jnp.int32, (cells, LANES), 0)
    lane = lax.broadcasted_iota(jnp.int32, (cells, LANES), 1)
    corner = (cell // cols % 2) * 2 + cell % 2
    alive = (t * frames + cell // (rows * cols) < count[0]) & (corner == 0)
    flagged = jnp.where((lane == 4 * width_latent) & alive, 1.0, 0.0)
    patches = jnp.where(lane // width_latent == corner, latent, flagged).astype(jnp.bfloat16)
    outgoing = jnp.dot(
        placing[...], patches, preferred_element_type=jnp.float32
    ).astype(jnp.bfloat16)
    tok_out[...] = outgoing.reshape(owners, SUBLANES, LANES)
    tok_in[pl.ds(me, 1)] = tok_out[pl.ds(me, 1)]

    def tok_start(d, carry):
        target = (me + d) % owners
        pltpu.make_async_remote_copy(
            src_ref=tok_out.at[target], dst_ref=tok_in.at[me],
            send_sem=tok_sem.at[0], recv_sem=tok_sem.at[1],
            device_id={"tm": target // ns, "space": target % ns}, device_id_type=MESH,
        ).start()
        return carry

    lax.fori_loop(1, owners, tok_start, 0)
    def line_sent(_, way):
        count = 1 if relays else n - 1
        gathered(field.at[pl.ds(0, frames * count)], block_send.at[way]).wait_send()
        gathered(shares.at[pl.ds(0, count), 0, 0], line_send.at[way]).wait_send()

    if relays:
        beside_line(line_sent)

        @pl.when(middle)
        def _():
            for i in range(3):
                gathered(field.at[pl.ds(0, frames)], relay_send.at[i]).wait_send()
                gathered(shares.at[0, 0, 0], line_relay_send.at[i]).wait_send()

    else:
        line_sent(0, 0)
    gathered(slab_out.at[pl.ds(0, n - 1)], slab_sem.at[0]).wait_send()
    for side in range(2):
        sided(side, lambda: gathered(edge_out.at[side], edge_sem.at[0, side]).wait_send())
    if shared:
        gathered(shares.at[pl.ds(0, n - 1), pl.ds(0, columns - 1), 0], bulk_sem.at[0]).wait_send()
        gathered(shares.at[pl.ds(0, n - 1), :, 0], bulk_sem.at[1]).wait_send()
    halo_copies(lambda copy: copy.wait_send())
    everyone = gathered(tok_in.at[pl.ds(0, owners - 1)], tok_sem.at[0], tok_sem.at[1])
    everyone.wait_recv()
    row = lax.broadcasted_iota(jnp.int32, (owners * most, owners * SUBLANES), 0)
    held = lax.broadcasted_iota(jnp.int32, (owners * most, owners * SUBLANES), 1)
    inner = held % SUBLANES
    chosen = (row == held // SUBLANES * most + inner) & (inner < most)
    tokens_out[...] = jnp.dot(
        jnp.where(chosen, 1.0, 0.0).astype(jnp.bfloat16),
        tok_in[...].reshape(owners * SUBLANES, LANES),
        preferred_element_type=jnp.float32,
    ).astype(jnp.bfloat16)
    everyone.wait_send()


def embedder(channels, tokens, weight, bias, packed):
    held = tokens[...]
    projected = jnp.dot(held[:, :channels], weight[...], preferred_element_type=jnp.float32)
    flags = held[:, channels : channels + 1].astype(jnp.float32)
    packed[...] = ((projected + bias[...]) * flags).astype(jnp.bfloat16)


def shards(
    features,
    frame_counts,
    routes,
    norm_gains,
    conv_weights,
    conv_biases,
    latent_weight,
    embed_weight,
    embed_bias,
):
    feat = features[0]
    frames, rows, cols, width = feat.shape
    cells = frames * rows * cols
    n, ns = lax.axis_size("tm"), lax.axis_size("space")
    ng, nc = lax.axis_size("groups"), lax.axis_size("clip")
    owners = n * ns
    out = conv_weights.shape[1]
    pack = max(1, LANES // out)
    latents = latent_weight.shape[1]
    tok_count = routes.shape[1]
    most = (tok_count + owners - 1) // owners + 1
    vmem = pl.BlockSpec(memory_space=pltpu.VMEM)
    hbm = pl.BlockSpec(memory_space=pltpu.HBM)
    away = lambda value: pltpu.with_memory_space_constraint(value, pltpu.HBM)
    dma = pltpu.SemaphoreType.DMA
    field = pltpu.VMEM((n * frames + 2, rows, cols, width), jnp.bfloat16)
    inner = pltpu.VMEM((frames + 2, rows + 2, cols, width), jnp.bfloat16)
    slab = pltpu.VMEM((n, cells // pack, pack * out), jnp.bfloat16)
    edge = pltpu.VMEM((2, n, frames * cols // pack, pack * out), jnp.bfloat16)
    columns, parts = ng * ns, nc
    if out % (SUBLANES * columns) or width % (LANES * parts):
        columns = parts = 1
    taps = conv_weights.shape[2]
    shares = pltpu.VMEM((n, columns, parts, taps, out // columns, width // parts), jnp.bfloat16)
    cuts = CUTS if frames % CUTS == 0 else 1
    bits = BITS if taps % BITS == 0 else 1
    tok = pltpu.VMEM((owners, SUBLANES, LANES), jnp.bfloat16)
    tokens = pl.pallas_call(
        functools.partial(encoder, n, ns, ng, nc, most, latents),
        out_shape=jax.ShapeDtypeStruct((owners * most, LANES), jnp.bfloat16),
        in_specs=[hbm] * 7 + [pl.BlockSpec(memory_space=pltpu.SMEM)],
        out_specs=vmem,
        scratch_shapes=[
            pltpu.VMEM(feat.shape, feat.dtype),
            pltpu.VMEM(norm_gains.shape, norm_gains.dtype),
            pltpu.VMEM(conv_biases.shape, conv_biases.dtype),
            pltpu.VMEM((latents, width), latent_weight.dtype),
            pltpu.VMEM((1, tok_count), routes.dtype),
            field, inner,
            pltpu.VMEM((9, 3 * out, width), jnp.bfloat16),
            pltpu.VMEM(shares.shape[3:], jnp.bfloat16), shares,
            pltpu.VMEM((owners * SUBLANES, cells), jnp.bfloat16),
            slab, slab, edge, edge, tok, tok,
            dma((5,)), dma, dma((2,)), dma((2,)), dma((3,)), dma((n, cuts)), dma((2,)), dma((2, 2)),
            dma((5,)), dma((5,)), dma((2,)), dma((3,)), dma((n, bits)), dma((n - 1, bits)),
            dma((3,)), dma((2,)),
        ],
        compiler_params=pltpu.CompilerParams(
            collective_id=0, has_side_effects=True, vmem_limit_bytes=GRANT
        ),
    )(
        away(feat),
        away(conv_weights.transpose(0, 2, 1, 3).reshape(2, 9, 3 * out, width)),
        away(conv_weights.transpose(0, 2, 1, 3)),
        away(norm_gains),
        away(conv_biases),
        away(latent_weight.T),
        away(routes.reshape(1, tok_count)),
        frame_counts,
    )
    channels = 4 * latents
    embed = embed_weight.shape[1]
    chunk = embed // 1 if embed % (1 * LANES) == 0 else embed
    packed = pl.pallas_call(
        functools.partial(embedder, channels),
        grid=(embed // chunk,),
        out_shape=jax.ShapeDtypeStruct((owners * most, embed), jnp.bfloat16),
        in_specs=[
            pl.BlockSpec((owners * most, LANES), lambda i: (0, 0)),
            pl.BlockSpec((channels, chunk), lambda i: (0, i)),
            pl.BlockSpec((1, chunk), lambda i: (0, i)),
        ],
        out_specs=pl.BlockSpec((owners * most, chunk), lambda i: (0, i)),
        compiler_params=pltpu.CompilerParams(vmem_limit_bytes=GRANT),
    )(tokens, embed_weight, embed_bias.reshape(1, embed))
    return packed[None]


def solution(mesh):
    return jax.shard_map(
        shards,
        mesh=mesh,
        in_specs=(
            P(("groups", "clip"), "tm", "space", None, None),
            P(("groups", "clip")),
            P(("groups", "clip"), ("tm", "space"), None),
            P(),
            P(None, "tm", None, None),
            P(),
            P(),
            P(),
            P(),
        ),
        out_specs=P(("groups", "clip"), ("tm", "space"), None),
        check_vma=False,
    )
```

```python
import functools

import jax
import jax.numpy as jnp
from jax import lax
from jax.experimental import pallas as pl
from jax.experimental.pallas import tpu as pltpu
from jax.sharding import PartitionSpec as P

MESH = pl.DeviceIdType.MESH
LANES = 128
SUBLANES = 16
CUTS = 2
BITS = 3
GRANT = 28 << 20


def norm_silu(values, gain):
    scale = lax.rsqrt(jnp.mean(values * values, axis=-1, keepdims=True) + 1e-06)
    scaled = values * scale * gain
    return scaled / (1.0 + jnp.exp(-scaled))


def encoder(
    n, ns, ng, nc, most, width_latent,
    feat_any, weights_any, shares_any, gains_any, biases_any, latent_any, owner_any, count,
    tokens_out,
    feat, gains, biases, latent_rows, owner_of, field, inner, taps, mine, shares, placing, slab_out, slab_in, edge_out, edge_in, tok_out, tok_in,
    load_sem, raw_sem, share_sem, block_send, relay_send, block_recv, slab_sem, edge_sem,
    halo_recv, line_send, line_relay_send, line_recv, plane_recv, bulk_sem, tok_sem,
):
    t = lax.axis_index("tm")
    s = lax.axis_index("space")
    g = lax.axis_index("groups")
    core = lax.axis_index("clip")
    me = t * ns + s
    owners = n * ns
    frames, rows, cols, width = feat.shape
    cells = frames * rows * cols
    out = weights_any.shape[2] // 3
    cuts = block_recv.shape[1]
    size = frames // cuts
    pack = max(1, LANES // out)
    relays = n == 4
    columns, parts, share_taps, share_rows, share_lanes = shares.shape[1:]
    bits = line_recv.shape[1]
    bit = share_taps // bits
    shared = columns > 1
    column_of = g * ns + s if shared else 0
    part_of = core if shared else 0

    barrier = pltpu.get_barrier_semaphore()

    def greet(d, carry):
        o = (me + d) % owners
        pl.semaphore_signal(
            barrier, inc=1, device_id={"tm": o // ns, "space": o % ns}, device_id_type=MESH
        )
        return carry

    lax.fori_loop(1, owners, greet, 0)
    expected = owners - 1
    if shared:
        for dg in range(1, ng):
            for other in range(ns):
                pl.semaphore_signal(
                    barrier, inc=1, device_id={"groups": (g + dg) % ng, "space": other},
                    device_id_type=MESH,
                )
                expected += 1
        for dc in range(1, nc):
            pl.semaphore_signal(
                barrier, inc=1, device_id={"clip": (core + dc) % nc}, device_id_type=MESH
            )
            expected += 1
    weight_copy = pltpu.make_async_copy(weights_any.at[0], taps, raw_sem)

    def share_load(col, part, target, sem):
        lanes = pl.ds(pl.multiple_of(part * share_lanes, LANES), share_lanes)
        return pltpu.make_async_copy(
            shares_any.at[1, :, pl.ds(col * share_rows, share_rows), lanes], target, sem
        )

    mine_load = share_load(column_of, part_of, mine, share_sem.at[0])
    loads = [
        pltpu.make_async_copy(source, target, load_sem.at[i])
        for i, (source, target) in enumerate((
            (feat_any, feat), (gains_any, gains), (owner_any, owner_of),
            (biases_any, biases), (latent_any, latent_rows),
        ))
    ]
    for copy in loads[:2]:
        copy.start()
    mine_load.start()
    for copy in loads[2:]:
        copy.start()
    weight_copy.start()

    for col in range(columns):
        for part in range(parts):
            share_load(col, part, shares.at[t, col, part], share_sem.at[1]).start()

    field[0:2] = jnp.zeros((2,) + field.shape[1:], field.dtype)

    @pl.when(t == 0)
    def _():
        inner[0:2] = jnp.zeros((2,) + inner.shape[1:], inner.dtype)

    @pl.when(s == 0)
    def _():
        edge_in[0] = jnp.zeros(edge_in.shape[1:], edge_in.dtype)
        inner[:, 0:1] = jnp.zeros((inner.shape[0], 1) + inner.shape[2:], inner.dtype)

    @pl.when(s == ns - 1)
    def _():
        edge_in[1] = jnp.zeros(edge_in.shape[1:], edge_in.dtype)
        inner[:, rows + 1 :] = jnp.zeros((inner.shape[0], 1) + inner.shape[2:], inner.dtype)

    for copy in loads[:2]:
        copy.wait()
    inputs = feat[...].reshape(cells, width).astype(jnp.float32)

    def block_copy(c, f, target, send_sem):
        span = field.at[pl.ds(2 + frames * c + size * f, size)]
        return pltpu.make_async_remote_copy(
            src_ref=span, dst_ref=span, send_sem=send_sem, recv_sem=block_recv.at[c, f],
            device_id={"tm": target}, device_id_type=MESH,
        )

    def slab_copy(source, target):
        return pltpu.make_async_remote_copy(
            src_ref=slab_out.at[target], dst_ref=slab_in.at[source],
            send_sem=slab_sem.at[0], recv_sem=slab_sem.at[1],
            device_id={"tm": target}, device_id_type=MESH,
        )

    def edge_copy(side, source, target):
        return pltpu.make_async_remote_copy(
            src_ref=edge_out.at[side, target], dst_ref=edge_in.at[side, source],
            send_sem=edge_sem.at[0, side], recv_sem=edge_sem.at[1, side],
            device_id={"tm": target, "space": (s + 1 - 2 * side + ns) % ns}, device_id_type=MESH,
        )

    def gathered(ref, send_sem, recv_sem=None):
        return pltpu.make_async_remote_copy(
            src_ref=ref, dst_ref=ref, send_sem=send_sem,
            recv_sem=send_sem if recv_sem is None else recv_sem,
            device_id={"tm": t}, device_id_type=MESH,
        )

    def sided(side, act):
        pl.when(s < ns - 1 if side == 0 else s > 0)(act)

    def fed(side, act):
        pl.when(s > 0 if side == 0 else s < ns - 1)(act)

    def line_copy(q, k, target, send_sem, own=False):
        piece = shares.at[q, column_of, part_of, pl.ds(bit * k, bit)]
        return pltpu.make_async_remote_copy(
            src_ref=mine.at[pl.ds(bit * k, bit)] if own else piece, dst_ref=piece,
            send_sem=send_sem, recv_sem=line_recv.at[q, k],
            device_id={"tm": target}, device_id_type=MESH,
        )

    def plane_copy(q, k, d):
        piece = shares.at[q, column_of, part_of, pl.ds(bit * k, bit)]
        return pltpu.make_async_remote_copy(
            src_ref=piece, dst_ref=piece, send_sem=bulk_sem.at[0],
            recv_sem=plane_recv.at[(q - t + n) % n - 1, k],
            device_id={"groups": (g + d // ns) % ng, "space": (s + d % ns) % ns}, device_id_type=MESH,
        )

    def core_copy(q, col, k, d):
        piece = shares.at[q, col, part_of, pl.ds(bit * k, bit)]
        return pltpu.make_async_remote_copy(
            src_ref=piece, dst_ref=piece, send_sem=bulk_sem.at[1], recv_sem=bulk_sem.at[2],
            device_id={"clip": (core + d) % nc}, device_id_type=MESH,
        )

    def beside_line(act):
        for way in range(2):
            target = t - 1 + 2 * way
            pl.when((target >= 0) & (target < n))(
                functools.partial(act, (target + n) % n, way)
            )

    def around(act):
        def each(d, carry):
            act((t + d) % n, 0)
            return carry

        lax.fori_loop(1, n, each, 0)

    reach = beside_line if relays else around
    def send_blocks(spot, way):
        for f in range(cuts):
            block_copy(t, f, spot, block_send.at[way]).start()

    def send_lines(spot, way):
        for k in range(bits):
            line_copy(t, k, spot, line_send.at[way], own=True).start()

    middle = (t == 1) | (t == 2)
    low = t == 1
    end, mate, far = [jnp.where(low, one, two) for one, two in ((0, 3), (2, 1), (3, 0))]
    courses = ((end, mate), (mate, end), (far, end))

    def relay_copy(i, f):
        q, target = courses[i]
        return block_copy(q, f, target, relay_send.at[i])

    def line_relay(i, k):
        q, target = courses[i]
        return line_copy(q, k, target, line_relay_send.at[i])

    def relay_block(*which):
        for f in range(cuts):
            for i in which:
                q = courses[i][0]
                block_copy(q, f, q, block_send.at[0]).wait_recv()
                relay_copy(i, f).start()

    def pass_bit(q, k):
        if shared:
            for d in range(1, columns):
                plane_copy(q, k, d).start()
            for d in range(1, nc):
                core_copy(q, column_of, k, d).start()

    def line_came(q, k):
        line_copy(q, k, q, line_send.at[0]).wait_recv()

    def pass_on(q):
        for k in range(bits):
            line_came(q, k)
            pass_bit(q, k)

    def cross(q):
        for k in range(bits):
            gathered(
                shares.at[0, pl.ds(0, columns - 1), 0, pl.ds(0, bit)],
                bulk_sem.at[0], plane_recv.at[(q - t + n) % n - 1, k],
            ).wait_recv()
            for d in range(1, columns):
                for dc in range(1, nc):
                    core_copy(q, (column_of + d) % columns, k, dc).start()

    def arrived(c):
        for f in range(cuts):
            block_copy(c, f, c, block_send.at[0]).wait_recv()

    grid_rows = rows + 2
    column = lax.broadcasted_iota(jnp.int32, (frames * grid_rows * cols, 1), 0) % cols

    def fold(values):
        part = values.shape[0] // pack
        return jnp.concatenate([values[j * part : (j + 1) * part] for j in range(pack)], axis=1)

    def unfold(pieces):
        return jnp.concatenate(
            [
                jnp.concatenate([piece[:, j * out : (j + 1) * out] for piece in pieces], axis=1)
                for j in range(pack)
            ],
            axis=0,
        )

    def beside(left, middle, right):
        count = left.shape[0]
        mark = column[:count]
        left = jnp.where(mark == 0, 0.0, pltpu.roll(left, 1, 0))
        right = jnp.where(mark == cols - 1, 0.0, pltpu.roll(right, count - 1, 0))
        return left + middle + right

    def one(b):
        span = jnp.concatenate(
            [field[pl.ds(frames * b + a, frames)].reshape(cells, width) for a in range(3)], axis=1
        )
        sums = [
            lax.dot_general(
                span, jnp.concatenate([taps[3 * a + r] for a in range(3)], axis=1),
                (((1,), (1,)), ((), ())), preferred_element_type=jnp.float32,
            ).reshape(frames, rows, cols, 3 * out)
            for r in range(3)
        ]
        wide = jnp.concatenate(
            [
                functools.reduce(
                    jnp.add,
                    [sums[r][:, row : row + 1] for r in range(3) for row in [j - 2 + r] if 0 <= row < rows],
                )
                for j in range(grid_rows)
            ],
            axis=1,
        ).reshape(frames * grid_rows * cols, 3 * out)
        summed = beside(wide[:, :out], wide[:, out : 2 * out], wide[:, 2 * out :])
        summed = summed.reshape(frames, grid_rows, cols, out)
        edges = (
            summed[:, rows + 1 :].reshape(frames * cols, out),
            summed[:, :1].reshape(frames * cols, out),
        )
        packed = fold(summed[:, 1 : rows + 1].reshape(cells, out)).astype(jnp.bfloat16)

        for side in range(2):

            def give(side=side):
                edge_out[side, pl.ds(b, 1)] = fold(edges[side]).astype(jnp.bfloat16)[None]
                edge_copy(side, t, b).start()

            sided(side, give)

        @pl.when(b == t)
        def _():
            slab_in[pl.ds(t, 1)] = packed[None]

        @pl.when(b != t)
        def _():
            slab_out[pl.ds(b, 1)] = packed[None]
            slab_copy(t, b).start()

    def halo_copies(act):
        near, far = pl.ds(frames, 2), pl.ds(0, 2)
        own, body = pl.ds(2, frames), pl.ds(1, rows)
        up = {"tm": (t + 1) % n}
        more = t < n - 1

        def copy(i, here, source, target, device):
            pl.when(here)(
                lambda: act(
                    pltpu.make_async_remote_copy(
                        src_ref=inner.at[source], dst_ref=inner.at[target],
                        send_sem=load_sem.at[i], recv_sem=halo_recv.at[i],
                        device_id=device, device_id_type=MESH,
                    )
                )
            )

        left, right = {"space": (s + ns - 1) % ns}, {"space": (s + 1) % ns}
        first, last = pl.ds(1, 1), pl.ds(rows, 1)
        above, below = pl.ds(0, 1), pl.ds(rows + 1, 1)
        copy(1, more & (s > 0), (near, first), (far, below), up | left)
        copy(2, more & (s < ns - 1), (near, last), (far, above), up | right)
        copy(0, more, (near, body), (far, body), up)
        copy(3, s > 0, (own, first), (own, below), left)
        copy(4, s < ns - 1, (own, last), (own, above), right)

    def halo_came():
        def wait(i, here, target):
            def act():
                span = inner.at[target]
                pltpu.make_async_remote_copy(
                    src_ref=span, dst_ref=span, send_sem=load_sem.at[i],
                    recv_sem=halo_recv.at[i], device_id={"tm": t}, device_id_type=MESH,
                ).wait_recv()

            pl.when(here)(act)

        far, own, body = pl.ds(0, 2), pl.ds(2, frames), pl.ds(1, rows)
        above, below = pl.ds(0, 1), pl.ds(rows + 1, 1)
        wait(3, s < ns - 1, (own, below))
        wait(4, s > 0, (own, above))
        wait(0, t > 0, (far, body))
        wait(1, (t > 0) & (s < ns - 1), (far, below))
        wait(2, (t > 0) & (s > 0), (far, above))

    def kernel_of(tap):
        return jnp.concatenate(
            [
                jnp.concatenate([shares[q, col, part, tap] for part in range(parts)], axis=1)
                for q in range(n)
                for col in range(columns)
            ],
            axis=0,
        )

    field[pl.ds(2 + frames * t, frames)] = norm_silu(inputs, gains[0:1]).astype(
        jnp.bfloat16
    ).reshape(frames, rows, cols, width)
    for copy in loads[2:]:
        copy.wait()
    toks = owner_of.shape[1]
    before = lax.broadcasted_iota(jnp.int32, (toks, toks), 0)
    after = lax.broadcasted_iota(jnp.int32, (toks, toks), 1)
    owner = owner_of[...]
    owner_column = jnp.sum(jnp.where(before == after, owner, 0), axis=1, keepdims=True)
    same = (owner_column == owner) & (before < after)
    rank = jnp.sum(jnp.where(same, 1, 0), axis=0, keepdims=True)
    slots = lax.broadcasted_iota(jnp.int32, (owners * SUBLANES, toks), 0)
    slotted = jnp.where(slots == owner * SUBLANES + rank, 1.0, 0.0).astype(jnp.bfloat16)
    spot = lax.broadcasted_iota(jnp.int32, (toks, cells), 1)
    patch = (spot // (2 * cols)) * (cols // 2) + spot % cols // 2
    held = patch == lax.broadcasted_iota(jnp.int32, (toks, cells), 0)
    placing[...] = jnp.dot(
        slotted, jnp.where(held, 1.0, 0.0).astype(jnp.bfloat16), preferred_element_type=jnp.float32
    ).astype(jnp.bfloat16)
    mine_load.wait()
    pl.semaphore_wait(barrier, expected)
    start = lambda copy: copy.start()
    reach(send_blocks)
    reach(send_lines)
    weight_copy.wait()
    if relays:
        order = ((0, 1, 2, 3), (3, 2, 0, 1), (0, 3, 1, 2), (3, 2, 0, 1))
        flow = ((1, 2, 3), (0, 2, 3), (3, 1, 0), (2, 1, 0))

        def forward():
            relay_block(0, 1)
            pass_on(end)
            pass_on(mate)
            for k in range(bits):
                line_relay(0, k).start()
                line_relay(1, k).start()
            relay_block(2)

        def last(q):
            for k in range(bits):
                line_came(q, k)
                line_relay(2, k).start()
                pass_bit(q, k)

        before = (
            ((), ((arrived, 1),), ((pass_on, 1), (arrived, 2)), ((pass_on, 2), (arrived, 3))),
            ((), ((last, 3),), (), ()),
            ((), (), ((last, 0),), ()),
            (((arrived, 2),), ((pass_on, 2), (arrived, 1)), ((pass_on, 1), (arrived, 0)), ()),
        )

        def pick(table, k):
            spot = table[0][k]
            for i in range(1, n):
                spot = jnp.where(t == i, table[i][k], spot)
            return spot

        def chosen(table, k):
            spot = pick(table, 0)
            for kk in range(1, len(table[0])):
                spot = jnp.where(k == kk, pick(table, kk), spot)
            return spot

        pl.when(middle)(forward)

        def step(k, carry):
            for i in range(n):
                for kk in range(n):
                    if before[i][kk]:

                        @pl.when((t == i) & (k == kk))
                        def _():
                            for act, c in before[i][kk]:
                                act(c)

            one(chosen(order, k))
            return carry

        lax.fori_loop(0, n, step, 0)
        pl.when(jnp.logical_not(middle))(lambda: pass_on(pick(flow, 2)))
    else:

        def hold(d, carry):
            arrived((t + d) % n)
            return carry

        lax.fori_loop(1, n, hold, 0)

        def step(d, carry):
            one((t + d) % n)
            return carry

        lax.fori_loop(1, n + 1, step, 0)

    gathered(slab_in.at[pl.ds(0, n - 1)], slab_sem.at[0], slab_sem.at[1]).wait_recv()
    for side in range(2):
        fed(side, lambda: gathered(edge_in.at[side], edge_sem.at[0, side], edge_sem.at[1, side]).wait_recv())
    hidden = unfold([slab_in[q].astype(jnp.float32) for q in range(n)])
    top, bottom = [
        unfold([edge_in[side, q].astype(jnp.float32) for q in range(n)]).reshape(
            frames, 1, cols, width
        )
        for side in range(2)
    ]
    hidden = hidden.reshape(frames, rows, cols, width)
    if rows > 1:
        hidden = jnp.concatenate(
            [hidden[:, :1] + top, hidden[:, 1 : rows - 1], hidden[:, rows - 1 :] + bottom], axis=1
        )
    else:
        hidden = hidden + top + bottom
    hidden = hidden.reshape(cells, width) + biases[0:1]
    inner[2:, 1 : rows + 1] = norm_silu(hidden, gains[1:2]).astype(jnp.bfloat16).reshape(
        frames, rows, cols, width
    )
    halo_copies(start)
    if not relays:

        def passed(d, carry):
            pass_on((t + d) % n)
            return carry

        lax.fori_loop(1, n, passed, 0)
    if shared:

        def crossed(k, carry):
            if relays:
                q = chosen(flow, k)
            else:
                q = (t + 1 + k) % n
            cross(q)
            return carry

        lax.fori_loop(0, n - 1, crossed, 0)
    pltpu.make_async_copy(shares.at[t], shares.at[t], share_sem.at[1]).wait()
    halo_came()
    if shared:

        gathered(shares.at[pl.ds(0, n - 1), :, 0], bulk_sem.at[1], bulk_sem.at[2]).wait_recv()
    sums = []
    for e in range(3):
        total = None
        for a in range(3):
            for r in range(3):
                block = inner[a : a + frames, r : r + rows].reshape(cells, width)
                term = lax.dot_general(
                    block, kernel_of(9 * a + 3 * r + e),
                    (((1,), (1,)), ((), ())), preferred_element_type=jnp.float32,
                )
                total = term if total is None else total + term
        sums.append(total)
    hidden = beside(*sums) + biases[1:2]
    merged = feat[...].reshape(cells, width).astype(jnp.float32) + hidden
    active = norm_silu(merged, gains[2:3]).astype(jnp.bfloat16)
    rest = jnp.zeros((LANES - 4 * width_latent, width), jnp.bfloat16)
    latent_wide = jnp.concatenate([latent_rows[...]] * 4 + [rest], axis=0)
    latent = lax.dot_general(
        active, latent_wide, (((1,), (1,)), ((), ())), preferred_element_type=jnp.float32
    )
    cell = lax.broadcasted_iota(jnp.int32, (cells, LANES), 0)
    lane = lax.broadcasted_iota(jnp.int32, (cells, LANES), 1)
    corner = (cell // cols % 2) * 2 + cell % 2
    alive = (t * frames + cell // (rows * cols) < count[0]) & (corner == 0)
    flagged = jnp.where((lane == 4 * width_latent) & alive, 1.0, 0.0)
    patches = jnp.where(lane // width_latent == corner, latent, flagged).astype(jnp.bfloat16)
    outgoing = jnp.dot(
        placing[...], patches, preferred_element_type=jnp.float32
    ).astype(jnp.bfloat16)
    tok_out[...] = outgoing.reshape(owners, SUBLANES, LANES)
    tok_in[pl.ds(me, 1)] = tok_out[pl.ds(me, 1)]

    def tok_start(d, carry):
        target = (me + d) % owners
        pltpu.make_async_remote_copy(
            src_ref=tok_out.at[target], dst_ref=tok_in.at[me],
            send_sem=tok_sem.at[0], recv_sem=tok_sem.at[1],
            device_id={"tm": target // ns, "space": target % ns}, device_id_type=MESH,
        ).start()
        return carry

    lax.fori_loop(1, owners, tok_start, 0)
    def line_sent(_, way):
        count = 1 if relays else n - 1
        gathered(field.at[pl.ds(0, frames * count)], block_send.at[way]).wait_send()
        gathered(shares.at[pl.ds(0, count), 0, 0], line_send.at[way]).wait_send()

    if relays:
        beside_line(line_sent)

        @pl.when(middle)
        def _():
            for i in range(3):
                gathered(field.at[pl.ds(0, frames)], relay_send.at[i]).wait_send()
                gathered(shares.at[0, 0, 0], line_relay_send.at[i]).wait_send()

    else:
        line_sent(0, 0)
    gathered(slab_out.at[pl.ds(0, n - 1)], slab_sem.at[0]).wait_send()
    for side in range(2):
        sided(side, lambda: gathered(edge_out.at[side], edge_sem.at[0, side]).wait_send())
    if shared:
        gathered(shares.at[pl.ds(0, n - 1), pl.ds(0, columns - 1), 0], bulk_sem.at[0]).wait_send()
        gathered(shares.at[pl.ds(0, n - 1), :, 0], bulk_sem.at[1]).wait_send()
    halo_copies(lambda copy: copy.wait_send())
    everyone = gathered(tok_in.at[pl.ds(0, owners - 1)], tok_sem.at[0], tok_sem.at[1])
    everyone.wait_recv()
    row = lax.broadcasted_iota(jnp.int32, (owners * most, owners * SUBLANES), 0)
    held = lax.broadcasted_iota(jnp.int32, (owners * most, owners * SUBLANES), 1)
    inner = held % SUBLANES
    chosen = (row == held // SUBLANES * most + inner) & (inner < most)
    tokens_out[...] = jnp.dot(
        jnp.where(chosen, 1.0, 0.0).astype(jnp.bfloat16),
        tok_in[...].reshape(owners * SUBLANES, LANES),
        preferred_element_type=jnp.float32,
    ).astype(jnp.bfloat16)
    everyone.wait_send()


def embedder(channels, tokens, weight, bias, packed):
    held = tokens[...]
    projected = jnp.dot(held[:, :channels], weight[...], preferred_element_type=jnp.float32)
    flags = held[:, channels : channels + 1].astype(jnp.float32)
    packed[...] = ((projected + bias[...]) * flags).astype(jnp.bfloat16)


def shards(
    features,
    frame_counts,
    routes,
    norm_gains,
    conv_weights,
    conv_biases,
    latent_weight,
    embed_weight,
    embed_bias,
):
    feat = features[0]
    frames, rows, cols, width = feat.shape
    cells = frames * rows * cols
    n, ns = lax.axis_size("tm"), lax.axis_size("space")
    ng, nc = lax.axis_size("groups"), lax.axis_size("clip")
    owners = n * ns
    out = conv_weights.shape[1]
    pack = max(1, LANES // out)
    latents = latent_weight.shape[1]
    tok_count = routes.shape[1]
    most = (tok_count + owners - 1) // owners + 1
    vmem = pl.BlockSpec(memory_space=pltpu.VMEM)
    hbm = pl.BlockSpec(memory_space=pltpu.HBM)
    away = lambda value: pltpu.with_memory_space_constraint(value, pltpu.HBM)
    dma = pltpu.SemaphoreType.DMA
    field = pltpu.VMEM((n * frames + 2, rows, cols, width), jnp.bfloat16)
    inner = pltpu.VMEM((frames + 2, rows + 2, cols, width), jnp.bfloat16)
    slab = pltpu.VMEM((n, cells // pack, pack * out), jnp.bfloat16)
    edge = pltpu.VMEM((2, n, frames * cols // pack, pack * out), jnp.bfloat16)
    columns, parts = ng * ns, nc
    if out % (SUBLANES * columns) or width % (LANES * parts):
        columns = parts = 1
    taps = conv_weights.shape[2]
    shares = pltpu.VMEM((n, columns, parts, taps, out // columns, width // parts), jnp.bfloat16)
    cuts = CUTS if frames % CUTS == 0 else 1
    bits = BITS if taps % BITS == 0 else 1
    tok = pltpu.VMEM((owners, SUBLANES, LANES), jnp.bfloat16)
    tokens = pl.pallas_call(
        functools.partial(encoder, n, ns, ng, nc, most, latents),
        out_shape=jax.ShapeDtypeStruct((owners * most, LANES), jnp.bfloat16),
        in_specs=[hbm] * 7 + [pl.BlockSpec(memory_space=pltpu.SMEM)],
        out_specs=vmem,
        scratch_shapes=[
            pltpu.VMEM(feat.shape, feat.dtype),
            pltpu.VMEM(norm_gains.shape, norm_gains.dtype),
            pltpu.VMEM(conv_biases.shape, conv_biases.dtype),
            pltpu.VMEM((latents, width), latent_weight.dtype),
            pltpu.VMEM((1, tok_count), routes.dtype),
            field, inner,
            pltpu.VMEM((9, 3 * out, width), jnp.bfloat16),
            pltpu.VMEM(shares.shape[3:], jnp.bfloat16), shares,
            pltpu.VMEM((owners * SUBLANES, cells), jnp.bfloat16),
            slab, slab, edge, edge, tok, tok,
            dma((5,)), dma, dma((2,)), dma((2,)), dma((3,)), dma((n, cuts)), dma((2,)), dma((2, 2)),
            dma((5,)), dma((2,)), dma((3,)), dma((n, bits)), dma((n - 1, bits)),
            dma((3,)), dma((2,)),
        ],
        compiler_params=pltpu.CompilerParams(
            collective_id=0, has_side_effects=True, vmem_limit_bytes=GRANT
        ),
    )(
        away(feat),
        away(conv_weights.transpose(0, 2, 1, 3).reshape(2, 9, 3 * out, width)),
        away(conv_weights.transpose(0, 2, 1, 3)),
        away(norm_gains),
        away(conv_biases),
        away(latent_weight.T),
        away(routes.reshape(1, tok_count)),
        frame_counts,
    )
    channels = 4 * latents
    embed = embed_weight.shape[1]
    chunk = embed // 1 if embed % (1 * LANES) == 0 else embed
    packed = pl.pallas_call(
        functools.partial(embedder, channels),
        grid=(embed // chunk,),
        out_shape=jax.ShapeDtypeStruct((owners * most, embed), jnp.bfloat16),
        in_specs=[
            pl.BlockSpec((owners * most, LANES), lambda i: (0, 0)),
            pl.BlockSpec((channels, chunk), lambda i: (0, i)),
            pl.BlockSpec((1, chunk), lambda i: (0, i)),
        ],
        out_specs=pl.BlockSpec((owners * most, chunk), lambda i: (0, i)),
        compiler_params=pltpu.CompilerParams(vmem_limit_bytes=GRANT),
    )(tokens, embed_weight, embed_bias.reshape(1, embed))
    return packed[None]


def solution(mesh):
    return jax.shard_map(
        shards,
        mesh=mesh,
        in_specs=(
            P(("groups", "clip"), "tm", "space", None, None),
            P(("groups", "clip")),
            P(("groups", "clip"), ("tm", "space"), None),
            P(),
            P(None, "tm", None, None),
            P(),
            P(),
            P(),
            P(),
        ),
        out_specs=P(("groups", "clip"), ("tm", "space"), None),
        check_vma=False,
    )
```

```python
import functools

import jax
import jax.numpy as jnp
from jax import lax
from jax.experimental import pallas as pl
from jax.experimental.pallas import tpu as pltpu
from jax.sharding import PartitionSpec as P

MESH = pl.DeviceIdType.MESH
LANES = 128
SUBLANES = 16
CUTS = 2
BITS = 3
GRANT = 28 << 20


def norm_silu(values, gain):
    scale = lax.rsqrt(jnp.mean(values * values, axis=-1, keepdims=True) + 1e-06)
    scaled = values * scale * gain
    return scaled / (1.0 + jnp.exp(-scaled))


def encoder(
    n, ns, ng, nc, most, width_latent,
    feat_any, weights_any, shares_any, gains_any, biases_any, latent_any, owner_any, count,
    tokens_out,
    feat, gains, biases, latent_rows, owner_of, field, inner, taps, mine, shares, placing, slab_out, slab_in, edge_out, edge_in, tok_out, tok_in,
    load_sem, raw_sem, share_sem, block_send, relay_send, block_recv, slab_sem, edge_sem,
    halo_recv, line_send, line_relay_send, line_recv, plane_recv, bulk_sem, tok_sem,
):
    t = lax.axis_index("tm")
    s = lax.axis_index("space")
    g = lax.axis_index("groups")
    core = lax.axis_index("clip")
    me = t * ns + s
    owners = n * ns
    frames, rows, cols, width = feat.shape
    cells = frames * rows * cols
    out = weights_any.shape[2] // 3
    cuts = block_recv.shape[1]
    size = frames // cuts
    pack = max(1, LANES // out)
    relays = n == 4
    columns, parts, share_taps, share_rows, share_lanes = shares.shape[1:]
    bits = line_recv.shape[1]
    bit = share_taps // bits
    shared = columns > 1
    column_of = g * ns + s if shared else 0
    part_of = core if shared else 0

    barrier = pltpu.get_barrier_semaphore()

    def greet(d, carry):
        o = (me + d) % owners
        pl.semaphore_signal(
            barrier, inc=1, device_id={"tm": o // ns, "space": o % ns}, device_id_type=MESH
        )
        return carry

    lax.fori_loop(1, owners, greet, 0)
    expected = owners - 1
    if shared:
        for dg in range(1, ng):
            for other in range(ns):
                pl.semaphore_signal(
                    barrier, inc=1, device_id={"groups": (g + dg) % ng, "space": other},
                    device_id_type=MESH,
                )
                expected += 1
        for dc in range(1, nc):
            pl.semaphore_signal(
                barrier, inc=1, device_id={"clip": (core + dc) % nc}, device_id_type=MESH
            )
            expected += 1
    weight_copy = pltpu.make_async_copy(weights_any.at[0], taps, raw_sem)

    def share_load(col, part, target, sem):
        lanes = pl.ds(pl.multiple_of(part * share_lanes, LANES), share_lanes)
        return pltpu.make_async_copy(
            shares_any.at[1, :, pl.ds(col * share_rows, share_rows), lanes], target, sem
        )

    mine_load = share_load(column_of, part_of, mine, share_sem.at[0])
    loads = [
        pltpu.make_async_copy(source, target, load_sem.at[i])
        for i, (source, target) in enumerate((
            (feat_any, feat), (gains_any, gains), (owner_any, owner_of),
            (biases_any, biases), (latent_any, latent_rows),
        ))
    ]
    for copy in loads[:2]:
        copy.start()
    mine_load.start()
    for copy in loads[2:]:
        copy.start()
    weight_copy.start()

    for col in range(columns):
        for part in range(parts):
            share_load(col, part, shares.at[t, col, part], share_sem.at[1]).start()

    field[0:2] = jnp.zeros((2,) + field.shape[1:], field.dtype)

    @pl.when(t == 0)
    def _():
        inner[0:2] = jnp.zeros((2,) + inner.shape[1:], inner.dtype)

    @pl.when(s == 0)
    def _():
        edge_in[0] = jnp.zeros(edge_in.shape[1:], edge_in.dtype)
        inner[:, 0:1] = jnp.zeros((inner.shape[0], 1) + inner.shape[2:], inner.dtype)

    @pl.when(s == ns - 1)
    def _():
        edge_in[1] = jnp.zeros(edge_in.shape[1:], edge_in.dtype)
        inner[:, rows + 1 :] = jnp.zeros((inner.shape[0], 1) + inner.shape[2:], inner.dtype)

    for copy in loads[:2]:
        copy.wait()
    inputs = feat[...].reshape(cells, width).astype(jnp.float32)

    def block_copy(c, f, target, send_sem):
        span = field.at[pl.ds(2 + frames * c + size * f, size)]
        return pltpu.make_async_remote_copy(
            src_ref=span, dst_ref=span, send_sem=send_sem, recv_sem=block_recv.at[c, f],
            device_id={"tm": target}, device_id_type=MESH,
        )

    def slab_copy(source, target):
        return pltpu.make_async_remote_copy(
            src_ref=slab_out.at[target], dst_ref=slab_in.at[source],
            send_sem=slab_sem.at[0], recv_sem=slab_sem.at[1],
            device_id={"tm": target}, device_id_type=MESH,
        )

    def edge_copy(side, source, target):
        return pltpu.make_async_remote_copy(
            src_ref=edge_out.at[side, target], dst_ref=edge_in.at[side, source],
            send_sem=edge_sem.at[0, side], recv_sem=edge_sem.at[1, side],
            device_id={"tm": target, "space": (s + 1 - 2 * side + ns) % ns}, device_id_type=MESH,
        )

    def gathered(ref, send_sem, recv_sem=None):
        return pltpu.make_async_remote_copy(
            src_ref=ref, dst_ref=ref, send_sem=send_sem,
            recv_sem=send_sem if recv_sem is None else recv_sem,
            device_id={"tm": t}, device_id_type=MESH,
        )

    def sided(side, act):
        pl.when(s < ns - 1 if side == 0 else s > 0)(act)

    def fed(side, act):
        pl.when(s > 0 if side == 0 else s < ns - 1)(act)

    def line_copy(q, k, target, send_sem, own=False):
        piece = shares.at[q, column_of, part_of, pl.ds(bit * k, bit)]
        return pltpu.make_async_remote_copy(
            src_ref=mine.at[pl.ds(bit * k, bit)] if own else piece, dst_ref=piece,
            send_sem=send_sem, recv_sem=line_recv.at[q, k],
            device_id={"tm": target}, device_id_type=MESH,
        )

    def plane_copy(q, k, d):
        piece = shares.at[q, column_of, part_of, pl.ds(bit * k, bit)]
        return pltpu.make_async_remote_copy(
            src_ref=piece, dst_ref=piece, send_sem=bulk_sem.at[0],
            recv_sem=plane_recv.at[(q - t + n) % n - 1, k],
            device_id={"groups": (g + d // ns) % ng, "space": (s + d % ns) % ns}, device_id_type=MESH,
        )

    def core_copy(q, col, k, d):
        piece = shares.at[q, col, part_of, pl.ds(bit * k, bit)]
        return pltpu.make_async_remote_copy(
            src_ref=piece, dst_ref=piece, send_sem=bulk_sem.at[1], recv_sem=bulk_sem.at[2],
            device_id={"clip": (core + d) % nc}, device_id_type=MESH,
        )

    def beside_line(act):
        for way in range(2):
            target = t - 1 + 2 * way
            pl.when((target >= 0) & (target < n))(
                functools.partial(act, (target + n) % n, way)
            )

    def around(act):
        def each(d, carry):
            act((t + d) % n, 0)
            return carry

        lax.fori_loop(1, n, each, 0)

    reach = beside_line if relays else around
    def send_blocks(spot, way):
        for f in range(cuts):
            block_copy(t, f, spot, block_send.at[way]).start()

    def send_lines(spot, way):
        for k in range(bits):
            line_copy(t, k, spot, line_send.at[way], own=True).start()

    middle = (t == 1) | (t == 2)
    low = t == 1
    end, mate, far = [jnp.where(low, one, two) for one, two in ((0, 3), (2, 1), (3, 0))]
    courses = ((end, mate), (mate, end), (far, end))

    def relay_copy(i, f):
        q, target = courses[i]
        return block_copy(q, f, target, relay_send.at[i])

    def line_relay(i, k):
        q, target = courses[i]
        return line_copy(q, k, target, line_relay_send.at[i])

    def relay_block(*which):
        for f in range(cuts):
            for i in which:
                q = courses[i][0]
                block_copy(q, f, q, block_send.at[0]).wait_recv()
                relay_copy(i, f).start()

    def pass_bit(q, k):
        if shared:
            for d in range(1, columns):
                plane_copy(q, k, d).start()
            for d in range(1, nc):
                core_copy(q, column_of, k, d).start()

    def line_came(q, k):
        line_copy(q, k, q, line_send.at[0]).wait_recv()

    def pass_on(q):
        for k in range(bits):
            line_came(q, k)
            pass_bit(q, k)

    def cross(q):
        for k in range(bits):
            gathered(
                shares.at[0, pl.ds(0, columns - 1), 0, pl.ds(0, bit)],
                bulk_sem.at[0], plane_recv.at[(q - t + n) % n - 1, k],
            ).wait_recv()
            for d in range(1, columns):
                for dc in range(1, nc):
                    core_copy(q, (column_of + d) % columns, k, dc).start()

    def arrived(c):
        for f in range(cuts):
            block_copy(c, f, c, block_send.at[0]).wait_recv()

    grid_rows = rows + 2
    column = lax.broadcasted_iota(jnp.int32, (frames * grid_rows * cols, 1), 0) % cols

    def fold(values):
        part = values.shape[0] // pack
        return jnp.concatenate([values[j * part : (j + 1) * part] for j in range(pack)], axis=1)

    def unfold(pieces):
        return jnp.concatenate(
            [
                jnp.concatenate([piece[:, j * out : (j + 1) * out] for piece in pieces], axis=1)
                for j in range(pack)
            ],
            axis=0,
        )

    def beside(left, middle, right):
        count = left.shape[0]
        mark = column[:count]
        left = jnp.where(mark == 0, 0.0, pltpu.roll(left, 1, 0))
        right = jnp.where(mark == cols - 1, 0.0, pltpu.roll(right, count - 1, 0))
        return left + middle + right

    def one(b):
        span = jnp.concatenate(
            [field[pl.ds(frames * b + a, frames)].reshape(cells, width) for a in range(3)], axis=1
        )
        sums = [
            lax.dot_general(
                span, jnp.concatenate([taps[3 * a + r] for a in range(3)], axis=1),
                (((1,), (1,)), ((), ())), preferred_element_type=jnp.float32,
            ).reshape(frames, rows, cols, 3 * out)
            for r in range(3)
        ]
        wide = jnp.concatenate(
            [
                functools.reduce(
                    jnp.add,
                    [sums[r][:, row : row + 1] for r in range(3) for row in [j - 2 + r] if 0 <= row < rows],
                )
                for j in range(grid_rows)
            ],
            axis=1,
        ).reshape(frames * grid_rows * cols, 3 * out)
        summed = beside(wide[:, :out], wide[:, out : 2 * out], wide[:, 2 * out :])
        summed = summed.reshape(frames, grid_rows, cols, out)
        edges = (
            summed[:, rows + 1 :].reshape(frames * cols, out),
            summed[:, :1].reshape(frames * cols, out),
        )
        packed = fold(summed[:, 1 : rows + 1].reshape(cells, out)).astype(jnp.bfloat16)

        for side in range(2):

            def give(side=side):
                edge_out[side, pl.ds(b, 1)] = fold(edges[side]).astype(jnp.bfloat16)[None]
                edge_copy(side, t, b).start()

            sided(side, give)

        @pl.when(b == t)
        def _():
            slab_in[pl.ds(t, 1)] = packed[None]

        @pl.when(b != t)
        def _():
            slab_out[pl.ds(b, 1)] = packed[None]
            slab_copy(t, b).start()

    def halo_copies(act):
        near, far = pl.ds(frames, 2), pl.ds(0, 2)
        own, body = pl.ds(2, frames), pl.ds(1, rows)
        up = {"tm": (t + 1) % n}
        more = t < n - 1

        def copy(i, here, source, target, device):
            pl.when(here)(
                lambda: act(
                    pltpu.make_async_remote_copy(
                        src_ref=inner.at[source], dst_ref=inner.at[target],
                        send_sem=load_sem.at[i], recv_sem=halo_recv.at[i],
                        device_id=device, device_id_type=MESH,
                    )
                )
            )

        left, right = {"space": (s + ns - 1) % ns}, {"space": (s + 1) % ns}
        first, last = pl.ds(1, 1), pl.ds(rows, 1)
        above, below = pl.ds(0, 1), pl.ds(rows + 1, 1)
        copy(1, more & (s > 0), (near, first), (far, below), up | left)
        copy(2, more & (s < ns - 1), (near, last), (far, above), up | right)
        copy(0, more, (near, body), (far, body), up)
        copy(3, s > 0, (own, first), (own, below), left)
        copy(4, s < ns - 1, (own, last), (own, above), right)

    def halo_came():
        def wait(i, here, target):
            def act():
                span = inner.at[target]
                pltpu.make_async_remote_copy(
                    src_ref=span, dst_ref=span, send_sem=load_sem.at[i],
                    recv_sem=halo_recv.at[i], device_id={"tm": t}, device_id_type=MESH,
                ).wait_recv()

            pl.when(here)(act)

        far, own, body = pl.ds(0, 2), pl.ds(2, frames), pl.ds(1, rows)
        above, below = pl.ds(0, 1), pl.ds(rows + 1, 1)
        wait(3, s < ns - 1, (own, below))
        wait(4, s > 0, (own, above))
        wait(0, t > 0, (far, body))
        wait(1, (t > 0) & (s < ns - 1), (far, below))
        wait(2, (t > 0) & (s > 0), (far, above))

    def kernel_of(tap):
        return jnp.concatenate(
            [
                jnp.concatenate([shares[q, col, part, tap] for part in range(parts)], axis=1)
                for q in range(n)
                for col in range(columns)
            ],
            axis=0,
        )

    field[pl.ds(2 + frames * t, frames)] = norm_silu(inputs, gains[0:1]).astype(
        jnp.bfloat16
    ).reshape(frames, rows, cols, width)
    for copy in loads[2:]:
        copy.wait()
    toks = owner_of.shape[1]
    before = lax.broadcasted_iota(jnp.int32, (toks, toks), 0)
    after = lax.broadcasted_iota(jnp.int32, (toks, toks), 1)
    owner = owner_of[...]
    owner_column = jnp.sum(jnp.where(before == after, owner, 0), axis=1, keepdims=True)
    same = (owner_column == owner) & (before < after)
    rank = jnp.sum(jnp.where(same, 1, 0), axis=0, keepdims=True)
    slots = lax.broadcasted_iota(jnp.int32, (owners * SUBLANES, toks), 0)
    slotted = jnp.where(slots == owner * SUBLANES + rank, 1.0, 0.0).astype(jnp.bfloat16)
    spot = lax.broadcasted_iota(jnp.int32, (toks, cells), 1)
    patch = (spot // (2 * cols)) * (cols // 2) + spot % cols // 2
    held = patch == lax.broadcasted_iota(jnp.int32, (toks, cells), 0)
    placing[...] = jnp.dot(
        slotted, jnp.where(held, 1.0, 0.0).astype(jnp.bfloat16), preferred_element_type=jnp.float32
    ).astype(jnp.bfloat16)
    mine_load.wait()
    pl.semaphore_wait(barrier, expected)
    start = lambda copy: copy.start()
    reach(send_blocks)
    reach(send_lines)
    weight_copy.wait()
    if relays:
        order = ((0, 1, 2, 3), (3, 2, 0, 1), (0, 1, 3, 2), (3, 2, 0, 1))
        flow = ((1, 2, 3), (0, 2, 3), (3, 1, 0), (2, 1, 0))

        def forward():
            relay_block(0, 1)
            pass_on(end)
            pass_on(mate)
            for k in range(bits):
                line_relay(0, k).start()
                line_relay(1, k).start()
            relay_block(2)

        def last(q):
            for k in range(bits):
                line_came(q, k)
                line_relay(2, k).start()
                pass_bit(q, k)

        before = (
            ((), ((arrived, 1),), ((pass_on, 1), (arrived, 2)), ((pass_on, 2), (arrived, 3))),
            ((), ((last, 3),), (), ()),
            ((), (), ((last, 0),), ()),
            (((arrived, 2),), ((pass_on, 2), (arrived, 1)), ((pass_on, 1), (arrived, 0)), ()),
        )

        def pick(table, k):
            spot = table[0][k]
            for i in range(1, n):
                spot = jnp.where(t == i, table[i][k], spot)
            return spot

        def chosen(table, k):
            spot = pick(table, 0)
            for kk in range(1, len(table[0])):
                spot = jnp.where(k == kk, pick(table, kk), spot)
            return spot

        pl.when(middle)(forward)

        def step(k, carry):
            for i in range(n):
                for kk in range(n):
                    if before[i][kk]:

                        @pl.when((t == i) & (k == kk))
                        def _():
                            for act, c in before[i][kk]:
                                act(c)

            one(chosen(order, k))
            return carry

        lax.fori_loop(0, n, step, 0)
        pl.when(jnp.logical_not(middle))(lambda: pass_on(pick(flow, 2)))
    else:

        def hold(d, carry):
            arrived((t + d) % n)
            return carry

        lax.fori_loop(1, n, hold, 0)

        def step(d, carry):
            one((t + d) % n)
            return carry

        lax.fori_loop(1, n + 1, step, 0)

    gathered(slab_in.at[pl.ds(0, n - 1)], slab_sem.at[0], slab_sem.at[1]).wait_recv()
    for side in range(2):
        fed(side, lambda: gathered(edge_in.at[side], edge_sem.at[0, side], edge_sem.at[1, side]).wait_recv())
    hidden = unfold([slab_in[q].astype(jnp.float32) for q in range(n)])
    top, bottom = [
        unfold([edge_in[side, q].astype(jnp.float32) for q in range(n)]).reshape(
            frames, 1, cols, width
        )
        for side in range(2)
    ]
    hidden = hidden.reshape(frames, rows, cols, width)
    if rows > 1:
        hidden = jnp.concatenate(
            [hidden[:, :1] + top, hidden[:, 1 : rows - 1], hidden[:, rows - 1 :] + bottom], axis=1
        )
    else:
        hidden = hidden + top + bottom
    hidden = hidden.reshape(cells, width) + biases[0:1]
    inner[2:, 1 : rows + 1] = norm_silu(hidden, gains[1:2]).astype(jnp.bfloat16).reshape(
        frames, rows, cols, width
    )
    halo_copies(start)
    if not relays:

        def passed(d, carry):
            pass_on((t + d) % n)
            return carry

        lax.fori_loop(1, n, passed, 0)
    if shared:

        def crossed(k, carry):
            if relays:
                q = chosen(flow, k)
            else:
                q = (t + 1 + k) % n
            cross(q)
            return carry

        lax.fori_loop(0, n - 1, crossed, 0)
    pltpu.make_async_copy(shares.at[t], shares.at[t], share_sem.at[1]).wait()
    halo_came()
    if shared:

        gathered(shares.at[pl.ds(0, n - 1), :, 0], bulk_sem.at[1], bulk_sem.at[2]).wait_recv()
    sums = []
    for e in range(3):
        total = None
        for a in range(3):
            for r in range(3):
                block = inner[a : a + frames, r : r + rows].reshape(cells, width)
                term = lax.dot_general(
                    block, kernel_of(9 * a + 3 * r + e),
                    (((1,), (1,)), ((), ())), preferred_element_type=jnp.float32,
                )
                total = term if total is None else total + term
        sums.append(total)
    hidden = beside(*sums) + biases[1:2]
    merged = feat[...].reshape(cells, width).astype(jnp.float32) + hidden
    active = norm_silu(merged, gains[2:3]).astype(jnp.bfloat16)
    rest = jnp.zeros((LANES - 4 * width_latent, width), jnp.bfloat16)
    latent_wide = jnp.concatenate([latent_rows[...]] * 4 + [rest], axis=0)
    latent = lax.dot_general(
        active, latent_wide, (((1,), (1,)), ((), ())), preferred_element_type=jnp.float32
    )
    cell = lax.broadcasted_iota(jnp.int32, (cells, LANES), 0)
    lane = lax.broadcasted_iota(jnp.int32, (cells, LANES), 1)
    corner = (cell // cols % 2) * 2 + cell % 2
    alive = (t * frames + cell // (rows * cols) < count[0]) & (corner == 0)
    flagged = jnp.where((lane == 4 * width_latent) & alive, 1.0, 0.0)
    patches = jnp.where(lane // width_latent == corner, latent, flagged).astype(jnp.bfloat16)
    outgoing = jnp.dot(
        placing[...], patches, preferred_element_type=jnp.float32
    ).astype(jnp.bfloat16)
    tok_out[...] = outgoing.reshape(owners, SUBLANES, LANES)
    tok_in[pl.ds(me, 1)] = tok_out[pl.ds(me, 1)]

    def tok_start(d, carry):
        target = (me + d) % owners
        pltpu.make_async_remote_copy(
            src_ref=tok_out.at[target], dst_ref=tok_in.at[me],
            send_sem=tok_sem.at[0], recv_sem=tok_sem.at[1],
            device_id={"tm": target // ns, "space": target % ns}, device_id_type=MESH,
        ).start()
        return carry

    lax.fori_loop(1, owners, tok_start, 0)
    def line_sent(_, way):
        count = 1 if relays else n - 1
        gathered(field.at[pl.ds(0, frames * count)], block_send.at[way]).wait_send()
        gathered(shares.at[pl.ds(0, count), 0, 0], line_send.at[way]).wait_send()

    if relays:
        beside_line(line_sent)

        @pl.when(middle)
        def _():
            for i in range(3):
                gathered(field.at[pl.ds(0, frames)], relay_send.at[i]).wait_send()
                gathered(shares.at[0, 0, 0], line_relay_send.at[i]).wait_send()

    else:
        line_sent(0, 0)
    gathered(slab_out.at[pl.ds(0, n - 1)], slab_sem.at[0]).wait_send()
    for side in range(2):
        sided(side, lambda: gathered(edge_out.at[side], edge_sem.at[0, side]).wait_send())
    if shared:
        gathered(shares.at[pl.ds(0, n - 1), pl.ds(0, columns - 1), 0], bulk_sem.at[0]).wait_send()
        gathered(shares.at[pl.ds(0, n - 1), :, 0], bulk_sem.at[1]).wait_send()
    halo_copies(lambda copy: copy.wait_send())
    everyone = gathered(tok_in.at[pl.ds(0, owners - 1)], tok_sem.at[0], tok_sem.at[1])
    everyone.wait_recv()
    row = lax.broadcasted_iota(jnp.int32, (owners * most, owners * SUBLANES), 0)
    held = lax.broadcasted_iota(jnp.int32, (owners * most, owners * SUBLANES), 1)
    inner = held % SUBLANES
    chosen = (row == held // SUBLANES * most + inner) & (inner < most)
    tokens_out[...] = jnp.dot(
        jnp.where(chosen, 1.0, 0.0).astype(jnp.bfloat16),
        tok_in[...].reshape(owners * SUBLANES, LANES),
        preferred_element_type=jnp.float32,
    ).astype(jnp.bfloat16)
    everyone.wait_send()


def embedder(channels, tokens, weight, bias, packed):
    held = tokens[...]
    projected = jnp.dot(held[:, :channels], weight[...], preferred_element_type=jnp.float32)
    flags = held[:, channels : channels + 1].astype(jnp.float32)
    packed[...] = ((projected + bias[...]) * flags).astype(jnp.bfloat16)


def shards(
    features,
    frame_counts,
    routes,
    norm_gains,
    conv_weights,
    conv_biases,
    latent_weight,
    embed_weight,
    embed_bias,
):
    feat = features[0]
    frames, rows, cols, width = feat.shape
    cells = frames * rows * cols
    n, ns = lax.axis_size("tm"), lax.axis_size("space")
    ng, nc = lax.axis_size("groups"), lax.axis_size("clip")
    owners = n * ns
    out = conv_weights.shape[1]
    pack = max(1, LANES // out)
    latents = latent_weight.shape[1]
    tok_count = routes.shape[1]
    most = (tok_count + owners - 1) // owners + 1
    vmem = pl.BlockSpec(memory_space=pltpu.VMEM)
    hbm = pl.BlockSpec(memory_space=pltpu.HBM)
    away = lambda value: pltpu.with_memory_space_constraint(value, pltpu.HBM)
    dma = pltpu.SemaphoreType.DMA
    field = pltpu.VMEM((n * frames + 2, rows, cols, width), jnp.bfloat16)
    inner = pltpu.VMEM((frames + 2, rows + 2, cols, width), jnp.bfloat16)
    slab = pltpu.VMEM((n, cells // pack, pack * out), jnp.bfloat16)
    edge = pltpu.VMEM((2, n, frames * cols // pack, pack * out), jnp.bfloat16)
    columns, parts = ng * ns, nc
    if out % (SUBLANES * columns) or width % (LANES * parts):
        columns = parts = 1
    taps = conv_weights.shape[2]
    shares = pltpu.VMEM((n, columns, parts, taps, out // columns, width // parts), jnp.bfloat16)
    cuts = CUTS if frames % CUTS == 0 else 1
    bits = BITS if taps % BITS == 0 else 1
    tok = pltpu.VMEM((owners, SUBLANES, LANES), jnp.bfloat16)
    tokens = pl.pallas_call(
        functools.partial(encoder, n, ns, ng, nc, most, latents),
        out_shape=jax.ShapeDtypeStruct((owners * most, LANES), jnp.bfloat16),
        in_specs=[hbm] * 7 + [pl.BlockSpec(memory_space=pltpu.SMEM)],
        out_specs=vmem,
        scratch_shapes=[
            pltpu.VMEM(feat.shape, feat.dtype),
            pltpu.VMEM(norm_gains.shape, norm_gains.dtype),
            pltpu.VMEM(conv_biases.shape, conv_biases.dtype),
            pltpu.VMEM((latents, width), latent_weight.dtype),
            pltpu.VMEM((1, tok_count), routes.dtype),
            field, inner,
            pltpu.VMEM((9, 3 * out, width), jnp.bfloat16),
            pltpu.VMEM(shares.shape[3:], jnp.bfloat16), shares,
            pltpu.VMEM((owners * SUBLANES, cells), jnp.bfloat16),
            slab, slab, edge, edge, tok, tok,
            dma((5,)), dma, dma((2,)), dma((2,)), dma((3,)), dma((n, cuts)), dma((2,)), dma((2, 2)),
            dma((5,)), dma((2,)), dma((3,)), dma((n, bits)), dma((n - 1, bits)),
            dma((3,)), dma((2,)),
        ],
        compiler_params=pltpu.CompilerParams(
            collective_id=0, has_side_effects=True, vmem_limit_bytes=GRANT
        ),
    )(
        away(feat),
        away(conv_weights.transpose(0, 2, 1, 3).reshape(2, 9, 3 * out, width)),
        away(conv_weights.transpose(0, 2, 1, 3)),
        away(norm_gains),
        away(conv_biases),
        away(latent_weight.T),
        away(routes.reshape(1, tok_count)),
        frame_counts,
    )
    channels = 4 * latents
    embed = embed_weight.shape[1]
    chunk = embed // 1 if embed % (1 * LANES) == 0 else embed
    packed = pl.pallas_call(
        functools.partial(embedder, channels),
        grid=(embed // chunk,),
        out_shape=jax.ShapeDtypeStruct((owners * most, embed), jnp.bfloat16),
        in_specs=[
            pl.BlockSpec((owners * most, LANES), lambda i: (0, 0)),
            pl.BlockSpec((channels, chunk), lambda i: (0, i)),
            pl.BlockSpec((1, chunk), lambda i: (0, i)),
        ],
        out_specs=pl.BlockSpec((owners * most, chunk), lambda i: (0, i)),
        compiler_params=pltpu.CompilerParams(vmem_limit_bytes=GRANT),
    )(tokens, embed_weight, embed_bias.reshape(1, embed))
    return packed[None]


def solution(mesh):
    return jax.shard_map(
        shards,
        mesh=mesh,
        in_specs=(
            P(("groups", "clip"), "tm", "space", None, None),
            P(("groups", "clip")),
            P(("groups", "clip"), ("tm", "space"), None),
            P(),
            P(None, "tm", None, None),
            P(),
            P(),
            P(),
            P(),
        ),
        out_specs=P(("groups", "clip"), ("tm", "space"), None),
        check_vma=False,
    )
```
